32 devices in a mesh: ax: 8 (over z, y), az: 4 (over x, core).
Axes of the slice: x: 2, y: 2, z: 4, core: 2. Of those that a mesh axis runs over, the one named last changes fastest.
Arguments:
- density: float32 [32, 256, 256], P('ax', 'az'), may hold values from 0.5 to 2
- velocity: float32 [3, 32, 256, 256], P(None, 'ax', 'az'), may hold values from -12 to 12
Outputs:
- stress_flux: float32 [3, 32, 256, 256], P(None, 'ax', 'az')
- coefficient: float32 [32, 256], P('ax')
The draws below stay inside these ranges and needn't reach their ends.
All inputs are finite; a program needn't handle non-finite values.
Results may differ from the reference program's by a relative error of at most 0.00002.
Values sent between devices are 32-bit elements; how exact they have to be, the bound alone decides.
A program may use at most 64 MiB of HBM per device.

```python
import math
import jax
import jax.numpy as jnp
from jax import lax

NR = 256
NX = 32
NT = 256


def draw_velocity(key, part):
    sector_at = jnp.arange(NT, dtype=jnp.float32) / NT
    amplitude = (0.5 + sector_at)[None, None, :, None]
    random_part = jnp.clip(jax.random.normal(key, (3, NX, NT, NR), jnp.float32), -6.0, 6.0)
    return random_part * amplitude


def levels(rng, shape, cuts, least, top_value):
    factor_of = 1.0
    for axis_at, blocks in cuts:
        draws = jax.random.uniform(jax.random.fold_in(jax.random.fold_in(rng, 6), axis_at), (blocks,), jnp.float32, least / len(cuts), top_value / len(cuts))
        factor_of = factor_of * jnp.repeat(jnp.exp(draws), shape[axis_at] // blocks).reshape((-1,) + (1,) * (len(shape) - 1 - axis_at))
    return factor_of


def setup_inputs(seed: int = 0) -> dict:
    splits = jax.random.split(jax.random.key(seed), 3)
    density = jnp.clip(0.5 + 1.5 * jax.random.uniform(splits[0], (NX, NT, NR), jnp.float32) ** levels(splits[0], (NX, NT, NR), ((0, 8), (1, 4)), -0.2, 0.2), 0.5, 2.0)
    velocity = draw_velocity(jax.random.fold_in(splits[2], 71), 0)
    return {"density": density, "velocity": velocity}


STEP_AXIAL = 0.5
STEP_RADIAL = 0.25
INNER_RADIUS = 10.0
FILTER_RATIO = 2.0
TINY = 1e-06
COMPONENT_PAIRS = ((0, 0), (1, 1), (2, 2), (0, 1), (0, 2), (1, 2))

def trim_cells(values, dim_at, amount):
    extent = values.shape[dim_at]
    return lax.slice_in_dim(values, amount, extent - amount, axis=dim_at)

def interior(values, amount):
    values = trim_cells(values, values.ndim - 3, amount)
    return trim_cells(values, values.ndim - 2, amount)

def pad_radial(values):
    return jnp.concatenate([values[..., :1], values, values[..., -1:]], axis=values.ndim - 1)

def smooth_axis(values, dim_at):
    extent = values.shape[dim_at]
    return 0.25 * lax.slice_in_dim(values, 0, extent - 2, axis=dim_at) + 0.5 * lax.slice_in_dim(values, 1, extent - 1, axis=dim_at) + 0.25 * lax.slice_in_dim(values, 2, extent, axis=dim_at)

def slope_axis(values, dim_at):
    extent = values.shape[dim_at]
    return 0.5 * (lax.slice_in_dim(values, 2, extent, axis=dim_at) - lax.slice_in_dim(values, 0, extent - 2, axis=dim_at))

def test_filter(values):
    smooth = smooth_axis(values, values.ndim - 3)
    smooth = smooth_axis(smooth, values.ndim - 2)
    return smooth_axis(pad_radial(smooth), values.ndim - 1)

def geometry(radial_cells, azimuth_cells):
    radius = INNER_RADIUS + (jnp.arange(radial_cells, dtype=jnp.float32) + 0.5) * STEP_RADIAL
    angle_step = 2.0 * math.pi / azimuth_cells
    width_sq = (STEP_AXIAL * STEP_RADIAL * angle_step * radius) ** (2.0 / 3.0)
    return (radius, angle_step, width_sq)

def strain(velocity, radius, angle_step):
    d_ax = trim_cells(slope_axis(velocity, 1), 2, 1) / STEP_AXIAL
    d_az = trim_cells(slope_axis(velocity, 2), 1, 1) / (radius * angle_step)
    d_rad = interior(slope_axis(pad_radial(velocity), 3), 1) / STEP_RADIAL
    centre = interior(velocity, 1)
    s_xx = d_ax[0]
    s_rr = d_rad[1]
    s_tt = d_az[2] + centre[1] / radius
    s_xr = 0.5 * (d_rad[0] + d_ax[1])
    s_xt = 0.5 * (d_az[0] + d_ax[2])
    s_rt = 0.5 * (d_az[1] + d_rad[2] - centre[2] / radius)
    strength = jnp.sqrt(2.0 * (s_xx * s_xx + s_rr * s_rr + s_tt * s_tt + 2.0 * (s_xr * s_xr + s_xt * s_xt + s_rt * s_rt)))
    third = (s_xx + s_rr + s_tt) / 3.0
    deviator = jnp.stack([s_xx - third, s_rr - third, s_tt - third, s_xr, s_xt, s_rt])
    return (deviator, strength)

def model_of(density, width_sq, strength, deviator):
    return density * width_sq * strength * deviator

def pair_products(left_v, right_v):
    return jnp.stack([left_v[first_c] * right_v[second_c] for first_c, second_c in COMPONENT_PAIRS])

def contract(left_t, right_t):
    return left_t[0] * right_t[0] + left_t[1] * right_t[1] + left_t[2] * right_t[2] + 2.0 * (left_t[3] * right_t[3] + left_t[4] * right_t[4] + left_t[5] * right_t[5])

def closure(hat_rho, hat_mom, hat_pairs, hat_model, hat_dev, hat_strength, width_sq):
    mixed_term = FILTER_RATIO * FILTER_RATIO * width_sq * hat_rho * hat_strength * hat_dev - hat_model
    resolved = jnp.stack([hat_mom[first_c] * hat_mom[second_c] / hat_rho for first_c, second_c in COMPONENT_PAIRS])
    leonard = hat_pairs - resolved
    return (contract(leonard, mixed_term), contract(mixed_term, mixed_term))

def lilly_ratio(lm_sum, mm_sum, azimuth_cells):
    return -0.5 * (lm_sum / azimuth_cells) / (mm_sum / azimuth_cells + TINY)

def divergence(stress, radius, angle_step):
    d_ax = trim_cells(slope_axis(stress, 1), 2, 1) / STEP_AXIAL
    d_az = trim_cells(slope_axis(stress, 2), 1, 1) / (radius * angle_step)
    radial_one = pad_radial(jnp.stack([stress[3], stress[1]]) * radius)
    radial_two = pad_radial(stress[5] * (radius * radius))
    d_one = interior(slope_axis(radial_one, 3), 1) / STEP_RADIAL / radius
    d_two = interior(slope_axis(radial_two, 2), 1) / STEP_RADIAL / (radius * radius)
    centre = interior(stress, 1)
    flux_x = d_ax[0] + d_one[0] + d_az[4]
    flux_r = d_ax[3] + d_one[1] + d_az[5] - centre[2] / radius
    flux_t = d_ax[4] + d_two + d_az[2]
    return jnp.stack([flux_x, flux_r, flux_t])

def pad_cells(values, width_cells):
    leading = [(0, 0)] * (values.ndim - 3)
    values = jnp.pad(values, leading + [(width_cells, width_cells), (0, 0), (0, 0)], mode='edge')
    return jnp.pad(values, leading + [(0, 0), (width_cells, width_cells), (0, 0)], mode='wrap')

def reference(density, velocity):
    radius, angle_step, width_sq = geometry(NR, NT)
    deviator, strength = strain(pad_cells(velocity, 1), radius, angle_step)
    model_stress = model_of(density, width_sq, strength, deviator)
    momentum = density * velocity
    pair_terms = pair_products(momentum, velocity)
    hat_rho = test_filter(pad_cells(density, 1))
    hat_mom = test_filter(pad_cells(momentum, 1))
    hat_pairs = test_filter(pad_cells(pair_terms, 1))
    hat_model = test_filter(pad_cells(model_stress, 1))
    hat_dev, hat_strength = strain(pad_cells(hat_mom / hat_rho, 1), radius, angle_step)
    lm_cells, mm_cells = closure(hat_rho, hat_mom, hat_pairs, hat_model, hat_dev, hat_strength, width_sq)
    coefficient = lilly_ratio(lax.optimization_barrier(jnp.sum(lm_cells, axis=1)), lax.optimization_barrier(jnp.sum(mm_cells, axis=1)), NT)
    stress = -2.0 * coefficient[:, None, :] * model_stress
    stress_flux = divergence(pad_cells(stress, 1), radius, angle_step)
    return (stress_flux, coefficient)
```

```python
import functools
import itertools
import math

import jax
import jax.numpy as jnp
import numpy as np
from jax import lax
from jax.experimental import pallas as pl
from jax.experimental.pallas import tpu as pltpu
from jax.sharding import PartitionSpec as P

STEP_AXIAL = 0.5
STEP_RADIAL = 0.25
INNER_RADIUS = 10.0
FILTER_RATIO = 2.0
TINY = 1e-06
PAIRS = ((0, 0), (0, 1), (0, 2), (1, 1), (2, 2), (1, 2))
DIAGONAL = (0, 3, 4)
CROSS = (1, 2, 5)
LANES = 128
SUB = 8
EDGE = 16
SEAM = 4
COPIES = 64
MESH_ID = pl.DeviceIdType.MESH


def geometry(radial, azimuth_cells):
    radius = INNER_RADIUS + (np.arange(radial, dtype=np.float64) + 0.5) * STEP_RADIAL
    angle = 2.0 * math.pi / azimuth_cells
    width = (STEP_AXIAL * STEP_RADIAL * angle * radius) ** (2.0 / 3.0)
    rows = np.stack(
        [
            1.0 / radius,
            0.5 / (radius * angle),
            width,
            FILTER_RATIO**2 * width,
            radius,
            0.5 / STEP_RADIAL / radius,
            radius * radius,
            0.5 / STEP_RADIAL / (radius * radius),
        ]
    ).astype(np.float32)
    halves = rows.reshape(rows.shape[0], radial // LANES, 1, LANES)
    at_seam = radial // 2 - SEAM // 2 + np.arange(LANES) % SEAM
    seam = rows[:4, None, at_seam]
    return (
        np.ascontiguousarray(np.broadcast_to(halves, halves.shape[:2] + (SUB, LANES))),
        np.ascontiguousarray(np.broadcast_to(seam, (4, SUB, LANES))),
    )


def lane_of(x):
    return lax.broadcasted_iota(jnp.int32, x.shape, x.ndim - 1)


def before(x):
    y = pltpu.roll(x, 1, x.ndim - 1)
    fill = jnp.concatenate([x[:1], y[:-1]], axis=0)
    return jnp.where(lane_of(x) == 0, fill, y)


def after(x):
    y = pltpu.roll(x, LANES - 1, x.ndim - 1)
    fill = jnp.concatenate([y[1:], x[-1:]], axis=0)
    return jnp.where(lane_of(x) == LANES - 1, fill, y)


def rise(x):
    return after(x) - before(x)


def sides(x, end):
    lane = lane_of(x)
    return (
        jnp.where(lane == 0, end, pltpu.roll(x, 1, 1)),
        jnp.where(lane == LANES - 1, end, pltpu.roll(x, LANES - 1, 1)),
    )


def strain(dx, dr, dt, ur, ut, inv_r):
    s_xx, s_rr = dx[0], dr[1]
    s_tt = dt[2] + ur * inv_r
    s_xr = 0.5 * (dr[0] + dx[1])
    s_xt = 0.5 * (dt[0] + dx[2])
    s_rt = 0.5 * (dt[1] + dr[2] - ut * inv_r)
    size = jnp.sqrt(
        2.0
        * (
            s_xx * s_xx
            + s_rr * s_rr
            + s_tt * s_tt
            + 2.0 * (s_xr * s_xr + s_xt * s_xt + s_rt * s_rt)
        )
    )
    third = (s_xx + s_rr + s_tt) * (1.0 / 3.0)
    return (s_xx - third, s_xr, s_xt, s_rr - third, s_tt - third, s_rt), size


def kernel(
    n_ax, n_az, nx, nt,
    rho_ref, vel_ref, geo_ref, seam_ref, flux_ref, coef_ref,
    S, T, M, H, V, HM, PX, MX, E, G, GM, GH, GP, GX, GV,
    part, rec, rec_out, CS, own_sem, send_sem, recv_sem, sum_send, sum_recv,
):
    pr = 2 * nx
    me_ax, me_az = lax.axis_index("ax"), lax.axis_index("az")
    left, right = lax.rem(me_az + n_az - 1, n_az), lax.rem(me_az + 1, n_az)
    odd = lax.rem(me_ax, 2)
    even = 1 - odd
    mine, other = odd, even
    azimuth_cells = nt * n_az

    def pick(at_even, at_odd):
        return jnp.where(odd == 0, at_even, at_odd)

    has_lo, has_hi = me_ax > 0, me_ax < n_ax - 1
    pair_lo, pair_hi = me_ax >= 2, me_ax < n_ax - 2
    partner = me_ax + 1 - 2 * odd
    near_ax = me_ax - 2 + 4 * odd
    far_ax = me_ax + 2 - 4 * odd
    edge_ax = me_ax - 1 + 2 * odd
    has_near = (near_ax >= 0) & (near_ax < n_ax)
    has_far = (far_ax >= 0) & (far_ax < n_ax)

    lanes_mine = pl.ds(pl.multiple_of(mine * LANES, LANES), LANES)
    lanes_other = pl.ds(pl.multiple_of(other * LANES, LANES), LANES)
    cols = pl.ds(EDGE, nt)
    own_row = nx * odd
    own_at = own_row + 2
    partner_at = nx * even + 2
    near_at = pick(0, nx - 2)
    beyond_at = pick(pr + 2, 0)
    ahead_at = pick(0, pr + 2)
    pass_at = pick(pr, 2)

    own = [
        pltpu.make_async_copy(rho_ref.at[:, :, lanes_mine], S.at[0, pl.ds(own_at, nx), cols, :], own_sem.at[0]),
        pltpu.make_async_copy(
            vel_ref.at[:, :, :, lanes_mine], S.at[pl.ds(1, 3), pl.ds(own_at, nx), cols, :], own_sem.at[1]),
        pltpu.make_async_copy(rho_ref.at[:, :, lanes_other], T.at[0, pl.ds(1, nx), cols, :], own_sem.at[2]),
        pltpu.make_async_copy(
            vel_ref.at[:, :, :, lanes_other], T.at[pl.ds(1, 3), pl.ds(1, nx), cols, :], own_sem.at[3]),
    ]
    for c in own:
        c.start()

    barrier = pltpu.get_barrier_semaphore()

    def greet(ax, az):
        pl.semaphore_signal(barrier, inc=1, device_id=(ax, az), device_id_type=MESH_ID)

    for d in range(1, n_az):
        greet(me_ax, lax.rem(me_az + d, n_az))
    peers = n_az - 1
    for step in (-1, 1, -2, 2):
        there = (me_ax + step >= 0) & (me_ax + step < n_ax)

        @pl.when(there)
        def _():
            for d in range(n_az):
                greet(me_ax + step, lax.rem(me_az + d, n_az))

        peers = peers + jnp.where(there, n_az, 0)

    ids = itertools.count()

    def remote(src, dst, ax, az):
        at = next(ids)
        return pltpu.make_async_remote_copy(
            src_ref=src, dst_ref=dst, send_sem=send_sem.at[at], recv_sem=recv_sem.at[at],
            device_id=(ax, az), device_id_type=MESH_ID)

    def block(src_row, count, first, width, lanes, dst, dst_row, dst_first, ax, az):
        rows, at = pl.ds(src_row, count), pl.ds(first, width)
        to_rows, to = pl.ds(dst_row, count), pl.ds(dst_first, width)
        return [
            remote(rho_ref.at[rows, at, lanes], dst.at[0, to_rows, to, :], ax, az),
            remote(vel_ref.at[:, rows, at, lanes], dst.at[pl.ds(1, 3), to_rows, to, :], ax, az),
        ]

    def ends(src_row, count, lanes, dst, dst_row, ax, az):
        out = []
        for first in (0, nt - SUB):
            out += block(src_row, count, first, SUB, lanes, dst, dst_row, EDGE + first, ax, az)
        return out

    def middle(src_row, count, lanes, dst, dst_row, ax, az):
        return block(src_row, count, SUB, nt - 2 * SUB, lanes, dst, dst_row, EDGE + SUB, ax, az)

    def around(ref, lead, rows):
        at = (pl.ds(EDGE + nt - SUB, SUB), pl.ds(EDGE - SUB, SUB), pl.ds(EDGE, SUB), pl.ds(EDGE + nt, SUB))
        return [
            remote(ref.at[lead, rows, at[0], :], ref.at[lead, rows, at[1], :], me_ax, right),
            remote(ref.at[lead, rows, at[2], :], ref.at[lead, rows, at[3], :], me_ax, left),
        ]

    fold = nt // 2
    whole = pl.ds(SUB, fold)

    def seam_around(s):
        return [
            remote(E.at[s, pl.ds(fold, SUB), :], E.at[s, pl.ds(0, SUB), :], me_ax, right),
            remote(E.at[s, pl.ds(SUB, SUB), :], E.at[s, pl.ds(SUB + fold, SUB), :], me_ax, left),
        ]

    s_own, s_partner, s_beyond, s_ahead = 1 + odd, 2 - odd, pick(3, 0), pick(0, 3)

    own_around = []
    for lanes, dst, row in ((lanes_mine, S, own_at), (lanes_other, T, 1)):
        own_around += block(0, nx, nt - SUB, SUB, lanes, dst, row, EDGE - SUB, me_ax, right)
        own_around += block(0, nx, 0, SUB, lanes, dst, row, EDGE + nt, me_ax, left)
    seam_own = seam_around(s_own)
    seam_partner_around = seam_around(s_partner)
    seam_beyond_around = seam_around(s_beyond)
    seam_ahead_around = seam_around(s_ahead)

    seam_swap = remote(E.at[s_own, whole, :], E.at[s_own, whole, :], partner, me_az)
    seam_near = remote(E.at[s_own, whole, :], E.at[pick(3, 0), whole, :], near_ax, me_az)
    seam_pass = remote(E.at[s_partner, whole, :], E.at[pick(0, 3), whole, :], far_ax, me_az)

    swap_ends = ends(0, nx, lanes_other, S, own_at, partner, me_az)
    swap_rows = {}
    for q in range(nx):
        row = pick(nx - 1 - q, q)
        swap_rows[q] = middle(row, 1, lanes_other, S, own_at + row, partner, me_az)
    near_ends = ends(near_at, 2, lanes_mine, S, beyond_at, near_ax, me_az)
    near_rows = middle(near_at, 2, lanes_mine, S, beyond_at, near_ax, me_az)

    every = pl.ds(0, 4)

    def forward(row, first, width, count):
        return remote(
            S.at[:, pl.ds(pass_at + row, count), pl.ds(EDGE + first, width), :],
            S.at[:, pl.ds(ahead_at + row, count), pl.ds(EDGE + first, width), :], far_ax, me_az)

    pass_ends = [forward(0, first, SUB, 2) for first in (0, nt - SUB)]
    last_row = pick(1, 0)
    pass_rows = [forward(last_row, SUB, nt - 2 * SUB, 1), forward(1 - last_row, SUB, nt - 2 * SUB, 1)]
    partner_around = around(S, every, pl.ds(partner_at, nx))
    beyond_around = around(S, every, pl.ds(beyond_at, 2))
    ahead_around = around(S, every, pl.ds(ahead_at, 2))

    swap_row, edge_row = pick(nx - 1, 0), pick(0, nx - 1)
    three = pl.ds(1, 3)

    def flux_rows(row, dst_row, ax):
        return remote(
            vel_ref.at[:, pl.ds(row, 1), :, lanes_mine], T.at[three, pl.ds(dst_row, 1), cols, :], ax, me_az)

    def flux_stress(row, dst_row, ax):
        return remote(
            M.at[mine, pl.ds(0, 3), own_row + row + 1, cols, :], M.at[mine, pl.ds(0, 3), dst_row, cols, :],
            ax, me_az)

    swap_vel = flux_rows(swap_row, pick(0, nx + 1), partner)
    edge_vel = flux_rows(edge_row, pick(nx + 1, 0), edge_ax)
    swap_vel_around = around(T, three, pl.ds(pick(nx + 1, 0), 1))
    edge_vel_around = around(T, three, pl.ds(pick(0, nx + 1), 1))
    swap_stress = flux_stress(swap_row, pick(nx, nx + 1), partner)
    edge_stress = flux_stress(edge_row, pick(pr + 1, 0), edge_ax)

    def start(copies):
        for c in copies:
            c.start()

    def arrive(copies):
        for c in copies:
            c.wait_recv()

    def leave(copies):
        for c in copies:
            c.wait_send()

    wide = nt + 2 * SUB
    outer_cols = EDGE - SUB

    def lanes_at(n):
        return lax.broadcasted_iota(jnp.int32, (n, LANES), 1)

    def spread(values, rows):
        return jnp.concatenate([values] * (rows // SUB), axis=values.ndim - 2)

    def pack_seam():
        lane = lanes_at(nt)
        from_mine = jnp.where(lane >= LANES - SEAM // 2, 1, 0) == even
        half = lanes_at(fold)
        packed = jnp.zeros((fold, LANES), jnp.float32)
        for a in range(4):
            for i in range(nx):
                first = (a * nx + i) * SEAM
                x = jnp.where(from_mine, S[a, own_at + i, pl.ds(EDGE, nt), :], T[a, 1 + i, pl.ds(EDGE, nt), :])
                low = pltpu.roll(x[:fold], (first + SEAM // 2) % LANES, 1)
                high = pltpu.roll(x[fold:], (first + SEAM // 2 + LANES // 2) % LANES, 1)
                packed = jnp.where((half >= first) & (half < first + SEAM), low, packed)
                first += LANES // 2
                packed = jnp.where((half >= first) & (half < first + SEAM), high, packed)
        E[s_own, pl.ds(SUB, fold), :] = packed

    seam_lane = lanes_at(wide)
    seam_row = seam_lane // SEAM
    at_bottom = seam_row == jnp.where(pair_lo, -1, nx)
    at_top = seam_row == jnp.where(pair_hi, -1, nx + pr - 1)

    def seam_below(x):
        return jnp.where(at_bottom, x, pltpu.roll(x, SEAM, 1))

    def seam_above(x):
        return jnp.where(at_top, x, pltpu.roll(x, LANES - SEAM, 1))

    def seam_axial(x):
        return (seam_below(x) + x) + (x + seam_above(x))

    def seam_rise(x):
        return pltpu.roll(x, LANES - 1, 1) - pltpu.roll(x, 1, 1)

    span = pl.ds(outer_cols, wide)
    span_before, span_after = pl.ds(outer_cols - 1, wide), pl.ds(outer_cols + 1, wide)

    def seam_turn(ref, a):
        x = ref[a, span, :]
        return (ref[a, span_before, :] + ref[a, span_after, :]) + (x + x)

    def seam_pass_all():
        lane = lanes_at(fold + SUB)
        per = nx * SEAM
        for a in range(4):
            low = jnp.zeros((fold + SUB, LANES), jnp.float32)
            high = low
            for s in range(4):
                here = (lane >= s * per) & (lane < (s + 1) * per)
                x = pltpu.roll(E[s, pl.ds(SUB, fold + SUB), :], (s * per - a * per) % LANES, 1)
                low = jnp.where(here, x, low)
                x = pltpu.roll(E[s, pl.ds(0, fold + SUB), :], (s * per - a * per - LANES // 2) % LANES, 1)
                high = jnp.where(here, x, high)
            G[a, pl.ds(EDGE - SUB, SUB), :] = high[:SUB]
            G[a, pl.ds(EDGE, fold), :] = low[:fold]
            G[a, pl.ds(EDGE + fold, fold), :] = high[SUB:]
            G[a, pl.ds(EDGE + nt, SUB), :] = low[fold:]
        rho = G[0, span, :]
        vel = [G[1 + a, span, :] for a in range(3)]
        inv_r, az_scale, width = (spread(seam_ref[g], wide) for g in (0, 1, 2))
        dx = [seam_above(v) - seam_below(v) for v in vel]
        dr = [seam_rise(v) * (0.5 / STEP_RADIAL) for v in vel]
        dt = [(G[1 + a, span_after, :] - G[1 + a, span_before, :]) * az_scale for a in range(3)]
        dev, size = strain(dx, dr, dt, vel[1], vel[2], inv_r)
        scale = rho * width * size
        for a in range(6):
            GM[a, span, :] = seam_axial(scale * dev[a])
        mom = [rho * v for v in vel]
        GH[0, span, :] = seam_axial(rho)
        for a in range(3):
            GH[1 + a, span, :] = seam_axial(mom[a])
        for at, (a, b) in enumerate(PAIRS):
            GP[at, span, :] = seam_axial(mom[a] * vel[b])
        hat = []
        for a in range(4):
            s = seam_turn(GH, a)
            GX[a, span, :] = s
            hat.append(((pltpu.roll(s, 1, 1) + pltpu.roll(s, LANES - 1, 1)) + (s + s)) * (1.0 / 64.0))
        inv = 1.0 / hat[0]
        for a in range(3):
            GV[a, span, :] = hat[1 + a] * inv
        for a in range(6):
            GX[4 + a, span, :] = seam_turn(GP, a)
            GX[10 + a, span, :] = seam_turn(GM, a)

    end_lane = pick(LANES - 1, 0)

    def seam_end(x, ref, a, first, r):
        shift = pick(LANES - 1 - SEAM // 2, LANES - SEAM // 2 + 1) - SEAM * (r + nx)
        g = pltpu.roll(ref[a, pl.ds(first, x.shape[0]), :], shift, 1)
        return jnp.where(lane_of(x) == end_lane, g, x)

    def seam_slope(x, ref, a, first, r):
        lo, hi = sides(x, seam_end(x, ref, a, first, r))
        return hi - lo

    def smooth(ref, a, row, first, n, at, r):
        x = ref[a, row, pl.ds(first, n), :]
        s = (ref[a, row, pl.ds(first - 1, n), :] + ref[a, row, pl.ds(first + 1, n), :]) + (x + x)
        lo, hi = sides(s, seam_end(s, GX, at, first, r))
        return ((lo + hi) + (s + s)) * (1.0 / 64.0)

    def low(r):
        return jnp.maximum(r - 1, jnp.where(pair_lo, -2, 0))

    def high(r):
        return jnp.minimum(r + 1, jnp.where(pair_hi, pr + 1, pr - 1))

    def sweep(first, count, body):
        def step(at, carry):
            t = first + at
            body(pick(t, pr - 1 - t))
            return carry

        lax.fori_loop(0, count, step, 0)

    def turn_slope(ref, a, row, first, n):
        return ref[a, row, pl.ds(first + 1, n), :] - ref[a, row, pl.ds(first - 1, n), :]

    def first_pass(r, with_pairs):
        n, c = wide, outer_cols
        rows = (low(r) + 2, r + 2, high(r) + 2)
        rho = [S[0, q, pl.ds(c, n), :] for q in rows]
        vel = [[S[1 + a, q, pl.ds(c, n), :] for a in range(3)] for q in rows]
        inv_r, az_scale, width = (spread(geo_ref[g, mine], n) for g in (0, 1, 2))
        dx = [vel[2][a] - vel[0][a] for a in range(3)]
        dr = [seam_slope(vel[1][a], G, 1 + a, c, r) * (0.5 / STEP_RADIAL) for a in range(3)]
        dt = [turn_slope(S, 1 + a, r + 2, c, n) * az_scale for a in range(3)]
        dev, size = strain(dx, dr, dt, vel[1][1], vel[1][2], inv_r)
        scale = rho[1] * width * size
        for a in range(6):
            M[mine, a, r + 1, pl.ds(c, n), :] = scale * dev[a]
        mom = [[rho[q] * vel[q][a] for a in range(3)] for q in range(3)]
        H[0, r + 1, pl.ds(c, n), :] = (rho[0] + rho[1]) + (rho[1] + rho[2])
        for a in range(3):
            H[1 + a, r + 1, pl.ds(c, n), :] = (mom[0][a] + mom[1][a]) + (mom[1][a] + mom[2][a])
        if with_pairs:
            for at, (a, b) in enumerate(PAIRS):
                p = [mom[q][a] * vel[q][b] for q in range(3)]
                PX[at, r, pl.ds(c, n), :] = (p[0] + p[1]) + (p[1] + p[2])

    def hat_pass(r):
        n, c = wide, outer_cols
        hat = [smooth(H, a, r + 1, c, n, a, r) for a in range(4)]
        inv = 1.0 / hat[0]
        for a in range(4):
            HM[a, r + 1, pl.ds(c, n), :] = hat[a]
        for a in range(3):
            V[a, r + 1, pl.ds(c, n), :] = hat[1 + a] * inv

    def model_pass(r):
        n, c = wide, outer_cols
        for a in range(6):
            x = M[mine, a, r + 1, pl.ds(c, n), :]
            lo = M[mine, a, low(r) + 1, pl.ds(c, n), :]
            MX[a, r, pl.ds(c, n), :] = (lo + x) + (x + M[mine, a, high(r) + 1, pl.ds(c, n), :])

    def closure_pass(r):
        n, c = nt, EDGE
        inv_r, az_scale, width4 = (spread(geo_ref[g, mine], n) for g in (0, 1, 3))
        hv = [V[a, r + 1, pl.ds(c, n), :] for a in range(3)]
        hm = [HM[1 + a, r + 1, pl.ds(c, n), :] for a in range(3)]
        dx = [V[a, high(r) + 1, pl.ds(c, n), :] - V[a, low(r) + 1, pl.ds(c, n), :] for a in range(3)]
        dr = [seam_slope(hv[a], GV, a, c, r) * (0.5 / STEP_RADIAL) for a in range(3)]
        dt = [turn_slope(V, a, r + 1, c, n) * az_scale for a in range(3)]
        dev, size = strain(dx, dr, dt, hv[1], hv[2], inv_r)
        scale = width4 * HM[0, r + 1, pl.ds(c, n), :] * size
        lm, mm = [], []
        for at, (a, b) in enumerate(PAIRS):
            mixed = scale * dev[at] - smooth(MX, at, r, c, n, 10 + at, r)
            leonard = smooth(PX, at, r, c, n, 4 + at, r) - hm[a] * hv[b]
            lm.append(leonard * mixed)
            mm.append(mixed * mixed)
        for q, terms in enumerate((lm, mm)):
            diagonal, cross = (sum(terms[a] for a in group) for group in (DIAGONAL, CROSS))
            part[r, pl.ds(q, 1), :] = jnp.sum(diagonal + 2.0 * cross, axis=0, keepdims=True)

    def first_two(first, count, with_pairs=True):
        sweep(first, count, lambda r: first_pass(r, with_pairs))
        sweep(first, count, hat_pass)

    def close(first, count):
        sweep(first, count, model_pass)
        sweep(first, count, closure_pass)

    seam_far = pick(LANES - 1, 1)

    def other_half(i):
        n, c = wide, outer_cols
        inv_r, az_scale, width = (spread(geo_ref[g, other], n) for g in (0, 1, 2))
        lo = jnp.maximum(i - 1, jnp.where(has_lo, -1, 0)) + 1
        hi = jnp.minimum(i + 1, jnp.where(has_hi, nx, nx - 1)) + 1
        vel = [T[1 + a, i + 1, pl.ds(c, n), :] for a in range(3)]
        dx = [T[1 + a, hi, pl.ds(c, n), :] - T[1 + a, lo, pl.ds(c, n), :] for a in range(3)]
        dr = []
        for a in range(3):
            far = pltpu.roll(S[1 + a, own_at + i, pl.ds(c, n), :], pick(1, LANES - 1), 1)
            before_, after_ = sides(vel[a], jnp.where(lane_of(far) == pick(0, LANES - 1), far, vel[a]))
            dr.append((after_ - before_) * (0.5 / STEP_RADIAL))
        dt = [turn_slope(T, 1 + a, i + 1, c, n) * az_scale for a in range(3)]
        dev, size = strain(dx, dr, dt, vel[1], vel[2], inv_r)
        scale = T[0, i + 1, pl.ds(c, n), :] * width * size
        for a in range(6):
            M[other, a, own_row + i + 1, pl.ds(c, n), :] = scale * dev[a]

    def rows_of(first, count, body):
        def step(at, carry):
            body(first + at)
            return carry

        lax.fori_loop(0, count, step, 0)

    for c in own:
        c.wait()
    pack_seam()
    pl.semaphore_wait(barrier, peers)
    start([seam_swap] + swap_ends)
    start(seam_own + own_around)

    @pl.when(has_near)
    def _():
        start([seam_near] + near_ends + near_rows)

    for q in [nx - 1, nx - 2] + list(range(nx - 2)):
        start(swap_rows[q])
    swap_vel.start()

    seam_swap.wait_recv()
    start(seam_partner_around)

    @pl.when(has_far)
    def _():
        seam_pass.start()
        seam_near.wait_recv()
        start(seam_beyond_around)

    arrive(own_around)
    rows_of(1, nx - 2, other_half)

    @pl.when(has_near)
    def _():
        seam_pass.wait_recv()
        start(seam_ahead_around)

    arrive(swap_ends)
    start(partner_around)

    @pl.when(has_far)
    def _():
        start(pass_ends)
        arrive(near_ends)
        start(beyond_around)

    arrive(seam_own + seam_partner_around)

    @pl.when(has_far)
    def _():
        arrive(seam_beyond_around)

    @pl.when(has_near)
    def _():
        arrive(seam_ahead_around)

    seam_pass_all()
    first_two(1, nx - 2)

    @pl.when(has_near)
    def _():
        arrive(pass_ends)
        start(ahead_around)

    for at in range(2):
        arrive(swap_rows[nx - 1 - at])

        @pl.when(has_far)
        def _():
            pass_rows[at].start()

    @pl.when(has_far)
    def _():
        arrive(near_rows)
        arrive(beyond_around)

    arrive(partner_around)
    first_two(pr - 1, 1)
    first_two(pr, 1, False)
    for q in range(nx - 3):
        arrive(swap_rows[q])
        first_two(nx - 1 + q, 1)
        close(nx - 2 + q, 1)

    @pl.when(has_near)
    def _():
        edge_vel.start()
        arrive(pass_rows)
        arrive(ahead_around)

    first_two(-1, 1, False)
    first_two(0, 1)
    close(0, 2)
    arrive(swap_rows[nx - 3])
    swap_stress.start()

    @pl.when(has_near)
    def _():
        edge_stress.start()

    first_two(pr - 4, 3)
    close(pr - 5, 5)

    def share(at, src, dst, ax, d):
        return pltpu.make_async_remote_copy(
            src_ref=src, dst_ref=dst, send_sem=sum_send.at[at], recv_sem=sum_recv.at[at],
            device_id=(ax, lax.rem(me_az + d, n_az)), device_id_type=MESH_ID)

    def end_row(kind, half, row, ax):
        return [
            share((2 + 2 * kind + half) * n_az + d, part.at[row], rec_out.at[half, me_az], ax, d)
            for d in range(n_az)
        ]

    across = [share(d, part, rec.at[mine, me_az], me_ax, d) for d in range(1, n_az)]
    over = [share(n_az + d, part, rec.at[mine, me_az], partner, d) for d in range(n_az)]
    lower_ax, upper_ax = me_ax - odd - 1, me_ax - odd + 2
    down, up = end_row(0, mine, 0, lower_ax), end_row(1, mine, pr - 1, upper_ax)
    end_sums = end_row(even, 0, 0, me_ax) + end_row(even, 1, 0, me_ax)

    @pl.when(pair_lo)
    def _():
        start(down)

    @pl.when(pair_hi)
    def _():
        start(up)

    start(over)
    start(across)
    rec[mine, me_az] = part[...]
    swap_vel.wait_recv()
    start(swap_vel_around)

    @pl.when(has_near)
    def _():
        edge_vel.wait_recv()
        start(edge_vel_around)

    arrive(swap_vel_around)
    other_half(swap_row)

    @pl.when(has_near)
    def _():
        arrive(edge_vel_around)

    other_half(edge_row)

    def ratio(sums):
        lm, mm = sums[0:1], sums[1:2]
        return -0.5 * (lm * (1.0 / azimuth_cells)) / (mm * (1.0 / azimuth_cells) + TINY)

    def total(ref, h, row):
        terms = [ref[h, d] if row is None else ref[h, d, row] for d in range(n_az)]
        sums = terms[0]
        for x in terms[1:]:
            sums = sums + x
        return sums

    def keep(row, h, value):
        CS[row, h] = jnp.broadcast_to(-2.0 * value, (SUB, LANES))

    arrive(across)
    arrive(over)
    for i in range(nx + 1):
        row = i + even
        for h in range(2):
            keep(row, h, ratio(total(rec, h, own_row + row - 1)))
    for i in range(nx):
        for h in range(2):
            coef_ref[pl.ds(i, 1), pl.ds(h * LANES, LANES)] = -0.5 * CS[i + 1, h, pl.ds(0, 1), :]

    def flux_pass(i):
        n, c = nt, EDGE
        r = own_row + i + 1
        inv_r, az_scale, radius, back, radius2, back2 = (spread(geo_ref[g], n) for g in (0, 1, 4, 5, 6, 7))
        lo = jnp.maximum(i - 1, jnp.where(has_lo, -1, 0)) + 1
        hi = jnp.minimum(i + 1, jnp.where(has_hi, nx, nx - 1)) + 1
        here, below, above = (spread(CS[q], n) for q in (i + 1, lo, hi))

        def at(a, row, shift=0):
            return M[:, a, row, pl.ds(c + shift, n), :]

        def axial(a):
            return above * at(a, own_row + hi) - below * at(a, own_row + lo)

        def around_of(a):
            return (at(a, r, 1) - at(a, r, -1)) * turn

        turn = here * az_scale
        once = here * radius
        d_xr = rise(once * at(1, r)) * back
        d_rr = rise(once * at(3, r)) * back
        d_rt = rise(here * radius2 * at(5, r)) * back2
        out = (
            axial(0) + d_xr + around_of(2),
            axial(1) + d_rr + around_of(5) - here * at(4, r) * inv_r,
            axial(2) + d_rt + around_of(4),
        )
        for a in range(3):
            for h in range(2):
                flux_ref[a, i, :, pl.ds(h * LANES, LANES)] = out[a][h]

    rows_of(1, nx - 2, flux_pass)

    @pl.when(has_near)
    def _():
        arrive(end_sums)

    swap_stress.wait_recv()
    flux_pass(swap_row)

    @pl.when(has_near)
    def _():
        for h in range(2):
            keep(pick(0, nx + 1), h, ratio(total(rec_out, h, None)))
        edge_stress.wait_recv()

    flux_pass(edge_row)

    leave([seam_swap, swap_vel, swap_stress] + swap_ends + own_around + seam_own + seam_partner_around)
    leave(partner_around + swap_vel_around + across + over)
    for q in range(nx):
        leave(swap_rows[q])

    @pl.when(has_near)
    def _():
        leave([seam_near, edge_vel, edge_stress] + near_ends + near_rows)
        leave(seam_ahead_around + ahead_around + edge_vel_around)

    @pl.when(has_far)
    def _():
        leave([seam_pass] + pass_ends + pass_rows + seam_beyond_around + beyond_around)

    @pl.when(pair_lo)
    def _():
        leave(down)

    @pl.when(pair_hi)
    def _():
        leave(up)


def hand_over(flux_in, coef_in, flux_out, coef_out, flux_buf, coef_buf, sems):
    count = flux_in.shape[0]
    pieces = [(flux_in.at[a], flux_buf.at[a], flux_out.at[a]) for a in range(count)]
    pieces.append((coef_in, coef_buf, coef_out))
    take = [pltpu.make_async_copy(a, b, sems.at[0, at]) for at, (a, b, _) in enumerate(pieces)]
    give = [pltpu.make_async_copy(b, c, sems.at[1, at]) for at, (_, b, c) in enumerate(pieces)]
    for c in take:
        c.start()
    for arrive, leave in zip(take, give):
        arrive.wait()
        leave.start()
    for c in give:
        c.wait()


def shards(n_ax, n_az, density, velocity):
    nx, nt, radial = density.shape
    assert radial == 2 * LANES and 2 * 4 * nx * SEAM == LANES and n_ax % 2 == 0
    pr, seam_rows = 2 * nx, nt // 2 + 2 * SUB
    halves, seam = geometry(radial, nt * n_az)

    def field(*lead):
        return pltpu.VMEM(lead + (nt + 2 * EDGE, LANES), jnp.float32)

    def vmem(*shape):
        return pltpu.VMEM(shape, jnp.float32)

    dma = pltpu.SemaphoreType.DMA
    flux, coef = pl.pallas_call(
        functools.partial(kernel, n_ax, n_az, nx, nt),
        out_shape=(
            jax.ShapeDtypeStruct(velocity.shape, jnp.float32),
            jax.ShapeDtypeStruct((nx, radial), jnp.float32),
        ),
        in_specs=[
            pl.BlockSpec(memory_space=pl.ANY),
            pl.BlockSpec(memory_space=pl.ANY),
            pl.BlockSpec(memory_space=pltpu.VMEM),
            pl.BlockSpec(memory_space=pltpu.VMEM),
        ],
        out_specs=(
            pl.BlockSpec(memory_space=pltpu.VMEM),
            pl.BlockSpec(memory_space=pltpu.VMEM),
        ),
        scratch_shapes=[
            field(4, pr + 4),
            field(4, nx + 2),
            field(2, 6, pr + 2),
            field(4, pr + 2),
            field(3, pr + 2),
            field(4, pr + 2),
            field(6, pr),
            field(6, pr),
            vmem(4, seam_rows, LANES),
            field(4),
            field(6),
            field(4),
            field(6),
            field(16),
            field(3),
            vmem(pr, 2, LANES),
            vmem(2, n_az, pr, 2, LANES),
            vmem(2, n_az, 2, LANES),
            vmem(nx + 2, 2, SUB, LANES),
            dma((4,)),
            dma((COPIES,)),
            dma((COPIES,)),
            dma((6 * n_az,)),
            dma((6 * n_az,)),
        ],
        compiler_params=pltpu.CompilerParams(collective_id=0, has_side_effects=True),
        name="closure",
    )(density, velocity, jnp.asarray(halves), jnp.asarray(seam))
    anywhere = pl.BlockSpec(memory_space=pl.ANY)
    return pl.pallas_call(
        hand_over,
        out_shape=(
            jax.ShapeDtypeStruct(flux.shape, jnp.float32),
            jax.ShapeDtypeStruct(coef.shape, jnp.float32),
        ),
        in_specs=[anywhere, anywhere],
        out_specs=(anywhere, anywhere),
        scratch_shapes=[
            pltpu.VMEM(flux.shape, jnp.float32),
            pltpu.VMEM(coef.shape, jnp.float32),
            dma((2, flux.shape[0] + 1)),
        ],
        name="hand_over",
    )(flux, coef)


def solution(mesh):
    in_specs = (P("ax", "az", None), P(None, "ax", "az", None))
    out_specs = (P(None, "ax", "az", None), P("ax", None))
    body = functools.partial(shards, mesh.shape["ax"], mesh.shape["az"])
    return jax.shard_map(body, mesh=mesh, in_specs=in_specs, out_specs=out_specs, check_vma=False)
```

```python
import functools
import itertools
import math

import jax
import jax.numpy as jnp
import numpy as np
from jax import lax
from jax.experimental import pallas as pl
from jax.experimental.pallas import tpu as pltpu
from jax.sharding import PartitionSpec as P

STEP_AXIAL = 0.5
STEP_RADIAL = 0.25
INNER_RADIUS = 10.0
FILTER_RATIO = 2.0
TINY = 1e-06
PAIRS = ((0, 0), (0, 1), (0, 2), (1, 1), (2, 2), (1, 2))
DIAGONAL = (0, 3, 4)
CROSS = (1, 2, 5)
LANES = 128
SUB = 8
EDGE = 16
SEAM = 4
COPIES = 64
BLOCKS = {'first': 16, 'hat': 16, 'model': 16, 'closure': 16, 'other': 16, 'flux': 16, 'seam': 16}
MESH_ID = pl.DeviceIdType.MESH


def geometry(radial, azimuth_cells):
    radius = INNER_RADIUS + (np.arange(radial, dtype=np.float64) + 0.5) * STEP_RADIAL
    angle = 2.0 * math.pi / azimuth_cells
    width = (STEP_AXIAL * STEP_RADIAL * angle * radius) ** (2.0 / 3.0)
    rows = np.stack(
        [
            1.0 / radius,
            0.5 / (radius * angle),
            width,
            FILTER_RATIO**2 * width,
            radius,
            0.5 / STEP_RADIAL / radius,
            radius * radius,
            0.5 / STEP_RADIAL / (radius * radius),
        ]
    ).astype(np.float32)
    halves = rows.reshape(rows.shape[0], radial // LANES, 1, LANES)
    at_seam = radial // 2 - SEAM // 2 + np.arange(LANES) % SEAM
    seam = rows[:4, None, at_seam]
    return (
        np.ascontiguousarray(np.broadcast_to(halves, halves.shape[:2] + (SUB, LANES))),
        np.ascontiguousarray(np.broadcast_to(seam, (4, SUB, LANES))),
    )


def lane_of(x):
    return lax.broadcasted_iota(jnp.int32, x.shape, x.ndim - 1)


def before(x):
    y = pltpu.roll(x, 1, x.ndim - 1)
    fill = jnp.concatenate([x[:1], y[:-1]], axis=0)
    return jnp.where(lane_of(x) == 0, fill, y)


def after(x):
    y = pltpu.roll(x, LANES - 1, x.ndim - 1)
    fill = jnp.concatenate([y[1:], x[-1:]], axis=0)
    return jnp.where(lane_of(x) == LANES - 1, fill, y)


def rise(x):
    return after(x) - before(x)


def sides(x, end):
    lane = lane_of(x)
    return (
        jnp.where(lane == 0, end, pltpu.roll(x, 1, 1)),
        jnp.where(lane == LANES - 1, end, pltpu.roll(x, LANES - 1, 1)),
    )


def strain(dx, dr, dt, ur, ut, inv_r):
    s_xx, s_rr = dx[0], dr[1]
    s_tt = dt[2] + ur * inv_r
    s_xr = 0.5 * (dr[0] + dx[1])
    s_xt = 0.5 * (dt[0] + dx[2])
    s_rt = 0.5 * (dt[1] + dr[2] - ut * inv_r)
    size = jnp.sqrt(
        2.0
        * (
            s_xx * s_xx
            + s_rr * s_rr
            + s_tt * s_tt
            + 2.0 * (s_xr * s_xr + s_xt * s_xt + s_rt * s_rt)
        )
    )
    third = (s_xx + s_rr + s_tt) * (1.0 / 3.0)
    return (s_xx - third, s_xr, s_xt, s_rr - third, s_tt - third, s_rt), size


def kernel(
    n_ax, n_az, nx, nt,
    rho_ref, vel_ref, geo_in, seam_in, flux_ref, coef_ref,
    S, T, M, H, V, HM, PX, MX, E, G, GM, GH, GP, GX, GV,
    part, rec, rec_out, CS, geo_ref, seam_ref, own_sem, send_sem, recv_sem, sum_send, sum_recv,
):
    pr = 2 * nx
    me_ax, me_az = lax.axis_index("ax"), lax.axis_index("az")
    left, right = lax.rem(me_az + n_az - 1, n_az), lax.rem(me_az + 1, n_az)
    odd = lax.rem(me_ax, 2)
    even = 1 - odd
    mine, other = odd, even
    azimuth_cells = nt * n_az

    def pick(at_even, at_odd):
        return jnp.where(odd == 0, at_even, at_odd)

    has_lo, has_hi = me_ax > 0, me_ax < n_ax - 1
    pair_lo, pair_hi = me_ax >= 2, me_ax < n_ax - 2
    partner = me_ax + 1 - 2 * odd
    near_ax = me_ax - 2 + 4 * odd
    far_ax = me_ax + 2 - 4 * odd
    edge_ax = me_ax - 1 + 2 * odd
    has_near = (near_ax >= 0) & (near_ax < n_ax)
    has_far = (far_ax >= 0) & (far_ax < n_ax)

    lanes_mine = pl.ds(pl.multiple_of(mine * LANES, LANES), LANES)
    lanes_other = pl.ds(pl.multiple_of(other * LANES, LANES), LANES)
    cols = pl.ds(EDGE, nt)
    own_row = nx * odd
    own_at = own_row + 2
    partner_at = nx * even + 2
    near_at = pick(0, nx - 2)
    beyond_at = pick(pr + 2, 0)
    ahead_at = pick(0, pr + 2)
    pass_at = pick(pr, 2)

    own = [
        pltpu.make_async_copy(rho_ref.at[:, :, lanes_mine], S.at[0, pl.ds(own_at, nx), cols, :], own_sem.at[0]),
        pltpu.make_async_copy(
            vel_ref.at[:, :, :, lanes_mine], S.at[pl.ds(1, 3), pl.ds(own_at, nx), cols, :], own_sem.at[1]),
        pltpu.make_async_copy(rho_ref.at[:, :, lanes_other], T.at[0, pl.ds(1, nx), cols, :], own_sem.at[2]),
        pltpu.make_async_copy(
            vel_ref.at[:, :, :, lanes_other], T.at[pl.ds(1, 3), pl.ds(1, nx), cols, :], own_sem.at[3]),
    ]
    tables = [
        pltpu.make_async_copy(geo_in, geo_ref, own_sem.at[4]),
        pltpu.make_async_copy(seam_in, seam_ref, own_sem.at[5]),
    ]
    for c in own + tables:
        c.start()

    barrier = pltpu.get_barrier_semaphore()

    def greet(ax, az):
        pl.semaphore_signal(barrier, inc=1, device_id=(ax, az), device_id_type=MESH_ID)

    for d in range(1, n_az):
        greet(me_ax, lax.rem(me_az + d, n_az))
    peers = n_az - 1
    for step in (-1, 1, -2, 2):
        there = (me_ax + step >= 0) & (me_ax + step < n_ax)

        @pl.when(there)
        def _():
            for d in range(n_az):
                greet(me_ax + step, lax.rem(me_az + d, n_az))

        peers = peers + jnp.where(there, n_az, 0)

    ids = itertools.count()

    def remote(src, dst, ax, az):
        at = next(ids)
        return pltpu.make_async_remote_copy(
            src_ref=src, dst_ref=dst, send_sem=send_sem.at[at], recv_sem=recv_sem.at[at],
            device_id=(ax, az), device_id_type=MESH_ID)

    def block(src_row, count, first, width, lanes, dst, dst_row, dst_first, ax, az):
        rows, at = pl.ds(src_row, count), pl.ds(first, width)
        to_rows, to = pl.ds(dst_row, count), pl.ds(dst_first, width)
        return [
            remote(rho_ref.at[rows, at, lanes], dst.at[0, to_rows, to, :], ax, az),
            remote(vel_ref.at[:, rows, at, lanes], dst.at[pl.ds(1, 3), to_rows, to, :], ax, az),
        ]

    def ends(src_row, count, lanes, dst, dst_row, ax, az):
        out = []
        for first in (0, nt - SUB):
            out += block(src_row, count, first, SUB, lanes, dst, dst_row, EDGE + first, ax, az)
        return out

    def middle(src_row, count, lanes, dst, dst_row, ax, az):
        return block(src_row, count, SUB, nt - 2 * SUB, lanes, dst, dst_row, EDGE + SUB, ax, az)

    def around(ref, lead, rows):
        at = (pl.ds(EDGE + nt - SUB, SUB), pl.ds(EDGE - SUB, SUB), pl.ds(EDGE, SUB), pl.ds(EDGE + nt, SUB))
        return [
            remote(ref.at[lead, rows, at[0], :], ref.at[lead, rows, at[1], :], me_ax, right),
            remote(ref.at[lead, rows, at[2], :], ref.at[lead, rows, at[3], :], me_ax, left),
        ]

    fold = nt // 2
    whole = pl.ds(SUB, fold)

    def seam_around(s):
        return [
            remote(E.at[s, pl.ds(fold, SUB), :], E.at[s, pl.ds(0, SUB), :], me_ax, right),
            remote(E.at[s, pl.ds(SUB, SUB), :], E.at[s, pl.ds(SUB + fold, SUB), :], me_ax, left),
        ]

    s_own, s_partner, s_beyond, s_ahead = 1 + odd, 2 - odd, pick(3, 0), pick(0, 3)

    own_around = []
    for lanes, dst, row in ((lanes_mine, S, own_at), (lanes_other, T, 1)):
        own_around += block(0, nx, nt - SUB, SUB, lanes, dst, row, EDGE - SUB, me_ax, right)
        own_around += block(0, nx, 0, SUB, lanes, dst, row, EDGE + nt, me_ax, left)
    seam_own = seam_around(s_own)
    seam_partner_around = seam_around(s_partner)
    seam_beyond_around = seam_around(s_beyond)
    seam_ahead_around = seam_around(s_ahead)

    seam_swap = remote(E.at[s_own, whole, :], E.at[s_own, whole, :], partner, me_az)
    seam_near = remote(E.at[s_own, whole, :], E.at[pick(3, 0), whole, :], near_ax, me_az)
    seam_pass = remote(E.at[s_partner, whole, :], E.at[pick(0, 3), whole, :], far_ax, me_az)

    swap_ends = ends(0, nx, lanes_other, S, own_at, partner, me_az)
    swap_rows = {}
    for q in range(nx):
        row = pick(nx - 1 - q, q)
        swap_rows[q] = middle(row, 1, lanes_other, S, own_at + row, partner, me_az)
    near_ends = ends(near_at, 2, lanes_mine, S, beyond_at, near_ax, me_az)
    near_rows = middle(near_at, 2, lanes_mine, S, beyond_at, near_ax, me_az)

    every = pl.ds(0, 4)

    def forward(row, first, width, count):
        return remote(
            S.at[:, pl.ds(pass_at + row, count), pl.ds(EDGE + first, width), :],
            S.at[:, pl.ds(ahead_at + row, count), pl.ds(EDGE + first, width), :], far_ax, me_az)

    pass_ends = [forward(0, first, SUB, 2) for first in (0, nt - SUB)]
    last_row = pick(1, 0)
    pass_rows = [forward(last_row, SUB, nt - 2 * SUB, 1), forward(1 - last_row, SUB, nt - 2 * SUB, 1)]
    partner_around = around(S, every, pl.ds(partner_at, nx))
    beyond_around = around(S, every, pl.ds(beyond_at, 2))
    ahead_around = around(S, every, pl.ds(ahead_at, 2))

    swap_row, edge_row = pick(nx - 1, 0), pick(0, nx - 1)
    three = pl.ds(1, 3)

    def flux_rows(row, dst_row, ax):
        return remote(
            vel_ref.at[:, pl.ds(row, 1), :, lanes_mine], T.at[three, pl.ds(dst_row, 1), cols, :], ax, me_az)

    def flux_stress(row, dst_row, ax):
        return remote(
            M.at[mine, pl.ds(0, 3), own_row + row + 1, cols, :], M.at[mine, pl.ds(0, 3), dst_row, cols, :],
            ax, me_az)

    swap_vel = flux_rows(swap_row, pick(0, nx + 1), partner)
    edge_vel = flux_rows(edge_row, pick(nx + 1, 0), edge_ax)
    swap_vel_around = around(T, three, pl.ds(pick(nx + 1, 0), 1))
    edge_vel_around = around(T, three, pl.ds(pick(0, nx + 1), 1))
    swap_stress = flux_stress(swap_row, pick(nx, nx + 1), partner)
    edge_stress = flux_stress(edge_row, pick(pr + 1, 0), edge_ax)

    def start(copies):
        for c in copies:
            c.start()

    def arrive(copies):
        for c in copies:
            c.wait_recv()

    def leave(copies):
        for c in copies:
            c.wait_send()

    wide = nt + 2 * SUB
    outer_cols = EDGE - SUB

    def lanes_at(n):
        return lax.broadcasted_iota(jnp.int32, (n, LANES), 1)

    def spread(values, rows):
        return jnp.concatenate([values] * (rows // SUB), axis=values.ndim - 2)

    def pack_seam():
        lane = lanes_at(nt)
        from_mine = jnp.where(lane >= LANES - SEAM // 2, 1, 0) == even
        half = lanes_at(fold)
        packed = jnp.zeros((fold, LANES), jnp.float32)
        for a in range(4):
            for i in range(nx):
                first = (a * nx + i) * SEAM
                x = jnp.where(from_mine, S[a, own_at + i, pl.ds(EDGE, nt), :], T[a, 1 + i, pl.ds(EDGE, nt), :])
                low = pltpu.roll(x[:fold], (first + SEAM // 2) % LANES, 1)
                high = pltpu.roll(x[fold:], (first + SEAM // 2 + LANES // 2) % LANES, 1)
                packed = jnp.where((half >= first) & (half < first + SEAM), low, packed)
                first += LANES // 2
                packed = jnp.where((half >= first) & (half < first + SEAM), high, packed)
        E[s_own, pl.ds(SUB, fold), :] = packed

    n_seam = math.gcd(BLOCKS["seam"], wide)
    seam_lane = lanes_at(n_seam)
    seam_row = seam_lane // SEAM
    at_bottom = seam_row == jnp.where(pair_lo, -1, nx)
    at_top = seam_row == jnp.where(pair_hi, -1, nx + pr - 1)

    def seam_below(x):
        return jnp.where(at_bottom, x, pltpu.roll(x, SEAM, 1))

    def seam_above(x):
        return jnp.where(at_top, x, pltpu.roll(x, LANES - SEAM, 1))

    def seam_axial(x):
        return (seam_below(x) + x) + (x + seam_above(x))

    def seam_rise(x):
        return pltpu.roll(x, LANES - 1, 1) - pltpu.roll(x, 1, 1)

    def seam_turn(ref, a, c, n):
        x = ref[a, pl.ds(c, n), :]
        return (ref[a, pl.ds(c - 1, n), :] + ref[a, pl.ds(c + 1, n), :]) + (x + x)

    def seam_pass_all():
        lane = lanes_at(fold + SUB)
        per = nx * SEAM
        for a in range(4):
            low = jnp.zeros((fold + SUB, LANES), jnp.float32)
            high = low
            for s in range(4):
                here = (lane >= s * per) & (lane < (s + 1) * per)
                x = pltpu.roll(E[s, pl.ds(SUB, fold + SUB), :], (s * per - a * per) % LANES, 1)
                low = jnp.where(here, x, low)
                x = pltpu.roll(E[s, pl.ds(0, fold + SUB), :], (s * per - a * per - LANES // 2) % LANES, 1)
                high = jnp.where(here, x, high)
            G[a, pl.ds(EDGE - SUB, SUB), :] = high[:SUB]
            G[a, pl.ds(EDGE, fold), :] = low[:fold]
            G[a, pl.ds(EDGE + fold, fold), :] = high[SUB:]
            G[a, pl.ds(EDGE + nt, SUB), :] = low[fold:]
        parts = [(c, n_seam) for c in range(outer_cols, outer_cols + wide, n_seam)]
        for c, n in parts:
            at, at_before, at_after = pl.ds(c, n), pl.ds(c - 1, n), pl.ds(c + 1, n)
            rho = G[0, at, :]
            vel = [G[1 + a, at, :] for a in range(3)]
            inv_r, az_scale, width = (spread(seam_ref[g], n) for g in (0, 1, 2))
            dx = [seam_above(v) - seam_below(v) for v in vel]
            dr = [seam_rise(v) * (0.5 / STEP_RADIAL) for v in vel]
            dt = [(G[1 + a, at_after, :] - G[1 + a, at_before, :]) * az_scale for a in range(3)]
            dev, size = strain(dx, dr, dt, vel[1], vel[2], inv_r)
            scale = rho * width * size
            for a in range(6):
                GM[a, at, :] = seam_axial(scale * dev[a])
            mom = [rho * v for v in vel]
            GH[0, at, :] = seam_axial(rho)
            for a in range(3):
                GH[1 + a, at, :] = seam_axial(mom[a])
            for q, (a, b) in enumerate(PAIRS):
                GP[q, at, :] = seam_axial(mom[a] * vel[b])
        for c, n in parts:
            at = pl.ds(c, n)
            hat = []
            for a in range(4):
                s = seam_turn(GH, a, c, n)
                GX[a, at, :] = s
                hat.append(((pltpu.roll(s, 1, 1) + pltpu.roll(s, LANES - 1, 1)) + (s + s)) * (1.0 / 64.0))
            inv = 1.0 / hat[0]
            for a in range(3):
                GV[a, at, :] = hat[1 + a] * inv
            for a in range(6):
                GX[4 + a, at, :] = seam_turn(GP, a, c, n)
                GX[10 + a, at, :] = seam_turn(GM, a, c, n)

    end_lane = pick(LANES - 1, 0)

    def seam_end(x, ref, a, first, r):
        shift = pick(LANES - 1 - SEAM // 2, LANES - SEAM // 2 + 1) - SEAM * (r + nx)
        g = pltpu.roll(ref[a, pl.ds(first, x.shape[0]), :], shift, 1)
        return jnp.where(lane_of(x) == end_lane, g, x)

    def seam_slope(x, ref, a, first, r):
        lo, hi = sides(x, seam_end(x, ref, a, first, r))
        return hi - lo

    def smooth(ref, a, row, first, n, at, r):
        x = ref[a, row, pl.ds(first, n), :]
        s = (ref[a, row, pl.ds(first - 1, n), :] + ref[a, row, pl.ds(first + 1, n), :]) + (x + x)
        lo, hi = sides(s, seam_end(s, GX, at, first, r))
        return ((lo + hi) + (s + s)) * (1.0 / 64.0)

    def low(r):
        return jnp.maximum(r - 1, jnp.where(pair_lo, -2, 0))

    def high(r):
        return jnp.minimum(r + 1, jnp.where(pair_hi, pr + 1, pr - 1))

    def sweep(first, count, body):
        def step(at, carry):
            t = first + at
            body(pick(t, pr - 1 - t))
            return carry

        lax.fori_loop(0, count, step, 0)

    def turn_slope(ref, a, row, first, n):
        return ref[a, row, pl.ds(first + 1, n), :] - ref[a, row, pl.ds(first - 1, n), :]

    def first_pass(r, with_pairs):
        n = math.gcd(BLOCKS["first"], wide)
        for c in range(outer_cols, outer_cols + wide, n):
            rows = (low(r) + 2, r + 2, high(r) + 2)
            rho = [S[0, q, pl.ds(c, n), :] for q in rows]
            vel = [[S[1 + a, q, pl.ds(c, n), :] for a in range(3)] for q in rows]
            inv_r, az_scale, width = (spread(geo_ref[g, mine], n) for g in (0, 1, 2))
            dx = [vel[2][a] - vel[0][a] for a in range(3)]
            dr = [seam_slope(vel[1][a], G, 1 + a, c, r) * (0.5 / STEP_RADIAL) for a in range(3)]
            dt = [turn_slope(S, 1 + a, r + 2, c, n) * az_scale for a in range(3)]
            dev, size = strain(dx, dr, dt, vel[1][1], vel[1][2], inv_r)
            scale = rho[1] * width * size
            for a in range(6):
                M[mine, a, r + 1, pl.ds(c, n), :] = scale * dev[a]
            mom = [[rho[q] * vel[q][a] for a in range(3)] for q in range(3)]
            H[0, r + 1, pl.ds(c, n), :] = (rho[0] + rho[1]) + (rho[1] + rho[2])
            for a in range(3):
                H[1 + a, r + 1, pl.ds(c, n), :] = (mom[0][a] + mom[1][a]) + (mom[1][a] + mom[2][a])
            if with_pairs:
                for at, (a, b) in enumerate(PAIRS):
                    p = [mom[q][a] * vel[q][b] for q in range(3)]
                    PX[at, r, pl.ds(c, n), :] = (p[0] + p[1]) + (p[1] + p[2])

    def hat_pass(r):
        n = math.gcd(BLOCKS["hat"], wide)
        for c in range(outer_cols, outer_cols + wide, n):
            hat = [smooth(H, a, r + 1, c, n, a, r) for a in range(4)]
            inv = 1.0 / hat[0]
            for a in range(4):
                HM[a, r + 1, pl.ds(c, n), :] = hat[a]
            for a in range(3):
                V[a, r + 1, pl.ds(c, n), :] = hat[1 + a] * inv

    def model_pass(r):
        n = math.gcd(BLOCKS["model"], wide)
        for c in range(outer_cols, outer_cols + wide, n):
            for a in range(6):
                x = M[mine, a, r + 1, pl.ds(c, n), :]
                lo = M[mine, a, low(r) + 1, pl.ds(c, n), :]
                MX[a, r, pl.ds(c, n), :] = (lo + x) + (x + M[mine, a, high(r) + 1, pl.ds(c, n), :])

    def closure_pass(r):
        sums = [0.0, 0.0]
        n = math.gcd(BLOCKS["closure"], nt)
        for c in range(EDGE, EDGE + nt, n):
            inv_r, az_scale, width4 = (spread(geo_ref[g, mine], n) for g in (0, 1, 3))
            hv = [V[a, r + 1, pl.ds(c, n), :] for a in range(3)]
            hm = [HM[1 + a, r + 1, pl.ds(c, n), :] for a in range(3)]
            dx = [V[a, high(r) + 1, pl.ds(c, n), :] - V[a, low(r) + 1, pl.ds(c, n), :] for a in range(3)]
            dr = [seam_slope(hv[a], GV, a, c, r) * (0.5 / STEP_RADIAL) for a in range(3)]
            dt = [turn_slope(V, a, r + 1, c, n) * az_scale for a in range(3)]
            dev, size = strain(dx, dr, dt, hv[1], hv[2], inv_r)
            scale = width4 * HM[0, r + 1, pl.ds(c, n), :] * size
            lm, mm = [], []
            for at, (a, b) in enumerate(PAIRS):
                mixed = scale * dev[at] - smooth(MX, at, r, c, n, 10 + at, r)
                leonard = smooth(PX, at, r, c, n, 4 + at, r) - hm[a] * hv[b]
                lm.append(leonard * mixed)
                mm.append(mixed * mixed)
            for q, terms in enumerate((lm, mm)):
                diagonal, cross = (sum(terms[a] for a in group) for group in (DIAGONAL, CROSS))
                cells = diagonal + 2.0 * cross
                sums[q] += sum(cells[at:at + SUB] for at in range(0, n, SUB))
        for q in range(2):
            part[r, pl.ds(q, 1), :] = jnp.sum(sums[q], axis=0, keepdims=True)

    def first_two(first, count, with_pairs=True):
        sweep(first, count, lambda r: first_pass(r, with_pairs))
        sweep(first, count, hat_pass)

    def close(first, count):
        sweep(first, count, model_pass)
        sweep(first, count, closure_pass)

    seam_far = pick(LANES - 1, 1)

    def other_half(i):
        n = math.gcd(BLOCKS["other"], wide)
        for c in range(outer_cols, outer_cols + wide, n):
            inv_r, az_scale, width = (spread(geo_ref[g, other], n) for g in (0, 1, 2))
            lo = jnp.maximum(i - 1, jnp.where(has_lo, -1, 0)) + 1
            hi = jnp.minimum(i + 1, jnp.where(has_hi, nx, nx - 1)) + 1
            vel = [T[1 + a, i + 1, pl.ds(c, n), :] for a in range(3)]
            dx = [T[1 + a, hi, pl.ds(c, n), :] - T[1 + a, lo, pl.ds(c, n), :] for a in range(3)]
            dr = []
            for a in range(3):
                far = pltpu.roll(S[1 + a, own_at + i, pl.ds(c, n), :], pick(1, LANES - 1), 1)
                before_, after_ = sides(vel[a], jnp.where(lane_of(far) == pick(0, LANES - 1), far, vel[a]))
                dr.append((after_ - before_) * (0.5 / STEP_RADIAL))
            dt = [turn_slope(T, 1 + a, i + 1, c, n) * az_scale for a in range(3)]
            dev, size = strain(dx, dr, dt, vel[1], vel[2], inv_r)
            scale = T[0, i + 1, pl.ds(c, n), :] * width * size
            for a in range(6):
                M[other, a, own_row + i + 1, pl.ds(c, n), :] = scale * dev[a]

    def rows_of(first, count, body):
        def step(at, carry):
            body(first + at)
            return carry

        lax.fori_loop(0, count, step, 0)

    for c in own:
        c.wait()
    pack_seam()
    pl.semaphore_wait(barrier, peers)
    start([seam_swap] + swap_ends)
    start(seam_own + own_around)

    @pl.when(has_near)
    def _():
        start([seam_near] + near_ends + near_rows)

    for q in [nx - 1, nx - 2] + list(range(nx - 2)):
        start(swap_rows[q])
    swap_vel.start()

    seam_swap.wait_recv()
    start(seam_partner_around)

    @pl.when(has_far)
    def _():
        seam_pass.start()
        seam_near.wait_recv()
        start(seam_beyond_around)

    arrive(own_around)
    for c in tables:
        c.wait()
    rows_of(1, nx - 2, other_half)

    @pl.when(has_near)
    def _():
        seam_pass.wait_recv()
        start(seam_ahead_around)

    arrive(swap_ends)
    start(partner_around)

    @pl.when(has_far)
    def _():
        start(pass_ends)
        arrive(near_ends)
        start(beyond_around)

    arrive(seam_own + seam_partner_around)

    @pl.when(has_far)
    def _():
        arrive(seam_beyond_around)

    @pl.when(has_near)
    def _():
        arrive(seam_ahead_around)

    seam_pass_all()
    first_two(1, nx - 2)

    @pl.when(has_near)
    def _():
        arrive(pass_ends)
        start(ahead_around)

    for at in range(2):
        arrive(swap_rows[nx - 1 - at])

        @pl.when(has_far)
        def _():
            pass_rows[at].start()

    @pl.when(has_far)
    def _():
        arrive(near_rows)
        arrive(beyond_around)

    arrive(partner_around)
    first_two(pr - 1, 1)
    first_two(pr, 1, False)
    for q in range(nx - 3):
        arrive(swap_rows[q])
        first_two(nx - 1 + q, 1)
        close(nx - 2 + q, 1)

    @pl.when(has_near)
    def _():
        edge_vel.start()
        arrive(pass_rows)
        arrive(ahead_around)

    first_two(-1, 1, False)
    first_two(0, 1)
    close(0, 2)
    arrive(swap_rows[nx - 3])
    swap_stress.start()

    @pl.when(has_near)
    def _():
        edge_stress.start()

    first_two(pr - 4, 3)
    close(pr - 5, 5)

    def share(at, src, dst, ax, d):
        return pltpu.make_async_remote_copy(
            src_ref=src, dst_ref=dst, send_sem=sum_send.at[at], recv_sem=sum_recv.at[at],
            device_id=(ax, lax.rem(me_az + d, n_az)), device_id_type=MESH_ID)

    def end_row(kind, half, row, ax):
        return [
            share((2 + 2 * kind + half) * n_az + d, part.at[row], rec_out.at[half, me_az], ax, d)
            for d in range(n_az)
        ]

    across = [share(d, part, rec.at[mine, me_az], me_ax, d) for d in range(1, n_az)]
    over = [share(n_az + d, part, rec.at[mine, me_az], partner, d) for d in range(n_az)]
    lower_ax, upper_ax = me_ax - odd - 1, me_ax - odd + 2
    down, up = end_row(0, mine, 0, lower_ax), end_row(1, mine, pr - 1, upper_ax)
    end_sums = end_row(even, 0, 0, me_ax) + end_row(even, 1, 0, me_ax)

    @pl.when(pair_lo)
    def _():
        start(down)

    @pl.when(pair_hi)
    def _():
        start(up)

    start(over)
    start(across)
    rec[mine, me_az] = part[...]
    swap_vel.wait_recv()
    start(swap_vel_around)

    @pl.when(has_near)
    def _():
        edge_vel.wait_recv()
        start(edge_vel_around)

    arrive(swap_vel_around)
    other_half(swap_row)

    @pl.when(has_near)
    def _():
        arrive(edge_vel_around)

    other_half(edge_row)

    def ratio(sums):
        lm, mm = sums[0:1], sums[1:2]
        return -0.5 * (lm * (1.0 / azimuth_cells)) / (mm * (1.0 / azimuth_cells) + TINY)

    def total(ref, h, row):
        terms = [ref[h, d] if row is None else ref[h, d, row] for d in range(n_az)]
        sums = terms[0]
        for x in terms[1:]:
            sums = sums + x
        return sums

    def keep(row, h, value):
        CS[row, h] = jnp.broadcast_to(-2.0 * value, (SUB, LANES))

    arrive(across)
    arrive(over)
    for i in range(nx + 1):
        row = i + even
        for h in range(2):
            keep(row, h, ratio(total(rec, h, own_row + row - 1)))
    for i in range(nx):
        for h in range(2):
            coef_ref[pl.ds(i, 1), pl.ds(h * LANES, LANES)] = -0.5 * CS[i + 1, h, pl.ds(0, 1), :]

    def flux_pass(i):
        n = math.gcd(BLOCKS["flux"], nt)
        for c in range(EDGE, EDGE + nt, n):
            r = own_row + i + 1
            inv_r, az_scale, radius, back, radius2, back2 = (spread(geo_ref[g], n) for g in (0, 1, 4, 5, 6, 7))
            lo = jnp.maximum(i - 1, jnp.where(has_lo, -1, 0)) + 1
            hi = jnp.minimum(i + 1, jnp.where(has_hi, nx, nx - 1)) + 1
            here, below, above = (spread(CS[q], n) for q in (i + 1, lo, hi))

            def at(a, row, shift=0):
                return M[:, a, row, pl.ds(c + shift, n), :]

            def axial(a):
                return above * at(a, own_row + hi) - below * at(a, own_row + lo)

            def around_of(a):
                return (at(a, r, 1) - at(a, r, -1)) * turn

            turn = here * az_scale
            once = here * radius
            d_xr = rise(once * at(1, r)) * back
            d_rr = rise(once * at(3, r)) * back
            d_rt = rise(here * radius2 * at(5, r)) * back2
            out = (
                axial(0) + d_xr + around_of(2),
                axial(1) + d_rr + around_of(5) - here * at(4, r) * inv_r,
                axial(2) + d_rt + around_of(4),
            )
            for a in range(3):
                for h in range(2):
                    flux_ref[a, i, pl.ds(c - EDGE, n), pl.ds(h * LANES, LANES)] = out[a][h]

    rows_of(1, nx - 2, flux_pass)

    @pl.when(has_near)
    def _():
        arrive(end_sums)

    swap_stress.wait_recv()
    flux_pass(swap_row)

    @pl.when(has_near)
    def _():
        for h in range(2):
            keep(pick(0, nx + 1), h, ratio(total(rec_out, h, None)))
        edge_stress.wait_recv()

    flux_pass(edge_row)

    leave([seam_swap, swap_vel, swap_stress] + swap_ends + own_around + seam_own + seam_partner_around)
    leave(partner_around + swap_vel_around + across + over)
    for q in range(nx):
        leave(swap_rows[q])

    @pl.when(has_near)
    def _():
        leave([seam_near, edge_vel, edge_stress] + near_ends + near_rows)
        leave(seam_ahead_around + ahead_around + edge_vel_around)

    @pl.when(has_far)
    def _():
        leave([seam_pass] + pass_ends + pass_rows + seam_beyond_around + beyond_around)

    @pl.when(pair_lo)
    def _():
        leave(down)

    @pl.when(pair_hi)
    def _():
        leave(up)


def hand_over(flux_in, coef_in, flux_out, coef_out, flux_buf, coef_buf, sems):
    count = flux_in.shape[0]
    pieces = [(flux_in.at[a], flux_buf.at[a], flux_out.at[a]) for a in range(count)]
    pieces.append((coef_in, coef_buf, coef_out))
    give = [pltpu.make_async_copy(a, c, sems.at[1, at]) for at, (a, b, c) in enumerate(pieces)]
    for c in give:
        c.start()
    for c in give:
        c.wait()


def shards(n_ax, n_az, density, velocity):
    nx, nt, radial = density.shape
    assert radial == 2 * LANES and 2 * 4 * nx * SEAM == LANES and n_ax % 2 == 0
    pr, seam_rows = 2 * nx, nt // 2 + 2 * SUB
    halves, seam = geometry(radial, nt * n_az)

    def field(*lead):
        return pltpu.VMEM(lead + (nt + 2 * EDGE, LANES), jnp.float32)

    def vmem(*shape):
        return pltpu.VMEM(shape, jnp.float32)

    dma = pltpu.SemaphoreType.DMA
    flux, coef = pl.pallas_call(
        functools.partial(kernel, n_ax, n_az, nx, nt),
        out_shape=(
            jax.ShapeDtypeStruct(velocity.shape, jnp.float32),
            jax.ShapeDtypeStruct((nx, radial), jnp.float32),
        ),
        in_specs=[
            pl.BlockSpec(memory_space=pltpu.HBM),
            pl.BlockSpec(memory_space=pltpu.HBM),
            pl.BlockSpec(memory_space=pltpu.HBM),
            pl.BlockSpec(memory_space=pltpu.HBM),
        ],
        out_specs=(
            pl.BlockSpec(memory_space=pltpu.VMEM),
            pl.BlockSpec(memory_space=pltpu.VMEM),
        ),
        scratch_shapes=[
            field(4, pr + 4),
            field(4, nx + 2),
            field(2, 6, pr + 2),
            field(4, pr + 2),
            field(3, pr + 2),
            field(4, pr + 2),
            field(6, pr),
            field(6, pr),
            vmem(4, seam_rows, LANES),
            field(4),
            field(6),
            field(4),
            field(6),
            field(16),
            field(3),
            vmem(pr, 2, LANES),
            vmem(2, n_az, pr, 2, LANES),
            vmem(2, n_az, 2, LANES),
            vmem(nx + 2, 2, SUB, LANES),
            vmem(*halves.shape),
            vmem(*seam.shape),
            dma((6,)),
            dma((COPIES,)),
            dma((COPIES,)),
            dma((6 * n_az,)),
            dma((6 * n_az,)),
        ],
        compiler_params=pltpu.CompilerParams(collective_id=0, has_side_effects=True, vmem_limit_bytes=40 << 20),
        name="closure",
    )(pltpu.with_memory_space_constraint(density, pltpu.HBM), pltpu.with_memory_space_constraint(velocity, pltpu.HBM), pltpu.with_memory_space_constraint(jnp.asarray(halves), pltpu.HBM), pltpu.with_memory_space_constraint(jnp.asarray(seam), pltpu.HBM))
    flux, coef = (pltpu.with_memory_space_constraint(x, pltpu.VMEM) for x in (flux, coef))
    anywhere = pl.BlockSpec(memory_space=pl.ANY)
    return pl.pallas_call(
        hand_over,
        out_shape=(
            jax.ShapeDtypeStruct(flux.shape, jnp.float32),
            jax.ShapeDtypeStruct(coef.shape, jnp.float32),
        ),
        in_specs=[pl.BlockSpec(memory_space=pltpu.VMEM)] * 2,
        out_specs=(pl.BlockSpec(memory_space=pltpu.HBM),) * 2,
        scratch_shapes=[
            pltpu.VMEM(flux.shape, jnp.float32),
            pltpu.VMEM(coef.shape, jnp.float32),
            dma((2, flux.shape[0] + 1)),
        ],
        name="hand_over",
    )(flux, coef)


def solution(mesh):
    in_specs = (P("ax", "az", None), P(None, "ax", "az", None))
    out_specs = (P(None, "ax", "az", None), P("ax", None))
    body = functools.partial(shards, mesh.shape["ax"], mesh.shape["az"])
    return jax.shard_map(body, mesh=mesh, in_specs=in_specs, out_specs=out_specs, check_vma=False)
```

```python
import functools
import itertools
import math

import jax
import jax.numpy as jnp
import numpy as np
from jax import lax
from jax.experimental import pallas as pl
from jax.experimental.pallas import tpu as pltpu
from jax.sharding import PartitionSpec as P

STEP_AXIAL = 0.5
STEP_RADIAL = 0.25
INNER_RADIUS = 10.0
FILTER_RATIO = 2.0
TINY = 1e-06
KEPT = (0, 3, 1, 2, 5)
CROSS = ((0, 1), (0, 2), (1, 2))
LANES = 128
SUB = 8
EDGE = 16
SEAM = 8
COPIES = 64
BLOCKS = {'first': 16, 'hat': 16, 'model': 16, 'closure': 16, 'other': 16, 'flux': 16, 'seam': 16}
MESH_ID = pl.DeviceIdType.MESH


def geometry(radial, azimuth_cells):
    radius = INNER_RADIUS + (np.arange(radial, dtype=np.float64) + 0.5) * STEP_RADIAL
    angle = 2.0 * math.pi / azimuth_cells
    width = (STEP_AXIAL * STEP_RADIAL * angle * radius) ** (2.0 / 3.0)
    rows = np.stack(
        [
            1.0 / radius,
            0.5 / (radius * angle),
            width,
            FILTER_RATIO**2 * width,
            radius,
            0.5 / STEP_RADIAL / radius,
            radius * radius,
            0.5 / STEP_RADIAL / (radius * radius),
        ]
    ).astype(np.float32)
    halves = rows.reshape(rows.shape[0], radial // LANES, 1, LANES)
    at_seam = radial // 2 - SEAM // 2 + np.arange(LANES) % SEAM
    seam = rows[:4, None, at_seam]
    return (
        np.ascontiguousarray(np.broadcast_to(halves, halves.shape[:2] + (SUB, LANES))),
        np.ascontiguousarray(np.broadcast_to(seam, (4, SUB, LANES))),
    )


def lane_of(x):
    return lax.broadcasted_iota(jnp.int32, x.shape, x.ndim - 1)


def before(x):
    y = pltpu.roll(x, 1, x.ndim - 1)
    fill = jnp.concatenate([x[:1], y[:-1]], axis=0)
    return jnp.where(lane_of(x) == 0, fill, y)


def after(x):
    y = pltpu.roll(x, LANES - 1, x.ndim - 1)
    fill = jnp.concatenate([y[1:], x[-1:]], axis=0)
    return jnp.where(lane_of(x) == LANES - 1, fill, y)


def rise(x):
    return after(x) - before(x)


def sides(x):
    lane = lane_of(x)
    return (
        jnp.where(lane == 0, x, pltpu.roll(x, 1, 1)),
        jnp.where(lane == LANES - 1, x, pltpu.roll(x, LANES - 1, 1)),
    )


def radial(s):
    lo, hi = sides(s)
    return ((lo + hi) + (s + s)) * (1.0 / 64.0)


def slope(x):
    lo, hi = sides(x)
    return (hi - lo) * (0.5 / STEP_RADIAL)


def pairs(mom, vel):
    azimuthal = mom[2] * vel[2]
    return [mom[a] * vel[a] - azimuthal for a in (0, 1)] + [mom[a] * vel[b] for a, b in CROSS]


def contractions(dev, scale, hat_pairs, hat_model, hat_mom, hat_vel):
    mixed = [scale * dev[a] - m for a, m in zip(KEPT, hat_model)]
    leonard = [p - q for p, q in zip(hat_pairs, pairs(hat_mom, hat_vel))]

    def cross(left, right):
        return 2.0 * (left[2] * right[2] + left[3] * right[3] + left[4] * right[4])

    azimuthal = mixed[0] + mixed[1]
    lm = leonard[0] * mixed[0] + leonard[1] * mixed[1] + cross(leonard, mixed)
    mm = mixed[0] * mixed[0] + mixed[1] * mixed[1] + azimuthal * azimuthal + cross(mixed, mixed)
    return lm, mm


def fold_rows(cells):
    return sum(cells[at:at + SUB] for at in range(0, cells.shape[0], SUB))


def strain(dx, dr, dt, ur, ut, inv_r):
    s_xx, s_rr = dx[0], dr[1]
    s_tt = dt[2] + ur * inv_r
    s_xr = 0.5 * (dr[0] + dx[1])
    s_xt = 0.5 * (dt[0] + dx[2])
    s_rt = 0.5 * (dt[1] + dr[2] - ut * inv_r)
    size = jnp.sqrt(
        2.0
        * (
            s_xx * s_xx
            + s_rr * s_rr
            + s_tt * s_tt
            + 2.0 * (s_xr * s_xr + s_xt * s_xt + s_rt * s_rt)
        )
    )
    third = (s_xx + s_rr + s_tt) * (1.0 / 3.0)
    return (s_xx - third, s_xr, s_xt, s_rr - third, s_tt - third, s_rt), size


def kernel(
    n_ax, n_az, nx, nt,
    rho_ref, vel_ref, geo_in, seam_in, flux_ref, coef_ref,
    S, T, M, H, V, HM, PX, MX, E, G, GM, GH, GP, GHM, GV, SP,
    part, rec, rec_out, CS, geo_ref, seam_ref, own_sem, send_sem, recv_sem, sum_send, sum_recv,
):
    pr = 2 * nx
    me_ax, me_az = lax.axis_index("ax"), lax.axis_index("az")
    left, right = lax.rem(me_az + n_az - 1, n_az), lax.rem(me_az + 1, n_az)
    odd = lax.rem(me_ax, 2)
    even = 1 - odd
    mine, other = odd, even
    azimuth_cells = nt * n_az

    def pick(at_even, at_odd):
        return jnp.where(odd == 0, at_even, at_odd)

    has_lo, has_hi = me_ax > 0, me_ax < n_ax - 1
    pair_lo, pair_hi = me_ax >= 2, me_ax < n_ax - 2
    partner = me_ax + 1 - 2 * odd
    near_ax = me_ax - 2 + 4 * odd
    far_ax = me_ax + 2 - 4 * odd
    edge_ax = me_ax - 1 + 2 * odd
    has_near = (near_ax >= 0) & (near_ax < n_ax)
    has_far = (far_ax >= 0) & (far_ax < n_ax)

    lanes_mine = pl.ds(pl.multiple_of(mine * LANES, LANES), LANES)
    lanes_other = pl.ds(pl.multiple_of(other * LANES, LANES), LANES)
    cols = pl.ds(EDGE, nt)
    own_row = nx * odd
    own_at = own_row + 2
    partner_at = nx * even + 2
    near_at = pick(0, nx - 2)
    beyond_at = pick(pr + 2, 0)
    ahead_at = pick(0, pr + 2)
    pass_at = pick(pr, 2)

    own = [
        pltpu.make_async_copy(rho_ref.at[:, :, lanes_mine], S.at[0, pl.ds(own_at, nx), cols, :], own_sem.at[0]),
        pltpu.make_async_copy(
            vel_ref.at[:, :, :, lanes_mine], S.at[pl.ds(1, 3), pl.ds(own_at, nx), cols, :], own_sem.at[1]),
        pltpu.make_async_copy(rho_ref.at[:, :, lanes_other], T.at[0, pl.ds(1, nx), cols, :], own_sem.at[2]),
        pltpu.make_async_copy(
            vel_ref.at[:, :, :, lanes_other], T.at[pl.ds(1, 3), pl.ds(1, nx), cols, :], own_sem.at[3]),
    ]
    tables = [
        pltpu.make_async_copy(geo_in, geo_ref, own_sem.at[4]),
        pltpu.make_async_copy(seam_in, seam_ref, own_sem.at[5]),
    ]
    for c in own + tables:
        c.start()

    barrier = pltpu.get_barrier_semaphore()

    def greet(ax, az):
        pl.semaphore_signal(barrier, inc=1, device_id=(ax, az), device_id_type=MESH_ID)

    short = n_az == 4
    for d in (1, n_az - 1) if short else range(1, n_az):
        greet(me_ax, lax.rem(me_az + d, n_az))
    peers = 2 if short else n_az - 1
    if short:
        greet(partner, me_az)
        peers = peers + 1
    for step in (-2, 2) if short else (-1, 1, -2, 2):
        there = (me_ax + step >= 0) & (me_ax + step < n_ax)
        reach = 1 if short else n_az

        @pl.when(there)
        def _():
            for d in range(reach):
                greet(me_ax + step, lax.rem(me_az + d, n_az))

        peers = peers + jnp.where(there, reach, 0)

    ids = itertools.count()

    def remote(src, dst, ax, az):
        at = next(ids)
        return pltpu.make_async_remote_copy(
            src_ref=src, dst_ref=dst, send_sem=send_sem.at[at], recv_sem=recv_sem.at[at],
            device_id=(ax, az), device_id_type=MESH_ID)

    def block(src_row, count, first, width, lanes, dst, dst_row, dst_first, ax, az):
        rows, at = pl.ds(src_row, count), pl.ds(first, width)
        to_rows, to = pl.ds(dst_row, count), pl.ds(dst_first, width)
        return [
            remote(rho_ref.at[rows, at, lanes], dst.at[0, to_rows, to, :], ax, az),
            remote(vel_ref.at[:, rows, at, lanes], dst.at[pl.ds(1, 3), to_rows, to, :], ax, az),
        ]

    def ends(src_row, count, lanes, dst, dst_row, ax, az):
        out = []
        for first in (0, nt - SUB):
            out += block(src_row, count, first, SUB, lanes, dst, dst_row, EDGE + first, ax, az)
        return out

    def middle(src_row, count, lanes, dst, dst_row, ax, az):
        return block(src_row, count, SUB, nt - 2 * SUB, lanes, dst, dst_row, EDGE + SUB, ax, az)

    def around(ref, lead, rows):
        at = (pl.ds(EDGE + nt - SUB, SUB), pl.ds(EDGE - SUB, SUB), pl.ds(EDGE, SUB), pl.ds(EDGE + nt, SUB))
        return [
            remote(ref.at[lead, rows, at[0], :], ref.at[lead, rows, at[1], :], me_ax, right),
            remote(ref.at[lead, rows, at[2], :], ref.at[lead, rows, at[3], :], me_ax, left),
        ]

    whole = pl.ds(SUB, nt)

    def seam_around(s):
        return [
            remote(E.at[s, pl.ds(nt, SUB), :], E.at[s, pl.ds(0, SUB), :], me_ax, right),
            remote(E.at[s, pl.ds(SUB, SUB), :], E.at[s, pl.ds(SUB + nt, SUB), :], me_ax, left),
        ]

    s_own, s_partner, s_beyond, s_ahead = 1 + odd, 2 - odd, pick(3, 0), pick(0, 3)

    own_around = []
    for lanes, dst, row in ((lanes_mine, S, own_at), (lanes_other, T, 1)):
        own_around += block(0, nx, nt - SUB, SUB, lanes, dst, row, EDGE - SUB, me_ax, right)
        own_around += block(0, nx, 0, SUB, lanes, dst, row, EDGE + nt, me_ax, left)
    seam_own = seam_around(s_own)
    seam_partner_around = seam_around(s_partner)
    seam_beyond_around = seam_around(s_beyond)
    seam_ahead_around = seam_around(s_ahead)

    seam_swap = remote(E.at[s_own, whole, :], E.at[s_own, whole, :], partner, me_az)
    seam_near = remote(E.at[s_own, whole, :], E.at[pick(3, 0), whole, :], near_ax, me_az)
    seam_pass = remote(E.at[s_partner, whole, :], E.at[pick(0, 3), whole, :], far_ax, me_az)

    swap_ends = ends(0, nx, lanes_other, S, own_at, partner, me_az)
    swap_rows = {}
    for q in range(nx):
        row = pick(nx - 1 - q, q)
        swap_rows[q] = middle(row, 1, lanes_other, S, own_at + row, partner, me_az)
    near_ends = ends(near_at, 2, lanes_mine, S, beyond_at, near_ax, me_az)
    near_rows = middle(near_at, 2, lanes_mine, S, beyond_at, near_ax, me_az)

    every = pl.ds(0, 4)

    def forward(row, first, width, count):
        return remote(
            S.at[:, pl.ds(pass_at + row, count), pl.ds(EDGE + first, width), :],
            S.at[:, pl.ds(ahead_at + row, count), pl.ds(EDGE + first, width), :], far_ax, me_az)

    pass_ends = [forward(0, first, SUB, 2) for first in (0, nt - SUB)]
    last_row = pick(1, 0)
    pass_rows = [forward(last_row, SUB, nt - 2 * SUB, 1), forward(1 - last_row, SUB, nt - 2 * SUB, 1)]
    partner_around = around(S, every, pl.ds(partner_at, nx))
    beyond_around = around(S, every, pl.ds(beyond_at, 2))
    ahead_around = around(S, every, pl.ds(ahead_at, 2))

    swap_row, edge_row = pick(nx - 1, 0), pick(0, nx - 1)
    three = pl.ds(1, 3)

    def flux_rows(row, dst_row, ax):
        return remote(
            vel_ref.at[:, pl.ds(row, 1), :, lanes_mine], T.at[three, pl.ds(dst_row, 1), cols, :], ax, me_az)

    def flux_stress(row, dst_row, ax):
        return remote(
            M.at[mine, pl.ds(0, 3), own_row + row + 1, cols, :], M.at[mine, pl.ds(0, 3), dst_row, cols, :],
            ax, me_az)

    swap_vel = flux_rows(swap_row, pick(0, nx + 1), partner)
    edge_vel = flux_rows(edge_row, pick(nx + 1, 0), edge_ax)
    swap_vel_around = around(T, three, pl.ds(pick(nx + 1, 0), 1))
    edge_vel_around = around(T, three, pl.ds(pick(0, nx + 1), 1))
    swap_stress = flux_stress(swap_row, pick(nx, nx + 1), partner)
    edge_stress = flux_stress(edge_row, pick(pr + 1, 0), edge_ax)

    def start(copies):
        for c in copies:
            c.start()

    def arrive(copies):
        for c in copies:
            c.wait_recv()

    def leave(copies):
        for c in copies:
            c.wait_send()

    wide = nt + 2 * SUB
    outer_cols = EDGE - SUB

    def lanes_at(n):
        return lax.broadcasted_iota(jnp.int32, (n, LANES), 1)

    def spread(values, rows):
        return jnp.concatenate([values] * (rows // SUB), axis=values.ndim - 2)

    def pack_seam():
        lane = lanes_at(nt)
        from_mine = jnp.where(lane >= LANES - SEAM // 2, 1, 0) == even
        packed = jnp.zeros((nt, LANES), jnp.float32)
        for a in range(4):
            for i in range(nx):
                first = (a * nx + i) * SEAM
                x = jnp.where(from_mine, S[a, own_at + i, pl.ds(EDGE, nt), :], T[a, 1 + i, pl.ds(EDGE, nt), :])
                x = pltpu.roll(x, (first + SEAM // 2) % LANES, 1)
                packed = jnp.where((lane >= first) & (lane < first + SEAM), x, packed)
        E[s_own, whole, :] = packed

    n_seam = math.gcd(BLOCKS["seam"], wide)
    seam_lane = lanes_at(n_seam)
    seam_row = seam_lane // SEAM
    at_bottom = seam_row == jnp.where(pair_lo, -1, nx)
    at_top = seam_row == jnp.where(pair_hi, -1, nx + pr - 1)

    def seam_below(x):
        return jnp.where(at_bottom, x, pltpu.roll(x, SEAM, 1))

    def seam_above(x):
        return jnp.where(at_top, x, pltpu.roll(x, LANES - SEAM, 1))

    def seam_axial(x):
        return (seam_below(x) + x) + (x + seam_above(x))

    def seam_slope(x):
        return (pltpu.roll(x, LANES - 1, 1) - pltpu.roll(x, 1, 1)) * (0.5 / STEP_RADIAL)

    def seam_radial(s):
        return ((pltpu.roll(s, 1, 1) + pltpu.roll(s, LANES - 1, 1)) + (s + s)) * (1.0 / 64.0)

    def seam_turn(ref, a, c, n):
        x = ref[a, pl.ds(c, n), :]
        return (ref[a, pl.ds(c - 1, n), :] + ref[a, pl.ds(c + 1, n), :]) + (x + x)

    def seam_pass_all():
        tiles = [(c, n_seam) for c in range(outer_cols, outer_cols + wide, n_seam)]
        inner = [(c, n_seam) for c in range(EDGE, EDGE + nt, n_seam)]
        lane = lanes_at(wide)
        per = nx * SEAM
        for a in range(4):
            packed = jnp.zeros((wide, LANES), jnp.float32)
            for s in range(4):
                x = E[s, :, :]
                if s != a:
                    x = pltpu.roll(x, (s - a) * per % LANES, 1)
                packed = jnp.where((lane >= s * per) & (lane < (s + 1) * per), x, packed)
            G[a, pl.ds(outer_cols, wide), :] = packed
        for c, n in tiles:
            at, at_before, at_after = pl.ds(c, n), pl.ds(c - 1, n), pl.ds(c + 1, n)
            rho = G[0, at, :]
            vel = [G[1 + a, at, :] for a in range(3)]
            inv_r, az_scale, width = (spread(seam_ref[g], n) for g in (0, 1, 2))
            dx = [seam_above(v) - seam_below(v) for v in vel]
            dr = [seam_slope(v) for v in vel]
            dt = [(G[1 + a, at_after, :] - G[1 + a, at_before, :]) * az_scale for a in range(3)]
            dev, size = strain(dx, dr, dt, vel[1], vel[2], inv_r)
            scale = rho * width * size
            for q, a in enumerate(KEPT):
                GM[q, at, :] = seam_axial(scale * dev[a])
            mom = [rho * v for v in vel]
            GH[0, at, :] = seam_axial(rho)
            for a in range(3):
                GH[1 + a, at, :] = seam_axial(mom[a])
            for q, p in enumerate(pairs(mom, vel)):
                GP[q, at, :] = seam_axial(p)
        for c, n in tiles:
            at = pl.ds(c, n)
            hat = [seam_radial(seam_turn(GH, a, c, n)) for a in range(4)]
            inv = 1.0 / hat[0]
            for a in range(4):
                GHM[a, at, :] = hat[a]
            for a in range(3):
                GV[a, at, :] = hat[1 + a] * inv
        sums = [0.0, 0.0]
        for c, n in inner:
            at, at_before, at_after = pl.ds(c, n), pl.ds(c - 1, n), pl.ds(c + 1, n)
            inv_r, az_scale, width4 = (spread(seam_ref[g], n) for g in (0, 1, 3))
            hv = [GV[a, at, :] for a in range(3)]
            dx = [seam_above(v) - seam_below(v) for v in hv]
            dr = [seam_slope(v) for v in hv]
            dt = [(GV[a, at_after, :] - GV[a, at_before, :]) * az_scale for a in range(3)]
            dev, size = strain(dx, dr, dt, hv[1], hv[2], inv_r)
            terms = contractions(
                dev, width4 * GHM[0, at, :] * size,
                [seam_radial(seam_turn(GP, q, c, n)) for q in range(5)],
                [seam_radial(seam_turn(GM, q, c, n)) for q in range(5)],
                [GHM[1 + a, at, :] for a in range(3)], hv)
            sums = [x + fold_rows(y) for x, y in zip(sums, terms)]
        for q in range(2):
            row = jnp.sum(sums[q], axis=0, keepdims=True)
            for r in range(pr):
                shift = LANES - SEAM // 2 - SEAM * (nx + r)
                SP[r, pl.ds(q, 1), :] = pltpu.roll(row, shift % LANES, 1)

    def smooth(ref, a, row, first, n):
        x = ref[a, row, pl.ds(first, n), :]
        s = (ref[a, row, pl.ds(first - 1, n), :] + ref[a, row, pl.ds(first + 1, n), :]) + (x + x)
        return radial(s)

    def whole_slope(a, x, first, r):
        shift = pick(LANES - 1, LANES + 1) - SEAM // 2 - SEAM * (r + nx)
        end = pick(LANES - 1, 0)
        far = pltpu.roll(G[1 + a, pl.ds(first, x.shape[0]), :], shift, 1)
        lane = lane_of(x)
        far = jnp.where(lane == end, far, x)
        lo = jnp.where(lane == 0, far, pltpu.roll(x, 1, 1))
        hi = jnp.where(lane == LANES - 1, far, pltpu.roll(x, LANES - 1, 1))
        return (hi - lo) * (0.5 / STEP_RADIAL)

    def low(r):
        return jnp.maximum(r - 1, jnp.where(pair_lo, -2, 0))

    def high(r):
        return jnp.minimum(r + 1, jnp.where(pair_hi, pr + 1, pr - 1))

    def sweep(first, count, body):
        def step(at, carry):
            t = first + at
            body(pick(t, pr - 1 - t))
            return carry

        lax.fori_loop(0, count, step, 0)

    def turn_slope(ref, a, row, first, n):
        return ref[a, row, pl.ds(first + 1, n), :] - ref[a, row, pl.ds(first - 1, n), :]

    def first_pass(r, with_pairs, exact):
        n = math.gcd(BLOCKS["first"], wide)
        for c in range(outer_cols, outer_cols + wide, n):
            rows = (low(r) + 2, r + 2, high(r) + 2)
            rho = [S[0, q, pl.ds(c, n), :] for q in rows]
            vel = [[S[1 + a, q, pl.ds(c, n), :] for a in range(3)] for q in rows]
            inv_r, az_scale, width = (spread(geo_ref[g, mine], n) for g in (0, 1, 2))
            dx = [vel[2][a] - vel[0][a] for a in range(3)]
            dr = [whole_slope(a, vel[1][a], c, r) if exact else slope(vel[1][a]) for a in range(3)]
            dt = [turn_slope(S, 1 + a, r + 2, c, n) * az_scale for a in range(3)]
            dev, size = strain(dx, dr, dt, vel[1][1], vel[1][2], inv_r)
            scale = rho[1] * width * size
            for a in range(6):
                M[mine, a, r + 1, pl.ds(c, n), :] = scale * dev[a]
            mom = [[rho[q] * vel[q][a] for a in range(3)] for q in range(3)]
            H[0, r + 1, pl.ds(c, n), :] = (rho[0] + rho[1]) + (rho[1] + rho[2])
            for a in range(3):
                H[1 + a, r + 1, pl.ds(c, n), :] = (mom[0][a] + mom[1][a]) + (mom[1][a] + mom[2][a])
            if with_pairs:
                for at, p in enumerate(zip(*(pairs(mom[q], vel[q]) for q in range(3)))):
                    PX[at, r, pl.ds(c, n), :] = (p[0] + p[1]) + (p[1] + p[2])

    def hat_pass(r):
        n = math.gcd(BLOCKS["hat"], wide)
        for c in range(outer_cols, outer_cols + wide, n):
            hat = [smooth(H, a, r + 1, c, n) for a in range(4)]
            inv = 1.0 / hat[0]
            for a in range(4):
                HM[a, r + 1, pl.ds(c, n), :] = hat[a]
            for a in range(3):
                V[a, r + 1, pl.ds(c, n), :] = hat[1 + a] * inv

    def model_pass(r):
        n = math.gcd(BLOCKS["model"], wide)
        for c in range(outer_cols, outer_cols + wide, n):
            for q, a in enumerate(KEPT):
                x = M[mine, a, r + 1, pl.ds(c, n), :]
                lo = M[mine, a, low(r) + 1, pl.ds(c, n), :]
                MX[q, r, pl.ds(c, n), :] = (lo + x) + (x + M[mine, a, high(r) + 1, pl.ds(c, n), :])

    def closure_pass(r):
        sums = [0.0, 0.0]
        n = math.gcd(BLOCKS["closure"], nt)
        for c in range(EDGE, EDGE + nt, n):
            inv_r, az_scale, width4 = (spread(geo_ref[g, mine], n) for g in (0, 1, 3))
            hv = [V[a, r + 1, pl.ds(c, n), :] for a in range(3)]
            hm = [HM[1 + a, r + 1, pl.ds(c, n), :] for a in range(3)]
            dx = [V[a, high(r) + 1, pl.ds(c, n), :] - V[a, low(r) + 1, pl.ds(c, n), :] for a in range(3)]
            dr = [slope(hv[a]) for a in range(3)]
            dt = [turn_slope(V, a, r + 1, c, n) * az_scale for a in range(3)]
            dev, size = strain(dx, dr, dt, hv[1], hv[2], inv_r)
            terms = contractions(
                dev, width4 * HM[0, r + 1, pl.ds(c, n), :] * size,
                [smooth(PX, q, r, c, n) for q in range(5)], [smooth(MX, q, r, c, n) for q in range(5)], hm, hv)
            sums = [x + fold_rows(y) for x, y in zip(sums, terms)]
        lane = lanes_at(1)
        at_seam = jnp.where(odd == 0, LANES - 1 - lane, lane) < 2
        for q in range(2):
            row = jnp.sum(sums[q], axis=0, keepdims=True)
            part[r, pl.ds(q, 1), :] = jnp.where(at_seam, SP[r, pl.ds(q, 1), :], row)

    def first_two(first, count, with_pairs=True):
        exact = min(max(nx + 1 - first, 0), count)
        if exact:
            sweep(first, exact, lambda r: first_pass(r, with_pairs, True))
        if exact < count:
            sweep(first + exact, count - exact, lambda r: first_pass(r, with_pairs, False))
        sweep(first, count, hat_pass)

    def close(first, count):
        sweep(first, count, model_pass)
        sweep(first, count, closure_pass)

    def other_half(i):
        n = math.gcd(BLOCKS["other"], wide)
        for c in range(outer_cols, outer_cols + wide, n):
            inv_r, az_scale, width = (spread(geo_ref[g, other], n) for g in (0, 1, 2))
            lo = jnp.maximum(i - 1, jnp.where(has_lo, -1, 0)) + 1
            hi = jnp.minimum(i + 1, jnp.where(has_hi, nx, nx - 1)) + 1
            vel = [T[1 + a, i + 1, pl.ds(c, n), :] for a in range(3)]
            dx = [T[1 + a, hi, pl.ds(c, n), :] - T[1 + a, lo, pl.ds(c, n), :] for a in range(3)]
            dr = []
            for a in range(3):
                far = pltpu.roll(S[1 + a, own_at + i, pl.ds(c, n), :], pick(1, LANES - 1), 1)
                lane = lane_of(far)
                end = jnp.where(lane == pick(0, LANES - 1), far, vel[a])
                lo_side = jnp.where(lane == 0, end, pltpu.roll(vel[a], 1, 1))
                hi_side = jnp.where(lane == LANES - 1, end, pltpu.roll(vel[a], LANES - 1, 1))
                dr.append((hi_side - lo_side) * (0.5 / STEP_RADIAL))
            dt = [turn_slope(T, 1 + a, i + 1, c, n) * az_scale for a in range(3)]
            dev, size = strain(dx, dr, dt, vel[1], vel[2], inv_r)
            scale = T[0, i + 1, pl.ds(c, n), :] * width * size
            for a in range(6):
                M[other, a, own_row + i + 1, pl.ds(c, n), :] = scale * dev[a]

    def rows_of(first, count, body):
        def step(at, carry):
            body(first + at)
            return carry

        lax.fori_loop(0, count, step, 0)

    for c in own:
        c.wait()
    pack_seam()
    pl.semaphore_wait(barrier, peers)
    start([seam_swap] + swap_ends)
    start(seam_own + own_around)

    @pl.when(has_near)
    def _():
        start([seam_near] + near_ends + near_rows)

    for q in [nx - 1, nx - 2] + list(range(nx - 2)):
        start(swap_rows[q])
    swap_vel.start()

    seam_swap.wait_recv()
    start(seam_partner_around)

    @pl.when(has_far)
    def _():
        seam_pass.start()
        seam_near.wait_recv()
        start(seam_beyond_around)

    arrive(own_around)
    for c in tables:
        c.wait()
    rows_of(1, nx - 2, other_half)

    @pl.when(has_near)
    def _():
        seam_pass.wait_recv()
        start(seam_ahead_around)

    arrive(swap_ends)
    start(partner_around)

    @pl.when(has_far)
    def _():
        start(pass_ends)
        arrive(near_ends)
        start(beyond_around)

    arrive(seam_own + seam_partner_around)

    @pl.when(has_far)
    def _():
        arrive(seam_beyond_around)

    @pl.when(has_near)
    def _():
        arrive(seam_ahead_around)

    seam_pass_all()
    first_two(1, nx - 2)

    @pl.when(has_near)
    def _():
        arrive(pass_ends)
        start(ahead_around)

    for at in range(2):
        arrive(swap_rows[nx - 1 - at])

        @pl.when(has_far)
        def _():
            pass_rows[at].start()

    @pl.when(has_far)
    def _():
        arrive(near_rows)
        arrive(beyond_around)

    arrive(partner_around)
    first_two(pr - 1, 1)
    first_two(pr, 1, False)
    for q in range(nx - 3):
        arrive(swap_rows[q])
        first_two(nx - 1 + q, 1)
        close(nx - 2 + q, 1)

    @pl.when(has_near)
    def _():
        edge_vel.start()
        arrive(pass_rows)
        arrive(ahead_around)

    first_two(-1, 1, False)
    first_two(0, 1)
    close(0, 2)
    arrive(swap_rows[nx - 3])
    swap_stress.start()

    @pl.when(has_near)
    def _():
        edge_stress.start()

    first_two(pr - 4, 3)
    close(pr - 5, 5)

    def share(at, src, dst, ax, d):
        return pltpu.make_async_remote_copy(
            src_ref=src, dst_ref=dst, send_sem=sum_send.at[at], recv_sem=sum_recv.at[at],
            device_id=(ax, lax.rem(me_az + d, n_az)), device_id_type=MESH_ID)

    def end_row(kind, half, row, ax):
        return [
            share((2 + 2 * kind + half) * n_az + d, part.at[row], rec_out.at[half, me_az], ax, d)
            for d in range(n_az)
        ]

    across = [share(d, part, rec.at[mine, me_az], me_ax, d) for d in range(1, n_az)]
    over = [share(n_az + d, part, rec.at[mine, me_az], partner, d) for d in range(n_az)]
    lower_ax, upper_ax = me_ax - odd - 1, me_ax - odd + 2
    down, up = end_row(0, mine, 0, lower_ax), end_row(1, mine, pr - 1, upper_ax)
    end_sums = end_row(even, 0, 0, me_ax) + end_row(even, 1, 0, me_ax)

    @pl.when(pair_lo)
    def _():
        start(down)

    @pl.when(pair_hi)
    def _():
        start(up)

    start(over)
    start(across)
    rec[mine, me_az] = part[...]
    swap_vel.wait_recv()
    start(swap_vel_around)

    @pl.when(has_near)
    def _():
        edge_vel.wait_recv()
        start(edge_vel_around)

    arrive(swap_vel_around)
    other_half(swap_row)

    @pl.when(has_near)
    def _():
        arrive(edge_vel_around)

    other_half(edge_row)

    def ratio(sums):
        lm, mm = sums[0:1], sums[1:2]
        return -0.5 * (lm * (1.0 / azimuth_cells)) / (mm * (1.0 / azimuth_cells) + TINY)

    def total(ref, h, row):
        terms = [ref[h, d] if row is None else ref[h, d, row] for d in range(n_az)]
        sums = terms[0]
        for x in terms[1:]:
            sums = sums + x
        return sums

    def keep(row, h, value):
        CS[row, h] = jnp.broadcast_to(-2.0 * value, (SUB, LANES))

    arrive(across)
    arrive(over)
    for i in range(nx + 1):
        row = i + even
        for h in range(2):
            keep(row, h, ratio(total(rec, h, own_row + row - 1)))
    for i in range(nx):
        for h in range(2):
            coef_ref[pl.ds(i, 1), pl.ds(h * LANES, LANES)] = -0.5 * CS[i + 1, h, pl.ds(0, 1), :]

    def flux_pass(i):
        n = math.gcd(BLOCKS["flux"], nt)
        for c in range(EDGE, EDGE + nt, n):
            r = own_row + i + 1
            inv_r, az_scale, radius, back, radius2, back2 = (spread(geo_ref[g], n) for g in (0, 1, 4, 5, 6, 7))
            lo = jnp.maximum(i - 1, jnp.where(has_lo, -1, 0)) + 1
            hi = jnp.minimum(i + 1, jnp.where(has_hi, nx, nx - 1)) + 1
            here, below, above = (spread(CS[q], n) for q in (i + 1, lo, hi))

            def at(a, row, shift=0):
                return M[:, a, row, pl.ds(c + shift, n), :]

            def axial(a):
                return above * at(a, own_row + hi) - below * at(a, own_row + lo)

            def around_of(a):
                return (at(a, r, 1) - at(a, r, -1)) * turn

            turn = here * az_scale
            once = here * radius
            d_xr = rise(once * at(1, r)) * back
            d_rr = rise(once * at(3, r)) * back
            d_rt = rise(here * radius2 * at(5, r)) * back2
            out = (
                axial(0) + d_xr + around_of(2),
                axial(1) + d_rr + around_of(5) - here * at(4, r) * inv_r,
                axial(2) + d_rt + around_of(4),
            )
            for a in range(3):
                for h in range(2):
                    flux_ref[a, i, pl.ds(c - EDGE, n), pl.ds(h * LANES, LANES)] = out[a][h]

    rows_of(1, nx - 2, flux_pass)

    @pl.when(has_near)
    def _():
        arrive(end_sums)

    swap_stress.wait_recv()
    flux_pass(swap_row)

    @pl.when(has_near)
    def _():
        for h in range(2):
            keep(pick(0, nx + 1), h, ratio(total(rec_out, h, None)))
        edge_stress.wait_recv()

    flux_pass(edge_row)

    leave([seam_swap, swap_vel, swap_stress] + swap_ends + own_around + seam_own + seam_partner_around)
    leave(partner_around + swap_vel_around + across + over)
    for q in range(nx):
        leave(swap_rows[q])

    @pl.when(has_near)
    def _():
        leave([seam_near, edge_vel, edge_stress] + near_ends + near_rows)
        leave(seam_ahead_around + ahead_around + edge_vel_around)

    @pl.when(has_far)
    def _():
        leave([seam_pass] + pass_ends + pass_rows + seam_beyond_around + beyond_around)

    @pl.when(pair_lo)
    def _():
        leave(down)

    @pl.when(pair_hi)
    def _():
        leave(up)


def hand_over(flux_in, coef_in, flux_out, coef_out, flux_buf, coef_buf, sems):
    count = flux_in.shape[0]
    pieces = [(flux_in.at[a], flux_buf.at[a], flux_out.at[a]) for a in range(count)]
    pieces.append((coef_in, coef_buf, coef_out))
    give = [pltpu.make_async_copy(a, c, sems.at[1, at]) for at, (a, b, c) in enumerate(pieces)]
    for c in give:
        c.start()
    for c in give:
        c.wait()


def shards(n_ax, n_az, density, velocity):
    nx, nt, radial = density.shape
    assert radial == 2 * LANES and 4 * nx * SEAM == LANES and n_ax % 2 == 0
    pr, seam_rows = 2 * nx, nt + 2 * SUB
    halves, seam = geometry(radial, nt * n_az)

    def field(*lead):
        return pltpu.VMEM(lead + (nt + 2 * EDGE, LANES), jnp.float32)

    def vmem(*shape):
        return pltpu.VMEM(shape, jnp.float32)

    dma = pltpu.SemaphoreType.DMA
    flux, coef = pl.pallas_call(
        functools.partial(kernel, n_ax, n_az, nx, nt),
        out_shape=(
            jax.ShapeDtypeStruct(velocity.shape, jnp.float32),
            jax.ShapeDtypeStruct((nx, radial), jnp.float32),
        ),
        in_specs=[
            pl.BlockSpec(memory_space=pltpu.HBM),
            pl.BlockSpec(memory_space=pltpu.HBM),
            pl.BlockSpec(memory_space=pltpu.HBM),
            pl.BlockSpec(memory_space=pltpu.HBM),
        ],
        out_specs=(
            pl.BlockSpec(memory_space=pltpu.VMEM),
            pl.BlockSpec(memory_space=pltpu.VMEM),
        ),
        scratch_shapes=[
            field(4, pr + 4),
            field(4, nx + 2),
            field(2, 6, pr + 2),
            field(4, pr + 2),
            field(3, pr + 2),
            field(4, pr + 2),
            field(5, pr),
            field(5, pr),
            vmem(4, seam_rows, LANES),
            field(4),
            field(5),
            field(4),
            field(5),
            field(4),
            field(3),
            vmem(pr, 2, LANES),
            vmem(pr, 2, LANES),
            vmem(2, n_az, pr, 2, LANES),
            vmem(2, n_az, 2, LANES),
            vmem(nx + 2, 2, SUB, LANES),
            vmem(*halves.shape),
            vmem(*seam.shape),
            dma((6,)),
            dma((COPIES,)),
            dma((COPIES,)),
            dma((6 * n_az,)),
            dma((6 * n_az,)),
        ],
        compiler_params=pltpu.CompilerParams(collective_id=0, has_side_effects=True, vmem_limit_bytes=40 << 20),
        name="closure",
    )(pltpu.with_memory_space_constraint(density, pltpu.HBM), pltpu.with_memory_space_constraint(velocity, pltpu.HBM), pltpu.with_memory_space_constraint(jnp.asarray(halves), pltpu.HBM), pltpu.with_memory_space_constraint(jnp.asarray(seam), pltpu.HBM))
    flux, coef = (pltpu.with_memory_space_constraint(x, pltpu.VMEM) for x in (flux, coef))
    anywhere = pl.BlockSpec(memory_space=pl.ANY)
    return pl.pallas_call(
        hand_over,
        out_shape=(
            jax.ShapeDtypeStruct(flux.shape, jnp.float32),
            jax.ShapeDtypeStruct(coef.shape, jnp.float32),
        ),
        in_specs=[pl.BlockSpec(memory_space=pltpu.VMEM)] * 2,
        out_specs=(pl.BlockSpec(memory_space=pltpu.HBM),) * 2,
        scratch_shapes=[
            pltpu.VMEM(flux.shape, jnp.float32),
            pltpu.VMEM(coef.shape, jnp.float32),
            dma((2, flux.shape[0] + 1)),
        ],
        name="hand_over",
    )(flux, coef)


def solution(mesh):
    in_specs = (P("ax", "az", None), P(None, "ax", "az", None))
    out_specs = (P(None, "ax", "az", None), P("ax", None))
    body = functools.partial(shards, mesh.shape["ax"], mesh.shape["az"])
    return jax.shard_map(body, mesh=mesh, in_specs=in_specs, out_specs=out_specs, check_vma=False)
```

```python
import functools
import itertools
import math

import jax
import jax.numpy as jnp
import numpy as np
from jax import lax
from jax.experimental import pallas as pl
from jax.experimental.pallas import tpu as pltpu
from jax.sharding import PartitionSpec as P

STEP_AXIAL = 0.5
STEP_RADIAL = 0.25
INNER_RADIUS = 10.0
FILTER_RATIO = 2.0
TINY = 1e-06
KEPT = (0, 3, 1, 2, 5)
CROSS = ((0, 1), (0, 2), (1, 2))
LANES = 128
SUB = 8
EDGE = 16
SEAM = 8
COPIES = 64
BLOCKS = {'first': 16, 'hat': 16, 'model': 16, 'closure': 16, 'other': 16, 'flux': 16, 'seam': 16}
MESH_ID = pl.DeviceIdType.MESH


def geometry(radial, azimuth_cells):
    radius = INNER_RADIUS + (np.arange(radial, dtype=np.float64) + 0.5) * STEP_RADIAL
    angle = 2.0 * math.pi / azimuth_cells
    width = (STEP_AXIAL * STEP_RADIAL * angle * radius) ** (2.0 / 3.0)
    rows = np.stack(
        [
            1.0 / radius,
            0.5 / (radius * angle),
            width,
            FILTER_RATIO**2 * width,
            radius,
            0.5 / STEP_RADIAL / radius,
            radius * radius,
            0.5 / STEP_RADIAL / (radius * radius),
        ]
    ).astype(np.float32)
    halves = rows.reshape(rows.shape[0], radial // LANES, 1, LANES)
    at_seam = radial // 2 - SEAM // 2 + np.arange(LANES) % SEAM
    seam = rows[:4, None, at_seam]
    return (
        np.ascontiguousarray(np.broadcast_to(halves, halves.shape[:2] + (SUB, LANES))),
        np.ascontiguousarray(np.broadcast_to(seam, (4, SUB, LANES))),
    )


def lane_of(x):
    return lax.broadcasted_iota(jnp.int32, x.shape, x.ndim - 1)


def before(x):
    y = pltpu.roll(x, 1, x.ndim - 1)
    fill = jnp.concatenate([x[:1], y[:-1]], axis=0)
    return jnp.where(lane_of(x) == 0, fill, y)


def after(x):
    y = pltpu.roll(x, LANES - 1, x.ndim - 1)
    fill = jnp.concatenate([y[1:], x[-1:]], axis=0)
    return jnp.where(lane_of(x) == LANES - 1, fill, y)


def rise(x):
    return after(x) - before(x)


def sides(x):
    lane = lane_of(x)
    return (
        jnp.where(lane == 0, x, pltpu.roll(x, 1, 1)),
        jnp.where(lane == LANES - 1, x, pltpu.roll(x, LANES - 1, 1)),
    )


def radial(s):
    lo, hi = sides(s)
    return ((lo + hi) + (s + s)) * (1.0 / 64.0)


def slope(x):
    lo, hi = sides(x)
    return (hi - lo) * (0.5 / STEP_RADIAL)


def pairs(mom, vel):
    azimuthal = mom[2] * vel[2]
    return [mom[a] * vel[a] - azimuthal for a in (0, 1)] + [mom[a] * vel[b] for a, b in CROSS]


def contractions(dev, scale, hat_pairs, hat_model, hat_mom, hat_vel):
    mixed = [scale * dev[a] - m for a, m in zip(KEPT, hat_model)]
    leonard = [p - q for p, q in zip(hat_pairs, pairs(hat_mom, hat_vel))]

    def cross(left, right):
        return 2.0 * (left[2] * right[2] + left[3] * right[3] + left[4] * right[4])

    azimuthal = mixed[0] + mixed[1]
    lm = leonard[0] * mixed[0] + leonard[1] * mixed[1] + cross(leonard, mixed)
    mm = mixed[0] * mixed[0] + mixed[1] * mixed[1] + azimuthal * azimuthal + cross(mixed, mixed)
    return lm, mm


def fold_rows(cells):
    return sum(cells[at:at + SUB] for at in range(0, cells.shape[0], SUB))


def strain(dx, dr, dt, ur, ut, inv_r):
    s_xx, s_rr = dx[0], dr[1]
    s_tt = dt[2] + ur * inv_r
    s_xr = 0.5 * (dr[0] + dx[1])
    s_xt = 0.5 * (dt[0] + dx[2])
    s_rt = 0.5 * (dt[1] + dr[2] - ut * inv_r)
    size = jnp.sqrt(
        2.0
        * (
            s_xx * s_xx
            + s_rr * s_rr
            + s_tt * s_tt
            + 2.0 * (s_xr * s_xr + s_xt * s_xt + s_rt * s_rt)
        )
    )
    third = (s_xx + s_rr + s_tt) * (1.0 / 3.0)
    return (s_xx - third, s_xr, s_xt, s_rr - third, s_tt - third, s_rt), size


def kernel(
    n_ax, n_az, nx, nt,
    rho_ref, vel_ref, geo_in, seam_in, flux_ref, coef_ref,
    S, T, M, H, V, HM, PX, MX, E, G, GM, GH, GP, GHM, GV, SP,
    part, rec, rec_out, CS, geo_ref, seam_ref, own_sem, send_sem, recv_sem, sum_send, sum_recv,
):
    pr = 2 * nx
    me_ax, me_az = lax.axis_index("ax"), lax.axis_index("az")
    left, right = lax.rem(me_az + n_az - 1, n_az), lax.rem(me_az + 1, n_az)
    odd = lax.rem(me_ax, 2)
    even = 1 - odd
    mine, other = odd, even
    azimuth_cells = nt * n_az

    def pick(at_even, at_odd):
        return jnp.where(odd == 0, at_even, at_odd)

    has_lo, has_hi = me_ax > 0, me_ax < n_ax - 1
    pair_lo, pair_hi = me_ax >= 2, me_ax < n_ax - 2
    partner = me_ax + 1 - 2 * odd
    near_ax = me_ax - 2 + 4 * odd
    far_ax = me_ax + 2 - 4 * odd
    edge_ax = me_ax - 1 + 2 * odd
    has_near = (near_ax >= 0) & (near_ax < n_ax)
    has_far = (far_ax >= 0) & (far_ax < n_ax)

    lanes_mine = pl.ds(pl.multiple_of(mine * LANES, LANES), LANES)
    lanes_other = pl.ds(pl.multiple_of(other * LANES, LANES), LANES)
    cols = pl.ds(EDGE, nt)
    own_row = nx * odd
    own_at = own_row + 2
    partner_at = nx * even + 2
    near_at = pick(0, nx - 2)
    beyond_at = pick(pr + 2, 0)
    ahead_at = pick(0, pr + 2)
    pass_at = pick(pr, 2)

    own = [
        pltpu.make_async_copy(rho_ref.at[:, :, lanes_mine], S.at[0, pl.ds(own_at, nx), cols, :], own_sem.at[0]),
        pltpu.make_async_copy(
            vel_ref.at[:, :, :, lanes_mine], S.at[pl.ds(1, 3), pl.ds(own_at, nx), cols, :], own_sem.at[1]),
        pltpu.make_async_copy(rho_ref.at[:, :, lanes_other], T.at[0, pl.ds(1, nx), cols, :], own_sem.at[2]),
        pltpu.make_async_copy(
            vel_ref.at[:, :, :, lanes_other], T.at[pl.ds(1, 3), pl.ds(1, nx), cols, :], own_sem.at[3]),
    ]
    tables = [
        pltpu.make_async_copy(geo_in, geo_ref, own_sem.at[4]),
        pltpu.make_async_copy(seam_in, seam_ref, own_sem.at[5]),
    ]
    for c in own + tables:
        c.start()

    barrier = pltpu.get_barrier_semaphore()

    def greet(ax, az):
        pl.semaphore_signal(barrier, inc=1, device_id=(ax, az), device_id_type=MESH_ID)

    short = n_az == 4
    for d in (1, n_az - 1) if short else range(1, n_az):
        greet(me_ax, lax.rem(me_az + d, n_az))
    peers = 2 if short else n_az - 1
    if short:
        greet(partner, me_az)
        peers = peers + 1
    for step in (-2, 2) if short else (-1, 1, -2, 2):
        there = (me_ax + step >= 0) & (me_ax + step < n_ax)
        reach = 1 if short else n_az

        @pl.when(there)
        def _():
            for d in range(reach):
                greet(me_ax + step, lax.rem(me_az + d, n_az))

        peers = peers + jnp.where(there, reach, 0)

    ids = itertools.count()

    def remote(src, dst, ax, az):
        at = next(ids)
        return pltpu.make_async_remote_copy(
            src_ref=src, dst_ref=dst, send_sem=send_sem.at[at], recv_sem=recv_sem.at[at],
            device_id=(ax, az), device_id_type=MESH_ID)

    def block(src_row, count, first, width, lanes, dst, dst_row, dst_first, ax, az):
        rows, at = pl.ds(src_row, count), pl.ds(first, width)
        to_rows, to = pl.ds(dst_row, count), pl.ds(dst_first, width)
        return [
            remote(rho_ref.at[rows, at, lanes], dst.at[0, to_rows, to, :], ax, az),
            remote(vel_ref.at[:, rows, at, lanes], dst.at[pl.ds(1, 3), to_rows, to, :], ax, az),
        ]

    def ends(src_row, count, lanes, dst, dst_row, ax, az):
        out = []
        for first in (0, nt - SUB):
            out += block(src_row, count, first, SUB, lanes, dst, dst_row, EDGE + first, ax, az)
        return out

    def middle(src_row, count, lanes, dst, dst_row, ax, az):
        return block(src_row, count, SUB, nt - 2 * SUB, lanes, dst, dst_row, EDGE + SUB, ax, az)

    def around(ref, lead, rows):
        at = (pl.ds(EDGE + nt - SUB, SUB), pl.ds(EDGE - SUB, SUB), pl.ds(EDGE, SUB), pl.ds(EDGE + nt, SUB))
        return [
            remote(ref.at[lead, rows, at[0], :], ref.at[lead, rows, at[1], :], me_ax, right),
            remote(ref.at[lead, rows, at[2], :], ref.at[lead, rows, at[3], :], me_ax, left),
        ]

    whole = pl.ds(SUB, nt)

    def seam_around(s):
        return [
            remote(E.at[s, pl.ds(nt, SUB), :], E.at[s, pl.ds(0, SUB), :], me_ax, right),
            remote(E.at[s, pl.ds(SUB, SUB), :], E.at[s, pl.ds(SUB + nt, SUB), :], me_ax, left),
        ]

    s_own, s_partner, s_beyond, s_ahead = 1 + odd, 2 - odd, pick(3, 0), pick(0, 3)

    own_around = []
    for lanes, dst, row in ((lanes_mine, S, own_at), (lanes_other, T, 1)):
        own_around += block(0, nx, nt - SUB, SUB, lanes, dst, row, EDGE - SUB, me_ax, right)
        own_around += block(0, nx, 0, SUB, lanes, dst, row, EDGE + nt, me_ax, left)
    seam_own = seam_around(s_own)
    seam_partner_around = seam_around(s_partner)
    seam_beyond_around = seam_around(s_beyond)
    seam_ahead_around = seam_around(s_ahead)

    seam_swap = remote(E.at[s_own, whole, :], E.at[s_own, whole, :], partner, me_az)
    seam_near = remote(E.at[s_own, whole, :], E.at[pick(3, 0), whole, :], near_ax, me_az)
    seam_pass = remote(E.at[s_partner, whole, :], E.at[pick(0, 3), whole, :], far_ax, me_az)

    swap_ends = ends(0, nx, lanes_other, S, own_at, partner, me_az)
    swap_rows = {}
    for q in range(nx):
        row = pick(nx - 1 - q, q)
        swap_rows[q] = middle(row, 1, lanes_other, S, own_at + row, partner, me_az)
    near_ends = ends(near_at, 2, lanes_mine, S, beyond_at, near_ax, me_az)
    near_rows = middle(near_at, 2, lanes_mine, S, beyond_at, near_ax, me_az)

    every = pl.ds(0, 4)

    def forward(row, first, width, count):
        return remote(
            S.at[:, pl.ds(pass_at + row, count), pl.ds(EDGE + first, width), :],
            S.at[:, pl.ds(ahead_at + row, count), pl.ds(EDGE + first, width), :], far_ax, me_az)

    pass_ends = [forward(0, first, SUB, 2) for first in (0, nt - SUB)]
    last_row = pick(1, 0)
    pass_rows = [forward(last_row, SUB, nt - 2 * SUB, 1), forward(1 - last_row, SUB, nt - 2 * SUB, 1)]
    partner_around = around(S, every, pl.ds(partner_at, nx))
    beyond_around = around(S, every, pl.ds(beyond_at, 2))
    ahead_around = around(S, every, pl.ds(ahead_at, 2))

    swap_row, edge_row = pick(nx - 1, 0), pick(0, nx - 1)
    three = pl.ds(1, 3)

    def flux_rows(row, dst_row, ax):
        return remote(
            vel_ref.at[:, pl.ds(row, 1), :, lanes_mine], T.at[three, pl.ds(dst_row, 1), cols, :], ax, me_az)

    def flux_stress(row, dst_row, ax):
        return remote(
            M.at[mine, pl.ds(0, 3), own_row + row + 1, cols, :], M.at[mine, pl.ds(0, 3), dst_row, cols, :],
            ax, me_az)

    swap_vel = flux_rows(swap_row, pick(0, nx + 1), partner)
    edge_vel = flux_rows(edge_row, pick(nx + 1, 0), edge_ax)
    swap_vel_around = around(T, three, pl.ds(pick(nx + 1, 0), 1))
    edge_vel_around = around(T, three, pl.ds(pick(0, nx + 1), 1))
    swap_stress = flux_stress(swap_row, pick(nx, nx + 1), partner)
    edge_stress = flux_stress(edge_row, pick(pr + 1, 0), edge_ax)

    def start(copies):
        for c in copies:
            c.start()

    def arrive(copies):
        for c in copies:
            c.wait_recv()

    def leave(copies):
        for c in copies:
            c.wait_send()

    wide = nt + 2 * SUB
    outer_cols = EDGE - SUB

    def lanes_at(n):
        return lax.broadcasted_iota(jnp.int32, (n, LANES), 1)

    def spread(values, rows):
        return jnp.concatenate([values] * (rows // SUB), axis=values.ndim - 2)

    def pack_seam():
        lane = lanes_at(nt)
        from_mine = jnp.where(lane >= LANES - SEAM // 2, 1, 0) == even
        packed = jnp.zeros((nt, LANES), jnp.float32)
        for a in range(4):
            for i in range(nx):
                first = (a * nx + i) * SEAM
                x = jnp.where(from_mine, S[a, own_at + i, pl.ds(EDGE, nt), :], T[a, 1 + i, pl.ds(EDGE, nt), :])
                x = pltpu.roll(x, (first + SEAM // 2) % LANES, 1)
                packed = jnp.where((lane >= first) & (lane < first + SEAM), x, packed)
        E[s_own, whole, :] = packed

    n_seam = math.gcd(BLOCKS["seam"], wide)
    seam_lane = lanes_at(n_seam)
    seam_row = seam_lane // SEAM
    at_bottom = seam_row == jnp.where(pair_lo, -1, nx)
    at_top = seam_row == jnp.where(pair_hi, -1, nx + pr - 1)

    def seam_below(x):
        return jnp.where(at_bottom, x, pltpu.roll(x, SEAM, 1))

    def seam_above(x):
        return jnp.where(at_top, x, pltpu.roll(x, LANES - SEAM, 1))

    def seam_axial(x):
        return (seam_below(x) + x) + (x + seam_above(x))

    def seam_slope(x):
        return (pltpu.roll(x, LANES - 1, 1) - pltpu.roll(x, 1, 1)) * (0.5 / STEP_RADIAL)

    def seam_radial(s):
        return ((pltpu.roll(s, 1, 1) + pltpu.roll(s, LANES - 1, 1)) + (s + s)) * (1.0 / 64.0)

    def seam_turn(ref, a, c, n):
        x = ref[a, pl.ds(c, n), :]
        return (ref[a, pl.ds(c - 1, n), :] + ref[a, pl.ds(c + 1, n), :]) + (x + x)

    def seam_pass_all():
        tiles = [(c, n_seam) for c in range(outer_cols, outer_cols + wide, n_seam)]
        inner = [(c, n_seam) for c in range(EDGE, EDGE + nt, n_seam)]
        lane = lanes_at(wide)
        per = nx * SEAM
        for a in range(4):
            packed = jnp.zeros((wide, LANES), jnp.float32)
            for s in range(4):
                x = E[s, :, :]
                if s != a:
                    x = pltpu.roll(x, (s - a) * per % LANES, 1)
                packed = jnp.where((lane >= s * per) & (lane < (s + 1) * per), x, packed)
            G[a, pl.ds(outer_cols, wide), :] = packed
        for c, n in tiles:
            at, at_before, at_after = pl.ds(c, n), pl.ds(c - 1, n), pl.ds(c + 1, n)
            rho = G[0, at, :]
            vel = [G[1 + a, at, :] for a in range(3)]
            inv_r, az_scale, width = (spread(seam_ref[g], n) for g in (0, 1, 2))
            dx = [seam_above(v) - seam_below(v) for v in vel]
            dr = [seam_slope(v) for v in vel]
            dt = [(G[1 + a, at_after, :] - G[1 + a, at_before, :]) * az_scale for a in range(3)]
            dev, size = strain(dx, dr, dt, vel[1], vel[2], inv_r)
            scale = rho * width * size
            for q, a in enumerate(KEPT):
                GM[q, at, :] = seam_axial(scale * dev[a])
            mom = [rho * v for v in vel]
            GH[0, at, :] = seam_axial(rho)
            for a in range(3):
                GH[1 + a, at, :] = seam_axial(mom[a])
            for q, p in enumerate(pairs(mom, vel)):
                GP[q, at, :] = seam_axial(p)
        for c, n in tiles:
            at = pl.ds(c, n)
            hat = [seam_radial(seam_turn(GH, a, c, n)) for a in range(4)]
            inv = 1.0 / hat[0]
            for a in range(4):
                GHM[a, at, :] = hat[a]
            for a in range(3):
                GV[a, at, :] = hat[1 + a] * inv
        sums = [0.0, 0.0]
        for c, n in inner:
            at, at_before, at_after = pl.ds(c, n), pl.ds(c - 1, n), pl.ds(c + 1, n)
            inv_r, az_scale, width4 = (spread(seam_ref[g], n) for g in (0, 1, 3))
            hv = [GV[a, at, :] for a in range(3)]
            dx = [seam_above(v) - seam_below(v) for v in hv]
            dr = [seam_slope(v) for v in hv]
            dt = [(GV[a, at_after, :] - GV[a, at_before, :]) * az_scale for a in range(3)]
            dev, size = strain(dx, dr, dt, hv[1], hv[2], inv_r)
            terms = contractions(
                dev, width4 * GHM[0, at, :] * size,
                [seam_radial(seam_turn(GP, q, c, n)) for q in range(5)],
                [seam_radial(seam_turn(GM, q, c, n)) for q in range(5)],
                [GHM[1 + a, at, :] for a in range(3)], hv)
            sums = [x + fold_rows(y) for x, y in zip(sums, terms)]
        for q in range(2):
            row = jnp.sum(sums[q], axis=0, keepdims=True)
            for r in range(pr):
                shift = LANES - SEAM // 2 - SEAM * (nx + r)
                SP[r, pl.ds(q, 1), :] = pltpu.roll(row, shift % LANES, 1)

    def smooth(ref, a, row, first, n):
        x = ref[a, row, pl.ds(first, n), :]
        s = (ref[a, row, pl.ds(first - 1, n), :] + ref[a, row, pl.ds(first + 1, n), :]) + (x + x)
        return radial(s)

    def whole_slope(a, x, first, r):
        shift = pick(LANES - 1, LANES + 1) - SEAM // 2 - SEAM * (r + nx)
        end = pick(LANES - 1, 0)
        far = pltpu.roll(G[1 + a, pl.ds(first, x.shape[0]), :], shift, 1)
        lane = lane_of(x)
        far = jnp.where(lane == end, far, x)
        lo = jnp.where(lane == 0, far, pltpu.roll(x, 1, 1))
        hi = jnp.where(lane == LANES - 1, far, pltpu.roll(x, LANES - 1, 1))
        return (hi - lo) * (0.5 / STEP_RADIAL)

    def low(r):
        return jnp.maximum(r - 1, jnp.where(pair_lo, -2, 0))

    def high(r):
        return jnp.minimum(r + 1, jnp.where(pair_hi, pr + 1, pr - 1))

    def sweep(first, count, body):
        def step(at, carry):
            t = first + at
            body(pick(t, pr - 1 - t))
            return carry

        lax.fori_loop(0, count, step, 0)

    def turn_slope(ref, a, row, first, n):
        return ref[a, row, pl.ds(first + 1, n), :] - ref[a, row, pl.ds(first - 1, n), :]

    def first_block(r, with_pairs, exact, c, n):
        rows = (low(r) + 2, r + 2, high(r) + 2)
        rho = [S[0, q, pl.ds(c, n), :] for q in rows]
        vel = [[S[1 + a, q, pl.ds(c, n), :] for a in range(3)] for q in rows]
        inv_r, az_scale, width = (spread(geo_ref[g, mine], n) for g in (0, 1, 2))
        dx = [vel[2][a] - vel[0][a] for a in range(3)]
        dr = [whole_slope(a, vel[1][a], c, r) if exact else slope(vel[1][a]) for a in range(3)]
        dt = [turn_slope(S, 1 + a, r + 2, c, n) * az_scale for a in range(3)]
        dev, size = strain(dx, dr, dt, vel[1][1], vel[1][2], inv_r)
        scale = rho[1] * width * size
        for a in range(6):
            M[mine, a, r + 1, pl.ds(c, n), :] = scale * dev[a]
        mom = [[rho[q] * vel[q][a] for a in range(3)] for q in range(3)]
        H[0, r + 1, pl.ds(c, n), :] = (rho[0] + rho[1]) + (rho[1] + rho[2])
        for a in range(3):
            H[1 + a, r + 1, pl.ds(c, n), :] = (mom[0][a] + mom[1][a]) + (mom[1][a] + mom[2][a])
        if with_pairs:
            for at, p in enumerate(zip(*(pairs(mom[q], vel[q]) for q in range(3)))):
                PX[at, r, pl.ds(c, n), :] = (p[0] + p[1]) + (p[1] + p[2])

    def hat_block(r, c, n):
        hat = [smooth(H, a, r + 1, c, n) for a in range(4)]
        inv = 1.0 / hat[0]
        for a in range(4):
            HM[a, r + 1, pl.ds(c, n), :] = hat[a]
        for a in range(3):
            V[a, r + 1, pl.ds(c, n), :] = hat[1 + a] * inv

    def model_pass(r):
        n = math.gcd(BLOCKS["model"], wide)
        for c in range(outer_cols, outer_cols + wide, n):
            for q, a in enumerate(KEPT):
                x = M[mine, a, r + 1, pl.ds(c, n), :]
                lo = M[mine, a, low(r) + 1, pl.ds(c, n), :]
                MX[q, r, pl.ds(c, n), :] = (lo + x) + (x + M[mine, a, high(r) + 1, pl.ds(c, n), :])

    def closure_pass(r):
        sums = [0.0, 0.0]
        n = math.gcd(BLOCKS["closure"], nt)
        for c in range(EDGE, EDGE + nt, n):
            inv_r, az_scale, width4 = (spread(geo_ref[g, mine], n) for g in (0, 1, 3))
            hv = [V[a, r + 1, pl.ds(c, n), :] for a in range(3)]
            hm = [HM[1 + a, r + 1, pl.ds(c, n), :] for a in range(3)]
            dx = [V[a, high(r) + 1, pl.ds(c, n), :] - V[a, low(r) + 1, pl.ds(c, n), :] for a in range(3)]
            dr = [slope(hv[a]) for a in range(3)]
            dt = [turn_slope(V, a, r + 1, c, n) * az_scale for a in range(3)]
            dev, size = strain(dx, dr, dt, hv[1], hv[2], inv_r)
            terms = contractions(
                dev, width4 * HM[0, r + 1, pl.ds(c, n), :] * size,
                [smooth(PX, q, r, c, n) for q in range(5)], [smooth(MX, q, r, c, n) for q in range(5)], hm, hv)
            sums = [x + fold_rows(y) for x, y in zip(sums, terms)]
        lane = lanes_at(1)
        at_seam = jnp.where(odd == 0, LANES - 1 - lane, lane) < 2
        for q in range(2):
            row = jnp.sum(sums[q], axis=0, keepdims=True)
            part[r, pl.ds(q, 1), :] = jnp.where(at_seam, SP[r, pl.ds(q, 1), :], row)

    def first_two(first, count, with_pairs=True):
        n = math.gcd(BLOCKS["first"], wide)
        blocks = list(range(outer_cols, outer_cols + wide, n))

        def both(exact, r):
            for at, c in enumerate(blocks):
                first_block(r, with_pairs, exact, c, n)
                if at >= 2:
                    hat_block(r, blocks[at - 2], n)
            for c in blocks[-2:]:
                hat_block(r, c, n)

        exact = min(max(nx + 1 - first, 0), count)
        if exact:
            sweep(first, exact, functools.partial(both, True))
        if exact < count:
            sweep(first + exact, count - exact, functools.partial(both, False))

    def close(first, count):
        sweep(first, count, model_pass)
        sweep(first, count, closure_pass)

    def other_half(i):
        n = math.gcd(BLOCKS["other"], wide)
        for c in range(outer_cols, outer_cols + wide, n):
            inv_r, az_scale, width = (spread(geo_ref[g, other], n) for g in (0, 1, 2))
            lo = jnp.maximum(i - 1, jnp.where(has_lo, -1, 0)) + 1
            hi = jnp.minimum(i + 1, jnp.where(has_hi, nx, nx - 1)) + 1
            vel = [T[1 + a, i + 1, pl.ds(c, n), :] for a in range(3)]
            dx = [T[1 + a, hi, pl.ds(c, n), :] - T[1 + a, lo, pl.ds(c, n), :] for a in range(3)]
            dr = []
            for a in range(3):
                far = pltpu.roll(S[1 + a, own_at + i, pl.ds(c, n), :], pick(1, LANES - 1), 1)
                lane = lane_of(far)
                end = jnp.where(lane == pick(0, LANES - 1), far, vel[a])
                lo_side = jnp.where(lane == 0, end, pltpu.roll(vel[a], 1, 1))
                hi_side = jnp.where(lane == LANES - 1, end, pltpu.roll(vel[a], LANES - 1, 1))
                dr.append((hi_side - lo_side) * (0.5 / STEP_RADIAL))
            dt = [turn_slope(T, 1 + a, i + 1, c, n) * az_scale for a in range(3)]
            dev, size = strain(dx, dr, dt, vel[1], vel[2], inv_r)
            scale = T[0, i + 1, pl.ds(c, n), :] * width * size
            for a in range(6):
                M[other, a, own_row + i + 1, pl.ds(c, n), :] = scale * dev[a]

    def rows_of(first, count, body):
        def step(at, carry):
            body(first + at)
            return carry

        lax.fori_loop(0, count, step, 0)

    for c in own:
        c.wait()
    pack_seam()
    pl.semaphore_wait(barrier, peers)
    seam_swap.start()

    @pl.when(has_near)
    def _():
        seam_near.start()

    start(swap_ends + seam_own + own_around)

    @pl.when(has_near)
    def _():
        start(near_ends + near_rows)

    for q in [nx - 1, nx - 2] + list(range(nx - 2)):
        start(swap_rows[q])
    swap_vel.start()

    seam_swap.wait_recv()
    start(seam_partner_around)

    @pl.when(has_far)
    def _():
        seam_pass.start()
        seam_near.wait_recv()
        start(seam_beyond_around)

    arrive(own_around)
    for c in tables:
        c.wait()
    rows_of(1, nx - 2, other_half)

    @pl.when(has_near)
    def _():
        seam_pass.wait_recv()
        start(seam_ahead_around)

    arrive(swap_ends)
    start(partner_around)

    @pl.when(has_far)
    def _():
        start(pass_ends)
        arrive(near_ends)
        start(beyond_around)

    arrive(seam_own + seam_partner_around)

    @pl.when(has_far)
    def _():
        arrive(seam_beyond_around)

    @pl.when(has_near)
    def _():
        arrive(seam_ahead_around)

    seam_pass_all()
    first_two(1, nx - 2)

    @pl.when(has_near)
    def _():
        arrive(pass_ends)
        start(ahead_around)

    def hand_on(at):
        arrive(swap_rows[nx - 1 - at])

        @pl.when(has_far)
        def _():
            pass_rows[at].start()

    hand_on(0)

    @pl.when(has_far)
    def _():
        arrive(near_rows + beyond_around)

    arrive(partner_around)
    first_two(pr, 1, False)
    hand_on(1)
    first_two(pr - 1, 1)

    @pl.when(has_near)
    def _():
        edge_vel.start()
        arrive([pass_rows[0]] + ahead_around)

    first_two(0, 1)
    close(1, 1)
    for q in range(nx - 3):
        arrive(swap_rows[q])
        first_two(nx - 1 + q, 1)
        close(nx - 2 + q, 1)

    @pl.when(has_near)
    def _():
        arrive([pass_rows[1]])

    first_two(-1, 1, False)
    close(0, 1)
    arrive(swap_rows[nx - 3])
    swap_stress.start()

    @pl.when(has_near)
    def _():
        edge_stress.start()

    first_two(pr - 4, 3)
    close(pr - 5, 5)

    def share(at, src, dst, ax, d):
        return pltpu.make_async_remote_copy(
            src_ref=src, dst_ref=dst, send_sem=sum_send.at[at], recv_sem=sum_recv.at[at],
            device_id=(ax, lax.rem(me_az + d, n_az)), device_id_type=MESH_ID)

    def end_row(kind, half, row, ax):
        return [
            share((2 + 2 * kind + half) * n_az + d, part.at[row], rec_out.at[half, me_az], ax, d)
            for d in range(n_az)
        ]

    across = [share(d, part, rec.at[mine, me_az], me_ax, d) for d in range(1, n_az)]
    over = [share(n_az + d, part, rec.at[mine, me_az], partner, d) for d in range(n_az)]
    lower_ax, upper_ax = me_ax - odd - 1, me_ax - odd + 2
    down, up = end_row(0, mine, 0, lower_ax), end_row(1, mine, pr - 1, upper_ax)
    end_sums = end_row(even, 0, 0, me_ax) + end_row(even, 1, 0, me_ax)

    @pl.when(pair_lo)
    def _():
        start(down)

    @pl.when(pair_hi)
    def _():
        start(up)

    start(over)
    start(across)
    rec[mine, me_az] = part[...]
    swap_vel.wait_recv()
    start(swap_vel_around)

    @pl.when(has_near)
    def _():
        edge_vel.wait_recv()
        start(edge_vel_around)

    arrive(swap_vel_around)
    other_half(swap_row)

    @pl.when(has_near)
    def _():
        arrive(edge_vel_around)

    other_half(edge_row)

    def ratio(sums):
        lm, mm = sums[0:1], sums[1:2]
        return -0.5 * (lm * (1.0 / azimuth_cells)) / (mm * (1.0 / azimuth_cells) + TINY)

    def total(ref, h, row):
        terms = [ref[h, d] if row is None else ref[h, d, row] for d in range(n_az)]
        sums = terms[0]
        for x in terms[1:]:
            sums = sums + x
        return sums

    def keep(row, h, value):
        CS[row, h] = jnp.broadcast_to(-2.0 * value, (SUB, LANES))

    arrive(across)
    arrive(over)
    for i in range(nx + 1):
        row = i + even
        for h in range(2):
            keep(row, h, ratio(total(rec, h, own_row + row - 1)))
    for i in range(nx):
        for h in range(2):
            coef_ref[pl.ds(i, 1), pl.ds(h * LANES, LANES)] = -0.5 * CS[i + 1, h, pl.ds(0, 1), :]

    def flux_pass(i):
        n = math.gcd(BLOCKS["flux"], nt)
        for c in range(EDGE, EDGE + nt, n):
            r = own_row + i + 1
            inv_r, az_scale, radius, back, radius2, back2 = (spread(geo_ref[g], n) for g in (0, 1, 4, 5, 6, 7))
            lo = jnp.maximum(i - 1, jnp.where(has_lo, -1, 0)) + 1
            hi = jnp.minimum(i + 1, jnp.where(has_hi, nx, nx - 1)) + 1
            here, below, above = (spread(CS[q], n) for q in (i + 1, lo, hi))

            def at(a, row, shift=0):
                return M[:, a, row, pl.ds(c + shift, n), :]

            def axial(a):
                return above * at(a, own_row + hi) - below * at(a, own_row + lo)

            def around_of(a):
                return (at(a, r, 1) - at(a, r, -1)) * turn

            turn = here * az_scale
            once = here * radius
            d_xr = rise(once * at(1, r)) * back
            d_rr = rise(once * at(3, r)) * back
            d_rt = rise(here * radius2 * at(5, r)) * back2
            out = (
                axial(0) + d_xr + around_of(2),
                axial(1) + d_rr + around_of(5) - here * at(4, r) * inv_r,
                axial(2) + d_rt + around_of(4),
            )
            for a in range(3):
                for h in range(2):
                    flux_ref[a, i, pl.ds(c - EDGE, n), pl.ds(h * LANES, LANES)] = out[a][h]

    rows_of(1, nx - 2, flux_pass)

    @pl.when(has_near)
    def _():
        arrive(end_sums)

    swap_stress.wait_recv()
    flux_pass(swap_row)

    @pl.when(has_near)
    def _():
        for h in range(2):
            keep(pick(0, nx + 1), h, ratio(total(rec_out, h, None)))
        edge_stress.wait_recv()

    flux_pass(edge_row)

    leave([seam_swap, swap_vel, swap_stress] + swap_ends + own_around + seam_own + seam_partner_around)
    leave(partner_around + swap_vel_around + across + over)
    for q in range(nx):
        leave(swap_rows[q])

    @pl.when(has_near)
    def _():
        leave([seam_near, edge_vel, edge_stress] + near_ends + near_rows)
        leave(seam_ahead_around + ahead_around + edge_vel_around)

    @pl.when(has_far)
    def _():
        leave([seam_pass] + pass_ends + pass_rows + seam_beyond_around + beyond_around)

    @pl.when(pair_lo)
    def _():
        leave(down)

    @pl.when(pair_hi)
    def _():
        leave(up)


def hand_over(flux_in, coef_in, flux_out, coef_out, flux_buf, coef_buf, sems):
    count = flux_in.shape[0]
    pieces = [(flux_in.at[a], flux_buf.at[a], flux_out.at[a]) for a in range(count)]
    pieces.append((coef_in, coef_buf, coef_out))
    give = [pltpu.make_async_copy(a, c, sems.at[1, at]) for at, (a, b, c) in enumerate(pieces)]
    for c in give:
        c.start()
    for c in give:
        c.wait()


def shards(n_ax, n_az, density, velocity):
    nx, nt, radial = density.shape
    assert radial == 2 * LANES and 4 * nx * SEAM == LANES and n_ax % 2 == 0
    pr, seam_rows = 2 * nx, nt + 2 * SUB
    halves, seam = geometry(radial, nt * n_az)

    def field(*lead):
        return pltpu.VMEM(lead + (nt + 2 * EDGE, LANES), jnp.float32)

    def vmem(*shape):
        return pltpu.VMEM(shape, jnp.float32)

    dma = pltpu.SemaphoreType.DMA
    flux, coef = pl.pallas_call(
        functools.partial(kernel, n_ax, n_az, nx, nt),
        out_shape=(
            jax.ShapeDtypeStruct(velocity.shape, jnp.float32),
            jax.ShapeDtypeStruct((nx, radial), jnp.float32),
        ),
        in_specs=[
            pl.BlockSpec(memory_space=pltpu.HBM),
            pl.BlockSpec(memory_space=pltpu.HBM),
            pl.BlockSpec(memory_space=pltpu.HBM),
            pl.BlockSpec(memory_space=pltpu.HBM),
        ],
        out_specs=(
            pl.BlockSpec(memory_space=pltpu.VMEM),
            pl.BlockSpec(memory_space=pltpu.VMEM),
        ),
        scratch_shapes=[
            field(4, pr + 4),
            field(4, nx + 2),
            field(2, 6, pr + 2),
            field(4, pr + 2),
            field(3, pr + 2),
            field(4, pr + 2),
            field(5, pr),
            field(5, pr),
            vmem(4, seam_rows, LANES),
            field(4),
            field(5),
            field(4),
            field(5),
            field(4),
            field(3),
            vmem(pr, 2, LANES),
            vmem(pr, 2, LANES),
            vmem(2, n_az, pr, 2, LANES),
            vmem(2, n_az, 2, LANES),
            vmem(nx + 2, 2, SUB, LANES),
            vmem(*halves.shape),
            vmem(*seam.shape),
            dma((6,)),
            dma((COPIES,)),
            dma((COPIES,)),
            dma((6 * n_az,)),
            dma((6 * n_az,)),
        ],
        compiler_params=pltpu.CompilerParams(collective_id=0, has_side_effects=True, vmem_limit_bytes=40 << 20),
        name="closure",
    )(pltpu.with_memory_space_constraint(density, pltpu.HBM), pltpu.with_memory_space_constraint(velocity, pltpu.HBM), pltpu.with_memory_space_constraint(jnp.asarray(halves), pltpu.HBM), pltpu.with_memory_space_constraint(jnp.asarray(seam), pltpu.HBM))
    flux, coef = (pltpu.with_memory_space_constraint(x, pltpu.VMEM) for x in (flux, coef))
    anywhere = pl.BlockSpec(memory_space=pl.ANY)
    return pl.pallas_call(
        hand_over,
        out_shape=(
            jax.ShapeDtypeStruct(flux.shape, jnp.float32),
            jax.ShapeDtypeStruct(coef.shape, jnp.float32),
        ),
        in_specs=[pl.BlockSpec(memory_space=pltpu.VMEM)] * 2,
        out_specs=(pl.BlockSpec(memory_space=pltpu.HBM),) * 2,
        scratch_shapes=[
            pltpu.VMEM(flux.shape, jnp.float32),
            pltpu.VMEM(coef.shape, jnp.float32),
            dma((2, flux.shape[0] + 1)),
        ],
        name="hand_over",
    )(flux, coef)


def solution(mesh):
    in_specs = (P("ax", "az", None), P(None, "ax", "az", None))
    out_specs = (P(None, "ax", "az", None), P("ax", None))
    body = functools.partial(shards, mesh.shape["ax"], mesh.shape["az"])
    return jax.shard_map(body, mesh=mesh, in_specs=in_specs, out_specs=out_specs, check_vma=False)
```

```python
import functools
import itertools
import math

import jax
import jax.numpy as jnp
import numpy as np
from jax import lax
from jax.experimental import pallas as pl
from jax.experimental.pallas import tpu as pltpu
from jax.sharding import PartitionSpec as P

STEP_AXIAL = 0.5
STEP_RADIAL = 0.25
INNER_RADIUS = 10.0
FILTER_RATIO = 2.0
TINY = 1e-06
KEPT = (0, 3, 1, 2, 5)
CROSS = ((0, 1), (0, 2), (1, 2))
LANES = 128
SUB = 8
EDGE = 16
SEAM = 8
COPIES = 64
BLOCKS = {'first': 16, 'hat': 16, 'model': 16, 'closure': 16, 'other': 16, 'flux': 16, 'seam': 16}
MESH_ID = pl.DeviceIdType.MESH


def geometry(radial, azimuth_cells):
    radius = INNER_RADIUS + (np.arange(radial, dtype=np.float64) + 0.5) * STEP_RADIAL
    angle = 2.0 * math.pi / azimuth_cells
    width = (STEP_AXIAL * STEP_RADIAL * angle * radius) ** (2.0 / 3.0)
    rows = np.stack(
        [
            1.0 / radius,
            0.5 / (radius * angle),
            width,
            FILTER_RATIO**2 * width,
            radius,
            0.5 / STEP_RADIAL / radius,
            radius * radius,
            0.5 / STEP_RADIAL / (radius * radius),
        ]
    ).astype(np.float32)
    halves = rows.reshape(rows.shape[0], radial // LANES, 1, LANES)
    at_seam = radial // 2 - SEAM // 2 + np.arange(LANES) % SEAM
    seam = rows[:4, None, at_seam]
    return (
        np.ascontiguousarray(np.broadcast_to(halves, halves.shape[:2] + (SUB, LANES))),
        np.ascontiguousarray(np.broadcast_to(seam, (4, SUB, LANES))),
    )


def lane_of(x):
    return lax.broadcasted_iota(jnp.int32, x.shape, x.ndim - 1)


def before(x):
    y = pltpu.roll(x, 1, x.ndim - 1)
    fill = jnp.concatenate([x[:1], y[:-1]], axis=0)
    return jnp.where(lane_of(x) == 0, fill, y)


def after(x):
    y = pltpu.roll(x, LANES - 1, x.ndim - 1)
    fill = jnp.concatenate([y[1:], x[-1:]], axis=0)
    return jnp.where(lane_of(x) == LANES - 1, fill, y)


def rise(x):
    return after(x) - before(x)


def sides(x):
    lane = lane_of(x)
    return (
        jnp.where(lane == 0, x, pltpu.roll(x, 1, 1)),
        jnp.where(lane == LANES - 1, x, pltpu.roll(x, LANES - 1, 1)),
    )


def radial(s):
    lo, hi = sides(s)
    return ((lo + hi) + (s + s)) * (1.0 / 64.0)


def slope(x):
    lo, hi = sides(x)
    return (hi - lo) * (0.5 / STEP_RADIAL)


def pairs(mom, vel):
    azimuthal = mom[2] * vel[2]
    return [mom[a] * vel[a] - azimuthal for a in (0, 1)] + [mom[a] * vel[b] for a, b in CROSS]


def contractions(dev, scale, leonard, hat_model):
    mixed = [scale * dev[a] - m for a, m in zip(KEPT, hat_model)]

    def cross(left, right):
        return 2.0 * (left[2] * right[2] + left[3] * right[3] + left[4] * right[4])

    azimuthal = mixed[0] + mixed[1]
    lm = leonard[0] * mixed[0] + leonard[1] * mixed[1] + cross(leonard, mixed)
    mm = mixed[0] * mixed[0] + mixed[1] * mixed[1] + azimuthal * azimuthal + cross(mixed, mixed)
    return lm, mm


def fold_rows(cells):
    return sum(cells[at:at + SUB] for at in range(0, cells.shape[0], SUB))


def strain(dx, dr, dt, ur, ut, inv_r):
    s_xx, s_rr = dx[0], dr[1]
    s_tt = dt[2] + ur * inv_r
    s_xr = 0.5 * (dr[0] + dx[1])
    s_xt = 0.5 * (dt[0] + dx[2])
    s_rt = 0.5 * (dt[1] + dr[2] - ut * inv_r)
    size = jnp.sqrt(
        2.0
        * (
            s_xx * s_xx
            + s_rr * s_rr
            + s_tt * s_tt
            + 2.0 * (s_xr * s_xr + s_xt * s_xt + s_rt * s_rt)
        )
    )
    third = (s_xx + s_rr + s_tt) * (1.0 / 3.0)
    return (s_xx - third, s_xr, s_xt, s_rr - third, s_tt - third, s_rt), size


def kernel(
    n_ax, n_az, nx, nt,
    rho_ref, vel_ref, geo_in, seam_in, flux_ref, coef_ref,
    S, T, M, H, V, HM, PX, MX, LE, E, G, GM, GH, GP, GHM, GV, SP,
    part, rec, rec_out, CS, geo_ref, seam_ref, own_sem, send_sem, recv_sem, sum_send, sum_recv,
):
    pr = 2 * nx
    me_ax, me_az = lax.axis_index("ax"), lax.axis_index("az")
    left, right = lax.rem(me_az + n_az - 1, n_az), lax.rem(me_az + 1, n_az)
    odd = lax.rem(me_ax, 2)
    even = 1 - odd
    mine, other = odd, even
    azimuth_cells = nt * n_az

    def pick(at_even, at_odd):
        return jnp.where(odd == 0, at_even, at_odd)

    has_lo, has_hi = me_ax > 0, me_ax < n_ax - 1
    pair_lo, pair_hi = me_ax >= 2, me_ax < n_ax - 2
    partner = me_ax + 1 - 2 * odd
    near_ax = me_ax - 2 + 4 * odd
    far_ax = me_ax + 2 - 4 * odd
    edge_ax = me_ax - 1 + 2 * odd
    has_near = (near_ax >= 0) & (near_ax < n_ax)
    has_far = (far_ax >= 0) & (far_ax < n_ax)

    lanes_mine = pl.ds(pl.multiple_of(mine * LANES, LANES), LANES)
    lanes_other = pl.ds(pl.multiple_of(other * LANES, LANES), LANES)
    cols = pl.ds(EDGE, nt)
    own_row = nx * odd
    own_at = own_row + 2
    partner_at = nx * even + 2
    near_at = pick(0, nx - 2)
    beyond_at = pick(pr + 2, 0)
    ahead_at = pick(0, pr + 2)
    pass_at = pick(pr, 2)

    own = [
        pltpu.make_async_copy(rho_ref.at[:, :, lanes_mine], S.at[0, pl.ds(own_at, nx), cols, :], own_sem.at[0]),
        pltpu.make_async_copy(
            vel_ref.at[:, :, :, lanes_mine], S.at[pl.ds(1, 3), pl.ds(own_at, nx), cols, :], own_sem.at[1]),
        pltpu.make_async_copy(rho_ref.at[:, :, lanes_other], T.at[0, pl.ds(1, nx), cols, :], own_sem.at[2]),
        pltpu.make_async_copy(
            vel_ref.at[:, :, :, lanes_other], T.at[pl.ds(1, 3), pl.ds(1, nx), cols, :], own_sem.at[3]),
    ]
    tables = [
        pltpu.make_async_copy(geo_in, geo_ref, own_sem.at[4]),
        pltpu.make_async_copy(seam_in, seam_ref, own_sem.at[5]),
    ]
    for c in own + tables:
        c.start()

    barrier = pltpu.get_barrier_semaphore()

    def greet(ax, az):
        pl.semaphore_signal(barrier, inc=1, device_id=(ax, az), device_id_type=MESH_ID)

    short = n_az == 4
    for d in (1, n_az - 1) if short else range(1, n_az):
        greet(me_ax, lax.rem(me_az + d, n_az))
    peers = 2 if short else n_az - 1
    if short:
        greet(partner, me_az)
        peers = peers + 1
    for step in (-2, 2) if short else (-1, 1, -2, 2):
        there = (me_ax + step >= 0) & (me_ax + step < n_ax)
        reach = 1 if short else n_az

        @pl.when(there)
        def _():
            for d in range(reach):
                greet(me_ax + step, lax.rem(me_az + d, n_az))

        peers = peers + jnp.where(there, reach, 0)

    ids = itertools.count()

    def remote(src, dst, ax, az):
        at = next(ids)
        return pltpu.make_async_remote_copy(
            src_ref=src, dst_ref=dst, send_sem=send_sem.at[at], recv_sem=recv_sem.at[at],
            device_id=(ax, az), device_id_type=MESH_ID)

    def block(src_row, count, first, width, lanes, dst, dst_row, dst_first, ax, az):
        rows, at = pl.ds(src_row, count), pl.ds(first, width)
        to_rows, to = pl.ds(dst_row, count), pl.ds(dst_first, width)
        return [
            remote(rho_ref.at[rows, at, lanes], dst.at[0, to_rows, to, :], ax, az),
            remote(vel_ref.at[:, rows, at, lanes], dst.at[pl.ds(1, 3), to_rows, to, :], ax, az),
        ]

    def ends(src_row, count, lanes, dst, dst_row, ax, az):
        out = []
        for first in (0, nt - SUB):
            out += block(src_row, count, first, SUB, lanes, dst, dst_row, EDGE + first, ax, az)
        return out

    def middle(src_row, count, lanes, dst, dst_row, ax, az):
        return block(src_row, count, SUB, nt - 2 * SUB, lanes, dst, dst_row, EDGE + SUB, ax, az)

    def around(ref, lead, rows):
        at = (pl.ds(EDGE + nt - SUB, SUB), pl.ds(EDGE - SUB, SUB), pl.ds(EDGE, SUB), pl.ds(EDGE + nt, SUB))
        return [
            remote(ref.at[lead, rows, at[0], :], ref.at[lead, rows, at[1], :], me_ax, right),
            remote(ref.at[lead, rows, at[2], :], ref.at[lead, rows, at[3], :], me_ax, left),
        ]

    whole = pl.ds(SUB, nt)

    def seam_around(s):
        return [
            remote(E.at[s, pl.ds(nt, SUB), :], E.at[s, pl.ds(0, SUB), :], me_ax, right),
            remote(E.at[s, pl.ds(SUB, SUB), :], E.at[s, pl.ds(SUB + nt, SUB), :], me_ax, left),
        ]

    s_own, s_partner, s_beyond, s_ahead = 1 + odd, 2 - odd, pick(3, 0), pick(0, 3)

    own_around = []
    for lanes, dst, row in ((lanes_mine, S, own_at), (lanes_other, T, 1)):
        own_around += block(0, nx, nt - SUB, SUB, lanes, dst, row, EDGE - SUB, me_ax, right)
        own_around += block(0, nx, 0, SUB, lanes, dst, row, EDGE + nt, me_ax, left)
    seam_own = seam_around(s_own)
    seam_partner_around = seam_around(s_partner)
    seam_beyond_around = seam_around(s_beyond)
    seam_ahead_around = seam_around(s_ahead)

    seam_swap = remote(E.at[s_own, whole, :], E.at[s_own, whole, :], partner, me_az)
    seam_near = remote(E.at[s_own, whole, :], E.at[pick(3, 0), whole, :], near_ax, me_az)
    seam_pass = remote(E.at[s_partner, whole, :], E.at[pick(0, 3), whole, :], far_ax, me_az)

    swap_ends = ends(0, nx, lanes_other, S, own_at, partner, me_az)
    swap_rows = {}
    for q in range(nx):
        row = pick(nx - 1 - q, q)
        swap_rows[q] = middle(row, 1, lanes_other, S, own_at + row, partner, me_az)
    near_ends = ends(near_at, 2, lanes_mine, S, beyond_at, near_ax, me_az)
    near_rows = middle(near_at, 2, lanes_mine, S, beyond_at, near_ax, me_az)

    every = pl.ds(0, 4)

    def forward(row, first, width, count):
        return remote(
            S.at[:, pl.ds(pass_at + row, count), pl.ds(EDGE + first, width), :],
            S.at[:, pl.ds(ahead_at + row, count), pl.ds(EDGE + first, width), :], far_ax, me_az)

    pass_ends = [forward(0, first, SUB, 2) for first in (0, nt - SUB)]
    last_row = pick(1, 0)
    pass_rows = [forward(last_row, SUB, nt - 2 * SUB, 1), forward(1 - last_row, SUB, nt - 2 * SUB, 1)]
    partner_around = around(S, every, pl.ds(partner_at, nx))
    beyond_around = around(S, every, pl.ds(beyond_at, 2))
    ahead_around = around(S, every, pl.ds(ahead_at, 2))

    swap_row, edge_row = pick(nx - 1, 0), pick(0, nx - 1)
    three = pl.ds(1, 3)

    def flux_rows(row, dst_row, ax):
        return remote(
            vel_ref.at[:, pl.ds(row, 1), :, lanes_mine], T.at[three, pl.ds(dst_row, 1), cols, :], ax, me_az)

    def flux_stress(row, dst_row, ax):
        return remote(
            M.at[mine, pl.ds(0, 3), own_row + row + 1, cols, :], M.at[mine, pl.ds(0, 3), dst_row, cols, :],
            ax, me_az)

    swap_vel = flux_rows(swap_row, pick(0, nx + 1), partner)
    edge_vel = flux_rows(edge_row, pick(nx + 1, 0), edge_ax)
    swap_vel_around = around(T, three, pl.ds(pick(nx + 1, 0), 1))
    edge_vel_around = around(T, three, pl.ds(pick(0, nx + 1), 1))
    swap_stress = flux_stress(swap_row, pick(nx, nx + 1), partner)
    edge_stress = flux_stress(edge_row, pick(pr + 1, 0), edge_ax)

    def start(copies):
        for c in copies:
            c.start()

    def arrive(copies):
        for c in copies:
            c.wait_recv()

    def leave(copies):
        for c in copies:
            c.wait_send()

    wide = nt + 2 * SUB
    outer_cols = EDGE - SUB

    def lanes_at(n):
        return lax.broadcasted_iota(jnp.int32, (n, LANES), 1)

    def spread(values, rows):
        return jnp.concatenate([values] * (rows // SUB), axis=values.ndim - 2)

    def pack_seam():
        lane = lanes_at(nt)
        from_mine = jnp.where(lane >= LANES - SEAM // 2, 1, 0) == even
        packed = jnp.zeros((nt, LANES), jnp.float32)
        for a in range(4):
            for i in range(nx):
                first = (a * nx + i) * SEAM
                x = jnp.where(from_mine, S[a, own_at + i, pl.ds(EDGE, nt), :], T[a, 1 + i, pl.ds(EDGE, nt), :])
                x = pltpu.roll(x, (first + SEAM // 2) % LANES, 1)
                packed = jnp.where((lane >= first) & (lane < first + SEAM), x, packed)
        E[s_own, whole, :] = packed

    n_seam = math.gcd(BLOCKS["seam"], wide)
    seam_lane = lanes_at(n_seam)
    seam_row = seam_lane // SEAM
    at_bottom = seam_row == jnp.where(pair_lo, -1, nx)
    at_top = seam_row == jnp.where(pair_hi, -1, nx + pr - 1)

    def seam_below(x):
        return jnp.where(at_bottom, x, pltpu.roll(x, SEAM, 1))

    def seam_above(x):
        return jnp.where(at_top, x, pltpu.roll(x, LANES - SEAM, 1))

    def seam_axial(x):
        return (seam_below(x) + x) + (x + seam_above(x))

    def seam_slope(x):
        return (pltpu.roll(x, LANES - 1, 1) - pltpu.roll(x, 1, 1)) * (0.5 / STEP_RADIAL)

    def seam_radial(s):
        return ((pltpu.roll(s, 1, 1) + pltpu.roll(s, LANES - 1, 1)) + (s + s)) * (1.0 / 64.0)

    def seam_turn(ref, a, c, n):
        x = ref[a, pl.ds(c, n), :]
        return (ref[a, pl.ds(c - 1, n), :] + ref[a, pl.ds(c + 1, n), :]) + (x + x)

    def seam_pass_all():
        tiles = [(c, n_seam) for c in range(outer_cols, outer_cols + wide, n_seam)]
        inner = [(c, n_seam) for c in range(EDGE, EDGE + nt, n_seam)]
        lane = lanes_at(wide)
        per = nx * SEAM
        for a in range(4):
            packed = jnp.zeros((wide, LANES), jnp.float32)
            for s in range(4):
                x = E[s, :, :]
                if s != a:
                    x = pltpu.roll(x, (s - a) * per % LANES, 1)
                packed = jnp.where((lane >= s * per) & (lane < (s + 1) * per), x, packed)
            G[a, pl.ds(outer_cols, wide), :] = packed
        for c, n in tiles:
            at, at_before, at_after = pl.ds(c, n), pl.ds(c - 1, n), pl.ds(c + 1, n)
            rho = G[0, at, :]
            vel = [G[1 + a, at, :] for a in range(3)]
            inv_r, az_scale, width = (spread(seam_ref[g], n) for g in (0, 1, 2))
            dx = [seam_above(v) - seam_below(v) for v in vel]
            dr = [seam_slope(v) for v in vel]
            dt = [(G[1 + a, at_after, :] - G[1 + a, at_before, :]) * az_scale for a in range(3)]
            dev, size = strain(dx, dr, dt, vel[1], vel[2], inv_r)
            scale = rho * width * size
            for q, a in enumerate(KEPT):
                GM[q, at, :] = seam_axial(scale * dev[a])
            mom = [rho * v for v in vel]
            GH[0, at, :] = seam_axial(rho)
            for a in range(3):
                GH[1 + a, at, :] = seam_axial(mom[a])
            for q, p in enumerate(pairs(mom, vel)):
                GP[q, at, :] = seam_axial(p)
        for c, n in tiles:
            at = pl.ds(c, n)
            hat = [seam_radial(seam_turn(GH, a, c, n)) for a in range(4)]
            inv = 1.0 / hat[0]
            for a in range(4):
                GHM[a, at, :] = hat[a]
            for a in range(3):
                GV[a, at, :] = hat[1 + a] * inv
        sums = [0.0, 0.0]
        for c, n in inner:
            at, at_before, at_after = pl.ds(c, n), pl.ds(c - 1, n), pl.ds(c + 1, n)
            inv_r, az_scale, width4 = (spread(seam_ref[g], n) for g in (0, 1, 3))
            hv = [GV[a, at, :] for a in range(3)]
            dx = [seam_above(v) - seam_below(v) for v in hv]
            dr = [seam_slope(v) for v in hv]
            dt = [(GV[a, at_after, :] - GV[a, at_before, :]) * az_scale for a in range(3)]
            dev, size = strain(dx, dr, dt, hv[1], hv[2], inv_r)
            terms = contractions(
                dev, width4 * GHM[0, at, :] * size,
                [seam_radial(seam_turn(GP, q, c, n)) - p for q, p in
                 enumerate(pairs([GHM[1 + a, at, :] for a in range(3)], hv))],
                [seam_radial(seam_turn(GM, q, c, n)) for q in range(5)])
            sums = [x + fold_rows(y) for x, y in zip(sums, terms)]
        for q in range(2):
            row = jnp.sum(sums[q], axis=0, keepdims=True)
            for r in range(pr):
                shift = LANES - SEAM // 2 - SEAM * (nx + r)
                SP[r, pl.ds(q, 1), :] = pltpu.roll(row, shift % LANES, 1)

    def smooth(ref, a, row, first, n):
        x = ref[a, row, pl.ds(first, n), :]
        s = (ref[a, row, pl.ds(first - 1, n), :] + ref[a, row, pl.ds(first + 1, n), :]) + (x + x)
        return radial(s)

    def whole_slope(a, x, first, r):
        shift = pick(LANES - 1, LANES + 1) - SEAM // 2 - SEAM * (r + nx)
        end = pick(LANES - 1, 0)
        far = pltpu.roll(G[1 + a, pl.ds(first, x.shape[0]), :], shift, 1)
        lane = lane_of(x)
        far = jnp.where(lane == end, far, x)
        lo = jnp.where(lane == 0, far, pltpu.roll(x, 1, 1))
        hi = jnp.where(lane == LANES - 1, far, pltpu.roll(x, LANES - 1, 1))
        return (hi - lo) * (0.5 / STEP_RADIAL)

    def low(r):
        return jnp.maximum(r - 1, jnp.where(pair_lo, -2, 0))

    def high(r):
        return jnp.minimum(r + 1, jnp.where(pair_hi, pr + 1, pr - 1))

    def sweep(first, count, body, stride=1):
        def step(at, carry):
            t = first + at * stride
            body(pick(t, pr - 1 - t))
            return carry

        lax.fori_loop(0, count, step, 0)

    def turn_slope(ref, a, row, first, n):
        return ref[a, row, pl.ds(first + 1, n), :] - ref[a, row, pl.ds(first - 1, n), :]

    def first_block(r, with_pairs, exact, c, n):
        rows = (low(r) + 2, r + 2, high(r) + 2)
        rho = [S[0, q, pl.ds(c, n), :] for q in rows]
        vel = [[S[1 + a, q, pl.ds(c, n), :] for a in range(3)] for q in rows]
        inv_r, az_scale, width = (spread(geo_ref[g, mine], n) for g in (0, 1, 2))
        dx = [vel[2][a] - vel[0][a] for a in range(3)]
        dr = [whole_slope(a, vel[1][a], c, r) if exact else slope(vel[1][a]) for a in range(3)]
        dt = [turn_slope(S, 1 + a, r + 2, c, n) * az_scale for a in range(3)]
        dev, size = strain(dx, dr, dt, vel[1][1], vel[1][2], inv_r)
        scale = rho[1] * width * size
        for a in range(6):
            M[mine, a, r + 1, pl.ds(c, n), :] = scale * dev[a]
        mom = [[rho[q] * vel[q][a] for a in range(3)] for q in range(3)]
        H[0, r + 1, pl.ds(c, n), :] = (rho[0] + rho[1]) + (rho[1] + rho[2])
        for a in range(3):
            H[1 + a, r + 1, pl.ds(c, n), :] = (mom[0][a] + mom[1][a]) + (mom[1][a] + mom[2][a])
        if with_pairs:
            for at, p in enumerate(zip(*(pairs(mom[q], vel[q]) for q in range(3)))):
                PX[at, r, pl.ds(c, n), :] = (p[0] + p[1]) + (p[1] + p[2])

    def hat_block(r, c, n):
        hat = [smooth(H, a, r + 1, c, n) for a in range(4)]
        inv = 1.0 / hat[0]
        for a in range(4):
            HM[a, r + 1, pl.ds(c, n), :] = hat[a]
        for a in range(3):
            V[a, r + 1, pl.ds(c, n), :] = hat[1 + a] * inv

    def model_pass(r):
        n = math.gcd(BLOCKS["model"], wide)
        for c in range(outer_cols, outer_cols + wide, n):
            for q, a in enumerate(KEPT):
                x = M[mine, a, r + 1, pl.ds(c, n), :]
                lo = M[mine, a, low(r) + 1, pl.ds(c, n), :]
                MX[q, r, pl.ds(c, n), :] = (lo + x) + (x + M[mine, a, high(r) + 1, pl.ds(c, n), :])

    def leonard_pass(r):
        n = math.gcd(BLOCKS["closure"], nt)
        for c in range(EDGE, EDGE + nt, n):
            hv = [V[a, r + 1, pl.ds(c, n), :] for a in range(3)]
            hm = [HM[1 + a, r + 1, pl.ds(c, n), :] for a in range(3)]
            for q, p in enumerate(pairs(hm, hv)):
                LE[q, r, pl.ds(c, n), :] = smooth(PX, q, r, c, n) - p

    def closure_pass(r):
        sums = [0.0, 0.0]
        n = math.gcd(BLOCKS["closure"], nt)
        for c in range(EDGE, EDGE + nt, n):
            inv_r, az_scale, width4 = (spread(geo_ref[g, mine], n) for g in (0, 1, 3))
            hv = [V[a, r + 1, pl.ds(c, n), :] for a in range(3)]
            dx = [V[a, high(r) + 1, pl.ds(c, n), :] - V[a, low(r) + 1, pl.ds(c, n), :] for a in range(3)]
            dr = [slope(hv[a]) for a in range(3)]
            dt = [turn_slope(V, a, r + 1, c, n) * az_scale for a in range(3)]
            dev, size = strain(dx, dr, dt, hv[1], hv[2], inv_r)
            terms = contractions(
                dev, width4 * HM[0, r + 1, pl.ds(c, n), :] * size,
                [LE[q, r, pl.ds(c, n), :] for q in range(5)], [smooth(MX, q, r, c, n) for q in range(5)])
            sums = [x + fold_rows(y) for x, y in zip(sums, terms)]
        lane = lanes_at(1)
        at_seam = jnp.where(odd == 0, LANES - 1 - lane, lane) < 2
        for q in range(2):
            row = jnp.sum(sums[q], axis=0, keepdims=True)
            part[r, pl.ds(q, 1), :] = jnp.where(at_seam, SP[r, pl.ds(q, 1), :], row)

    def first_two(first, count, with_pairs=True):
        n = math.gcd(BLOCKS["first"], wide)
        blocks = list(range(outer_cols, outer_cols + wide, n))

        def both(exact, r):
            for at, c in enumerate(blocks):
                first_block(r, with_pairs, exact, c, n)
                if at >= 2:
                    hat_block(r, blocks[at - 2], n)
            for c in blocks[-2:]:
                hat_block(r, c, n)

        exact = min(max(nx + 1 - first, 0), count)
        if exact:
            sweep(first, exact, functools.partial(both, True))
        if exact < count:
            sweep(first + exact, count - exact, functools.partial(both, False))

    def close(first, count, stride=1, leonard=True):
        def both(r):
            if leonard:
                leonard_pass(r)
            model_pass(r)
            closure_pass(r)

        sweep(first, count, both, stride)

    def other_half(i):
        n = math.gcd(BLOCKS["other"], wide)
        for c in range(outer_cols, outer_cols + wide, n):
            inv_r, az_scale, width = (spread(geo_ref[g, other], n) for g in (0, 1, 2))
            lo = jnp.maximum(i - 1, jnp.where(has_lo, -1, 0)) + 1
            hi = jnp.minimum(i + 1, jnp.where(has_hi, nx, nx - 1)) + 1
            vel = [T[1 + a, i + 1, pl.ds(c, n), :] for a in range(3)]
            dx = [T[1 + a, hi, pl.ds(c, n), :] - T[1 + a, lo, pl.ds(c, n), :] for a in range(3)]
            dr = []
            for a in range(3):
                far = pltpu.roll(S[1 + a, own_at + i, pl.ds(c, n), :], pick(1, LANES - 1), 1)
                lane = lane_of(far)
                end = jnp.where(lane == pick(0, LANES - 1), far, vel[a])
                lo_side = jnp.where(lane == 0, end, pltpu.roll(vel[a], 1, 1))
                hi_side = jnp.where(lane == LANES - 1, end, pltpu.roll(vel[a], LANES - 1, 1))
                dr.append((hi_side - lo_side) * (0.5 / STEP_RADIAL))
            dt = [turn_slope(T, 1 + a, i + 1, c, n) * az_scale for a in range(3)]
            dev, size = strain(dx, dr, dt, vel[1], vel[2], inv_r)
            scale = T[0, i + 1, pl.ds(c, n), :] * width * size
            for a in range(6):
                M[other, a, own_row + i + 1, pl.ds(c, n), :] = scale * dev[a]

    def rows_of(first, count, body):
        def step(at, carry):
            body(first + at)
            return carry

        lax.fori_loop(0, count, step, 0)

    for c in own:
        c.wait()
    pack_seam()
    pl.semaphore_wait(barrier, peers)
    seam_swap.start()

    @pl.when(has_near)
    def _():
        seam_near.start()

    start(swap_ends + seam_own + own_around)

    @pl.when(has_near)
    def _():
        start(near_ends + near_rows)

    for q in [nx - 1, nx - 2] + list(range(nx - 2)):
        start(swap_rows[q])
    swap_vel.start()

    seam_swap.wait_recv()
    start(seam_partner_around)

    @pl.when(has_far)
    def _():
        seam_pass.start()
        seam_near.wait_recv()
        start(seam_beyond_around)

    arrive(own_around)
    for c in tables:
        c.wait()
    rows_of(1, nx - 2, other_half)

    @pl.when(has_near)
    def _():
        seam_pass.wait_recv()
        start(seam_ahead_around)

    arrive(swap_ends)
    start(partner_around)

    @pl.when(has_far)
    def _():
        start(pass_ends)
        arrive(near_ends)
        start(beyond_around)

    arrive(seam_own + seam_partner_around)

    @pl.when(has_far)
    def _():
        arrive(seam_beyond_around)

    @pl.when(has_near)
    def _():
        arrive(seam_ahead_around)

    seam_pass_all()
    first_two(1, nx - 2)

    @pl.when(has_near)
    def _():
        arrive(pass_ends)
        start(ahead_around)

    def hand_on(at):
        arrive(swap_rows[nx - 1 - at])

        @pl.when(has_far)
        def _():
            pass_rows[at].start()

    hand_on(0)

    @pl.when(has_far)
    def _():
        arrive(near_rows + beyond_around)

    arrive(partner_around)
    first_two(pr, 1, False)
    hand_on(1)
    first_two(pr - 1, 1)
    sweep(pr - 1, 1, leonard_pass)

    @pl.when(has_near)
    def _():
        edge_vel.start()
        arrive([pass_rows[0]] + ahead_around)

    first_two(0, 1)
    close(1, 1)
    for q in range(nx - 3):
        arrive(swap_rows[q])
        first_two(nx - 1 + q, 1)
        close(nx - 2 + q, 1)
    sweep(pr - 5, 1, leonard_pass)

    @pl.when(has_near)
    def _():
        arrive([pass_rows[1]])

    first_two(-1, 1, False)
    close(0, 1)
    arrive(swap_rows[nx - 3])
    swap_stress.start()

    @pl.when(has_near)
    def _():
        edge_stress.start()

    first_two(pr - 4, 3)
    close(pr - 4, 3)
    close(pr - 5, 2, 4, False)

    def share(at, src, dst, ax, d):
        return pltpu.make_async_remote_copy(
            src_ref=src, dst_ref=dst, send_sem=sum_send.at[at], recv_sem=sum_recv.at[at],
            device_id=(ax, lax.rem(me_az + d, n_az)), device_id_type=MESH_ID)

    def end_row(kind, half, row, ax):
        return [
            share((2 + 2 * kind + half) * n_az + d, part.at[row], rec_out.at[half, me_az], ax, d)
            for d in range(n_az)
        ]

    across = [share(d, part, rec.at[mine, me_az], me_ax, d) for d in range(1, n_az)]
    over = [share(n_az + d, part, rec.at[mine, me_az], partner, d) for d in range(n_az)]
    lower_ax, upper_ax = me_ax - odd - 1, me_ax - odd + 2
    down, up = end_row(0, mine, 0, lower_ax), end_row(1, mine, pr - 1, upper_ax)
    end_sums = end_row(even, 0, 0, me_ax) + end_row(even, 1, 0, me_ax)

    start(over)
    start(across)

    @pl.when(pair_lo)
    def _():
        start(down)

    @pl.when(pair_hi)
    def _():
        start(up)

    rec[mine, me_az] = part[...]
    swap_vel.wait_recv()
    start(swap_vel_around)

    @pl.when(has_near)
    def _():
        edge_vel.wait_recv()
        start(edge_vel_around)

    arrive(swap_vel_around)
    other_half(swap_row)

    @pl.when(has_near)
    def _():
        arrive(edge_vel_around)

    other_half(edge_row)

    def ratio(sums):
        lm, mm = sums[0:1], sums[1:2]
        return -0.5 * (lm * (1.0 / azimuth_cells)) / (mm * (1.0 / azimuth_cells) + TINY)

    def total(ref, h, row):
        terms = [ref[h, d] if row is None else ref[h, d, row] for d in range(n_az)]
        sums = terms[0]
        for x in terms[1:]:
            sums = sums + x
        return sums

    def keep(row, h, value):
        CS[row, h] = jnp.broadcast_to(-2.0 * value, (SUB, LANES))

    arrive(across)
    arrive(over)
    for i in range(nx + 1):
        row = i + even
        for h in range(2):
            keep(row, h, ratio(total(rec, h, own_row + row - 1)))
    for i in range(nx):
        for h in range(2):
            coef_ref[pl.ds(i, 1), pl.ds(h * LANES, LANES)] = -0.5 * CS[i + 1, h, pl.ds(0, 1), :]

    def flux_pass(i):
        n = math.gcd(BLOCKS["flux"], nt)
        for c in range(EDGE, EDGE + nt, n):
            r = own_row + i + 1
            inv_r, az_scale, radius, back, radius2, back2 = (spread(geo_ref[g], n) for g in (0, 1, 4, 5, 6, 7))
            lo = jnp.maximum(i - 1, jnp.where(has_lo, -1, 0)) + 1
            hi = jnp.minimum(i + 1, jnp.where(has_hi, nx, nx - 1)) + 1
            here, below, above = (spread(CS[q], n) for q in (i + 1, lo, hi))

            def at(a, row, shift=0):
                return M[:, a, row, pl.ds(c + shift, n), :]

            def axial(a):
                return above * at(a, own_row + hi) - below * at(a, own_row + lo)

            def around_of(a):
                return (at(a, r, 1) - at(a, r, -1)) * turn

            turn = here * az_scale
            once = here * radius
            d_xr = rise(once * at(1, r)) * back
            d_rr = rise(once * at(3, r)) * back
            d_rt = rise(here * radius2 * at(5, r)) * back2
            out = (
                axial(0) + d_xr + around_of(2),
                axial(1) + d_rr + around_of(5) - here * at(4, r) * inv_r,
                axial(2) + d_rt + around_of(4),
            )
            for a in range(3):
                for h in range(2):
                    flux_ref[a, i, pl.ds(c - EDGE, n), pl.ds(h * LANES, LANES)] = out[a][h]

    rows_of(1, nx - 2, flux_pass)

    @pl.when(has_near)
    def _():
        arrive(end_sums)

    swap_stress.wait_recv()
    flux_pass(swap_row)

    @pl.when(has_near)
    def _():
        for h in range(2):
            keep(pick(0, nx + 1), h, ratio(total(rec_out, h, None)))
        edge_stress.wait_recv()

    flux_pass(edge_row)

    leave([seam_swap, swap_vel, swap_stress] + swap_ends + own_around + seam_own + seam_partner_around)
    leave(partner_around + swap_vel_around + across + over)
    for q in range(nx):
        leave(swap_rows[q])

    @pl.when(has_near)
    def _():
        leave([seam_near, edge_vel, edge_stress] + near_ends + near_rows)
        leave(seam_ahead_around + ahead_around + edge_vel_around)

    @pl.when(has_far)
    def _():
        leave([seam_pass] + pass_ends + pass_rows + seam_beyond_around + beyond_around)

    @pl.when(pair_lo)
    def _():
        leave(down)

    @pl.when(pair_hi)
    def _():
        leave(up)


def hand_over(flux_in, coef_in, flux_out, coef_out, flux_buf, coef_buf, sems):
    count = flux_in.shape[0]
    pieces = [(flux_in.at[a], flux_buf.at[a], flux_out.at[a]) for a in range(count)]
    pieces.append((coef_in, coef_buf, coef_out))
    give = [pltpu.make_async_copy(a, c, sems.at[1, at]) for at, (a, b, c) in enumerate(pieces)]
    for c in give:
        c.start()
    for c in give:
        c.wait()


def shards(n_ax, n_az, density, velocity):
    nx, nt, radial = density.shape
    assert radial == 2 * LANES and 4 * nx * SEAM == LANES and n_ax % 2 == 0
    pr, seam_rows = 2 * nx, nt + 2 * SUB
    halves, seam = geometry(radial, nt * n_az)

    def field(*lead):
        return pltpu.VMEM(lead + (nt + 2 * EDGE, LANES), jnp.float32)

    def vmem(*shape):
        return pltpu.VMEM(shape, jnp.float32)

    dma = pltpu.SemaphoreType.DMA
    flux, coef = pl.pallas_call(
        functools.partial(kernel, n_ax, n_az, nx, nt),
        out_shape=(
            jax.ShapeDtypeStruct(velocity.shape, jnp.float32),
            jax.ShapeDtypeStruct((nx, radial), jnp.float32),
        ),
        in_specs=[
            pl.BlockSpec(memory_space=pltpu.HBM),
            pl.BlockSpec(memory_space=pltpu.HBM),
            pl.BlockSpec(memory_space=pltpu.HBM),
            pl.BlockSpec(memory_space=pltpu.HBM),
        ],
        out_specs=(
            pl.BlockSpec(memory_space=pltpu.VMEM),
            pl.BlockSpec(memory_space=pltpu.VMEM),
        ),
        scratch_shapes=[
            field(4, pr + 4),
            field(4, nx + 2),
            field(2, 6, pr + 2),
            field(4, pr + 2),
            field(3, pr + 2),
            field(4, pr + 2),
            field(5, pr),
            field(5, pr),
            field(5, pr),
            vmem(4, seam_rows, LANES),
            field(4),
            field(5),
            field(4),
            field(5),
            field(4),
            field(3),
            vmem(pr, 2, LANES),
            vmem(pr, 2, LANES),
            vmem(2, n_az, pr, 2, LANES),
            vmem(2, n_az, 2, LANES),
            vmem(nx + 2, 2, SUB, LANES),
            vmem(*halves.shape),
            vmem(*seam.shape),
            dma((6,)),
            dma((COPIES,)),
            dma((COPIES,)),
            dma((6 * n_az,)),
            dma((6 * n_az,)),
        ],
        compiler_params=pltpu.CompilerParams(collective_id=0, has_side_effects=True, vmem_limit_bytes=40 << 20),
        name="closure",
    )(pltpu.with_memory_space_constraint(density, pltpu.HBM), pltpu.with_memory_space_constraint(velocity, pltpu.HBM), pltpu.with_memory_space_constraint(jnp.asarray(halves), pltpu.HBM), pltpu.with_memory_space_constraint(jnp.asarray(seam), pltpu.HBM))
    flux, coef = (pltpu.with_memory_space_constraint(x, pltpu.VMEM) for x in (flux, coef))
    anywhere = pl.BlockSpec(memory_space=pl.ANY)
    return pl.pallas_call(
        hand_over,
        out_shape=(
            jax.ShapeDtypeStruct(flux.shape, jnp.float32),
            jax.ShapeDtypeStruct(coef.shape, jnp.float32),
        ),
        in_specs=[pl.BlockSpec(memory_space=pltpu.VMEM)] * 2,
        out_specs=(pl.BlockSpec(memory_space=pltpu.HBM),) * 2,
        scratch_shapes=[
            pltpu.VMEM(flux.shape, jnp.float32),
            pltpu.VMEM(coef.shape, jnp.float32),
            dma((2, flux.shape[0] + 1)),
        ],
        name="hand_over",
    )(flux, coef)


def solution(mesh):
    in_specs = (P("ax", "az", None), P(None, "ax", "az", None))
    out_specs = (P(None, "ax", "az", None), P("ax", None))
    body = functools.partial(shards, mesh.shape["ax"], mesh.shape["az"])
    return jax.shard_map(body, mesh=mesh, in_specs=in_specs, out_specs=out_specs, check_vma=False)
```

```python
import functools
import itertools
import math

import jax
import jax.numpy as jnp
import numpy as np
from jax import lax
from jax.experimental import pallas as pl
from jax.experimental.pallas import tpu as pltpu
from jax.sharding import PartitionSpec as P

STEP_AXIAL = 0.5
STEP_RADIAL = 0.25
INNER_RADIUS = 10.0
FILTER_RATIO = 2.0
TINY = 1e-06
KEPT = (0, 3, 1, 2, 5)
CROSS = ((0, 1), (0, 2), (1, 2))
LANES = 128
SUB = 8
EDGE = 16
SEAM = 8
COPIES = 64
BLOCKS = {'first': 8, 'hat': 16, 'model': 16, 'closure': 16, 'other': 16, 'flux': 8, 'seam': 16}
MESH_ID = pl.DeviceIdType.MESH


def geometry(radial, azimuth_cells):
    radius = INNER_RADIUS + (np.arange(radial, dtype=np.float64) + 0.5) * STEP_RADIAL
    angle = 2.0 * math.pi / azimuth_cells
    width = (STEP_AXIAL * STEP_RADIAL * angle * radius) ** (2.0 / 3.0)
    rows = np.stack(
        [
            1.0 / radius,
            0.5 / (radius * angle),
            width,
            FILTER_RATIO**2 * width,
            radius,
            0.5 / STEP_RADIAL / radius,
            radius * radius,
            0.5 / STEP_RADIAL / (radius * radius),
        ]
    ).astype(np.float32)
    halves = rows.reshape(rows.shape[0], radial // LANES, 1, LANES)
    at_seam = radial // 2 - SEAM // 2 + np.arange(LANES) % SEAM
    seam = rows[:4, None, at_seam]
    return (
        np.ascontiguousarray(np.broadcast_to(halves, halves.shape[:2] + (SUB, LANES))),
        np.ascontiguousarray(np.broadcast_to(seam, (4, SUB, LANES))),
    )


def lane_of(x):
    return lax.broadcasted_iota(jnp.int32, x.shape, x.ndim - 1)


def before(x):
    y = pltpu.roll(x, 1, x.ndim - 1)
    fill = jnp.concatenate([x[:1], y[:-1]], axis=0)
    return jnp.where(lane_of(x) == 0, fill, y)


def after(x):
    y = pltpu.roll(x, LANES - 1, x.ndim - 1)
    fill = jnp.concatenate([y[1:], x[-1:]], axis=0)
    return jnp.where(lane_of(x) == LANES - 1, fill, y)


def rise(x):
    return after(x) - before(x)


def sides(x):
    lane = lane_of(x)
    return (
        jnp.where(lane == 0, x, pltpu.roll(x, 1, 1)),
        jnp.where(lane == LANES - 1, x, pltpu.roll(x, LANES - 1, 1)),
    )


def radial(s):
    lo, hi = sides(s)
    return ((lo + hi) + (s + s)) * (1.0 / 64.0)


def slope(x):
    lo, hi = sides(x)
    return (hi - lo) * (0.5 / STEP_RADIAL)


def pairs(mom, vel):
    azimuthal = mom[2] * vel[2]
    return [mom[a] * vel[a] - azimuthal for a in (0, 1)] + [mom[a] * vel[b] for a, b in CROSS]


def contractions(dev, scale, leonard, hat_model):
    mixed = [scale * dev[a] - m for a, m in zip(KEPT, hat_model)]

    def cross(left, right):
        return 2.0 * (left[2] * right[2] + left[3] * right[3] + left[4] * right[4])

    azimuthal = mixed[0] + mixed[1]
    lm = leonard[0] * mixed[0] + leonard[1] * mixed[1] + cross(leonard, mixed)
    mm = mixed[0] * mixed[0] + mixed[1] * mixed[1] + azimuthal * azimuthal + cross(mixed, mixed)
    return lm, mm


def fold_rows(cells):
    return sum(cells[at:at + SUB] for at in range(0, cells.shape[0], SUB))


def strain(dx, dr, dt, ur, ut, inv_r):
    s_xx, s_rr = dx[0], dr[1]
    s_tt = dt[2] + ur * inv_r
    s_xr = 0.5 * (dr[0] + dx[1])
    s_xt = 0.5 * (dt[0] + dx[2])
    s_rt = 0.5 * (dt[1] + dr[2] - ut * inv_r)
    size = jnp.sqrt(
        2.0
        * (
            s_xx * s_xx
            + s_rr * s_rr
            + s_tt * s_tt
            + 2.0 * (s_xr * s_xr + s_xt * s_xt + s_rt * s_rt)
        )
    )
    third = (s_xx + s_rr + s_tt) * (1.0 / 3.0)
    return (s_xx - third, s_xr, s_xt, s_rr - third, s_tt - third, s_rt), size


def kernel(
    n_ax, n_az, nx, nt,
    rho_ref, vel_ref, geo_in, seam_in, flux_ref, coef_ref,
    S, T, M, H, V, HM, PX, MX, LE, E, G, GM, GH, GP, GHM, GV, SP,
    part, rec, rec_out, CS, geo_ref, seam_ref, own_sem, send_sem, recv_sem, sum_send, sum_recv,
):
    pr = 2 * nx
    me_ax, me_az = lax.axis_index("ax"), lax.axis_index("az")
    left, right = lax.rem(me_az + n_az - 1, n_az), lax.rem(me_az + 1, n_az)
    odd = lax.rem(me_ax, 2)
    even = 1 - odd
    mine, other = odd, even
    azimuth_cells = nt * n_az

    def pick(at_even, at_odd):
        return jnp.where(odd == 0, at_even, at_odd)

    has_lo, has_hi = me_ax > 0, me_ax < n_ax - 1
    pair_lo, pair_hi = me_ax >= 2, me_ax < n_ax - 2
    partner = me_ax + 1 - 2 * odd
    near_ax = me_ax - 2 + 4 * odd
    far_ax = me_ax + 2 - 4 * odd
    edge_ax = me_ax - 1 + 2 * odd
    has_near = (near_ax >= 0) & (near_ax < n_ax)
    has_far = (far_ax >= 0) & (far_ax < n_ax)

    lanes_mine = pl.ds(pl.multiple_of(mine * LANES, LANES), LANES)
    lanes_other = pl.ds(pl.multiple_of(other * LANES, LANES), LANES)
    cols = pl.ds(EDGE, nt)
    own_row = nx * odd
    own_at = own_row + 2
    partner_at = nx * even + 2
    near_at = pick(0, nx - 2)
    beyond_at = pick(pr + 2, 0)
    ahead_at = pick(0, pr + 2)
    pass_at = pick(pr, 2)

    own = [
        pltpu.make_async_copy(rho_ref.at[:, :, lanes_mine], S.at[0, pl.ds(own_at, nx), cols, :], own_sem.at[0]),
        pltpu.make_async_copy(
            vel_ref.at[:, :, :, lanes_mine], S.at[pl.ds(1, 3), pl.ds(own_at, nx), cols, :], own_sem.at[1]),
        pltpu.make_async_copy(rho_ref.at[:, :, lanes_other], T.at[0, pl.ds(1, nx), cols, :], own_sem.at[2]),
        pltpu.make_async_copy(
            vel_ref.at[:, :, :, lanes_other], T.at[pl.ds(1, 3), pl.ds(1, nx), cols, :], own_sem.at[3]),
    ]
    tables = [
        pltpu.make_async_copy(geo_in, geo_ref, own_sem.at[4]),
        pltpu.make_async_copy(seam_in, seam_ref, own_sem.at[5]),
    ]
    for c in own + tables:
        c.start()

    barrier = pltpu.get_barrier_semaphore()

    def greet(ax, az):
        pl.semaphore_signal(barrier, inc=1, device_id=(ax, az), device_id_type=MESH_ID)

    short = n_az == 4
    for d in (1, n_az - 1) if short else range(1, n_az):
        greet(me_ax, lax.rem(me_az + d, n_az))
    peers = 2 if short else n_az - 1
    if short:
        greet(partner, me_az)
        peers = peers + 1
    for step in (-2, 2) if short else (-1, 1, -2, 2):
        there = (me_ax + step >= 0) & (me_ax + step < n_ax)
        reach = 1 if short else n_az

        @pl.when(there)
        def _():
            for d in range(reach):
                greet(me_ax + step, lax.rem(me_az + d, n_az))

        peers = peers + jnp.where(there, reach, 0)

    ids = itertools.count()

    def remote(src, dst, ax, az):
        at = next(ids)
        return pltpu.make_async_remote_copy(
            src_ref=src, dst_ref=dst, send_sem=send_sem.at[at], recv_sem=recv_sem.at[at],
            device_id=(ax, az), device_id_type=MESH_ID)

    def block(src_row, count, first, width, lanes, dst, dst_row, dst_first, ax, az):
        rows, at = pl.ds(src_row, count), pl.ds(first, width)
        to_rows, to = pl.ds(dst_row, count), pl.ds(dst_first, width)
        return [
            remote(rho_ref.at[rows, at, lanes], dst.at[0, to_rows, to, :], ax, az),
            remote(vel_ref.at[:, rows, at, lanes], dst.at[pl.ds(1, 3), to_rows, to, :], ax, az),
        ]

    def ends(src_row, count, lanes, dst, dst_row, ax, az):
        out = []
        for first in (0, nt - SUB):
            out += block(src_row, count, first, SUB, lanes, dst, dst_row, EDGE + first, ax, az)
        return out

    def middle(src_row, count, lanes, dst, dst_row, ax, az):
        return block(src_row, count, SUB, nt - 2 * SUB, lanes, dst, dst_row, EDGE + SUB, ax, az)

    def around(ref, lead, rows):
        at = (pl.ds(EDGE + nt - SUB, SUB), pl.ds(EDGE - SUB, SUB), pl.ds(EDGE, SUB), pl.ds(EDGE + nt, SUB))
        return [
            remote(ref.at[lead, rows, at[0], :], ref.at[lead, rows, at[1], :], me_ax, right),
            remote(ref.at[lead, rows, at[2], :], ref.at[lead, rows, at[3], :], me_ax, left),
        ]

    whole = pl.ds(SUB, nt)

    def seam_around(s):
        return [
            remote(E.at[s, pl.ds(nt, SUB), :], E.at[s, pl.ds(0, SUB), :], me_ax, right),
            remote(E.at[s, pl.ds(SUB, SUB), :], E.at[s, pl.ds(SUB + nt, SUB), :], me_ax, left),
        ]

    s_own, s_partner, s_beyond, s_ahead = 1 + odd, 2 - odd, pick(3, 0), pick(0, 3)

    own_around = []
    for lanes, dst, row in ((lanes_mine, S, own_at), (lanes_other, T, 1)):
        own_around += block(0, nx, nt - SUB, SUB, lanes, dst, row, EDGE - SUB, me_ax, right)
        own_around += block(0, nx, 0, SUB, lanes, dst, row, EDGE + nt, me_ax, left)
    seam_own = seam_around(s_own)
    seam_partner_around = seam_around(s_partner)
    seam_beyond_around = seam_around(s_beyond)
    seam_ahead_around = seam_around(s_ahead)

    seam_swap = remote(E.at[s_own, whole, :], E.at[s_own, whole, :], partner, me_az)
    seam_near = remote(E.at[s_own, whole, :], E.at[pick(3, 0), whole, :], near_ax, me_az)
    seam_pass = remote(E.at[s_partner, whole, :], E.at[pick(0, 3), whole, :], far_ax, me_az)

    swap_ends = ends(0, nx, lanes_other, S, own_at, partner, me_az)
    swap_rows = {}
    for q in range(nx):
        row = pick(nx - 1 - q, q)
        swap_rows[q] = middle(row, 1, lanes_other, S, own_at + row, partner, me_az)
    near_ends = ends(near_at, 2, lanes_mine, S, beyond_at, near_ax, me_az)
    near_rows = middle(near_at, 2, lanes_mine, S, beyond_at, near_ax, me_az)

    every = pl.ds(0, 4)

    def forward(row, first, width, count):
        return remote(
            S.at[:, pl.ds(pass_at + row, count), pl.ds(EDGE + first, width), :],
            S.at[:, pl.ds(ahead_at + row, count), pl.ds(EDGE + first, width), :], far_ax, me_az)

    pass_ends = [forward(0, first, SUB, 2) for first in (0, nt - SUB)]
    last_row = pick(1, 0)
    pass_rows = [forward(last_row, SUB, nt - 2 * SUB, 1), forward(1 - last_row, SUB, nt - 2 * SUB, 1)]
    partner_around = around(S, every, pl.ds(partner_at, nx))
    beyond_around = around(S, every, pl.ds(beyond_at, 2))
    ahead_around = around(S, every, pl.ds(ahead_at, 2))

    swap_row, edge_row = pick(nx - 1, 0), pick(0, nx - 1)
    three = pl.ds(1, 3)

    def flux_rows(row, dst_row, ax):
        return remote(
            vel_ref.at[:, pl.ds(row, 1), :, lanes_mine], T.at[three, pl.ds(dst_row, 1), cols, :], ax, me_az)

    def flux_stress(row, dst_row, ax):
        return remote(
            M.at[mine, pl.ds(0, 3), own_row + row + 1, cols, :], M.at[mine, pl.ds(0, 3), dst_row, cols, :],
            ax, me_az)

    swap_vel = flux_rows(swap_row, pick(0, nx + 1), partner)
    edge_vel = flux_rows(edge_row, pick(nx + 1, 0), edge_ax)
    swap_vel_around = around(T, three, pl.ds(pick(nx + 1, 0), 1))
    edge_vel_around = around(T, three, pl.ds(pick(0, nx + 1), 1))
    swap_stress = flux_stress(swap_row, pick(nx, nx + 1), partner)
    edge_stress = flux_stress(edge_row, pick(pr + 1, 0), edge_ax)

    def start(copies):
        for c in copies:
            c.start()

    def arrive(copies):
        for c in copies:
            c.wait_recv()

    def leave(copies):
        for c in copies:
            c.wait_send()

    wide = nt + 2 * SUB
    outer_cols = EDGE - SUB

    def lanes_at(n):
        return lax.broadcasted_iota(jnp.int32, (n, LANES), 1)

    def spread(values, rows):
        return jnp.concatenate([values] * (rows // SUB), axis=values.ndim - 2)

    def pack_seam():
        lane = lanes_at(nt)
        from_mine = jnp.where(lane >= LANES - SEAM // 2, 1, 0) == even
        packed = jnp.zeros((nt, LANES), jnp.float32)
        for a in range(4):
            for i in range(nx):
                first = (a * nx + i) * SEAM
                x = jnp.where(from_mine, S[a, own_at + i, pl.ds(EDGE, nt), :], T[a, 1 + i, pl.ds(EDGE, nt), :])
                x = pltpu.roll(x, (first + SEAM // 2) % LANES, 1)
                packed = jnp.where((lane >= first) & (lane < first + SEAM), x, packed)
        E[s_own, whole, :] = packed

    n_seam = math.gcd(BLOCKS["seam"], wide)
    seam_lane = lanes_at(n_seam)
    seam_row = seam_lane // SEAM
    at_bottom = seam_row == jnp.where(pair_lo, -1, nx)
    at_top = seam_row == jnp.where(pair_hi, -1, nx + pr - 1)

    def seam_below(x):
        return jnp.where(at_bottom, x, pltpu.roll(x, SEAM, 1))

    def seam_above(x):
        return jnp.where(at_top, x, pltpu.roll(x, LANES - SEAM, 1))

    def seam_axial(x):
        return (seam_below(x) + x) + (x + seam_above(x))

    def seam_slope(x):
        return (pltpu.roll(x, LANES - 1, 1) - pltpu.roll(x, 1, 1)) * (0.5 / STEP_RADIAL)

    def seam_radial(s):
        return ((pltpu.roll(s, 1, 1) + pltpu.roll(s, LANES - 1, 1)) + (s + s)) * (1.0 / 64.0)

    def seam_turn(ref, a, c, n):
        x = ref[a, pl.ds(c, n), :]
        return (ref[a, pl.ds(c - 1, n), :] + ref[a, pl.ds(c + 1, n), :]) + (x + x)

    def seam_pass_all():
        tiles = [(c, n_seam) for c in range(outer_cols, outer_cols + wide, n_seam)]
        inner = [(c, n_seam) for c in range(EDGE, EDGE + nt, n_seam)]
        lane = lanes_at(wide)
        per = nx * SEAM
        for a in range(4):
            packed = jnp.zeros((wide, LANES), jnp.float32)
            for s in range(4):
                x = E[s, :, :]
                if s != a:
                    x = pltpu.roll(x, (s - a) * per % LANES, 1)
                packed = jnp.where((lane >= s * per) & (lane < (s + 1) * per), x, packed)
            G[a, pl.ds(outer_cols, wide), :] = packed
        for c, n in tiles:
            at, at_before, at_after = pl.ds(c, n), pl.ds(c - 1, n), pl.ds(c + 1, n)
            rho = G[0, at, :]
            vel = [G[1 + a, at, :] for a in range(3)]
            inv_r, az_scale, width = (spread(seam_ref[g], n) for g in (0, 1, 2))
            dx = [seam_above(v) - seam_below(v) for v in vel]
            dr = [seam_slope(v) for v in vel]
            dt = [(G[1 + a, at_after, :] - G[1 + a, at_before, :]) * az_scale for a in range(3)]
            dev, size = strain(dx, dr, dt, vel[1], vel[2], inv_r)
            scale = rho * width * size
            for q, a in enumerate(KEPT):
                GM[q, at, :] = seam_axial(scale * dev[a])
            mom = [rho * v for v in vel]
            GH[0, at, :] = seam_axial(rho)
            for a in range(3):
                GH[1 + a, at, :] = seam_axial(mom[a])
            for q, p in enumerate(pairs(mom, vel)):
                GP[q, at, :] = seam_axial(p)
        for c, n in tiles:
            at = pl.ds(c, n)
            hat = [seam_radial(seam_turn(GH, a, c, n)) for a in range(4)]
            inv = 1.0 / hat[0]
            for a in range(4):
                GHM[a, at, :] = hat[a]
            for a in range(3):
                GV[a, at, :] = hat[1 + a] * inv
        sums = [0.0, 0.0]
        for c, n in inner:
            at, at_before, at_after = pl.ds(c, n), pl.ds(c - 1, n), pl.ds(c + 1, n)
            inv_r, az_scale, width4 = (spread(seam_ref[g], n) for g in (0, 1, 3))
            hv = [GV[a, at, :] for a in range(3)]
            dx = [seam_above(v) - seam_below(v) for v in hv]
            dr = [seam_slope(v) for v in hv]
            dt = [(GV[a, at_after, :] - GV[a, at_before, :]) * az_scale for a in range(3)]
            dev, size = strain(dx, dr, dt, hv[1], hv[2], inv_r)
            terms = contractions(
                dev, width4 * GHM[0, at, :] * size,
                [seam_radial(seam_turn(GP, q, c, n)) - p for q, p in
                 enumerate(pairs([GHM[1 + a, at, :] for a in range(3)], hv))],
                [seam_radial(seam_turn(GM, q, c, n)) for q in range(5)])
            sums = [x + fold_rows(y) for x, y in zip(sums, terms)]
        for q in range(2):
            row = jnp.sum(sums[q], axis=0, keepdims=True)
            for r in range(pr):
                shift = LANES - SEAM // 2 - SEAM * (nx + r)
                SP[r, pl.ds(q, 1), :] = pltpu.roll(row, shift % LANES, 1)

    def smooth(ref, a, row, first, n):
        x = ref[a, row, pl.ds(first, n), :]
        s = (ref[a, row, pl.ds(first - 1, n), :] + ref[a, row, pl.ds(first + 1, n), :]) + (x + x)
        return radial(s)

    def whole_slope(a, x, first, r, held):
        shift = pick(LANES - 1, LANES + 1) - SEAM // 2 - SEAM * (r + nx)
        end = pick(LANES - 1, 0)
        if held:
            far = pltpu.roll(T[1 + a, r - own_row + 1, pl.ds(first, x.shape[0]), :], pick(LANES - 1, 1), 1)
        else:
            far = pltpu.roll(G[1 + a, pl.ds(first, x.shape[0]), :], shift, 1)
        lane = lane_of(x)
        far = jnp.where(lane == end, far, x)
        lo = jnp.where(lane == 0, far, pltpu.roll(x, 1, 1))
        hi = jnp.where(lane == LANES - 1, far, pltpu.roll(x, LANES - 1, 1))
        return (hi - lo) * (0.5 / STEP_RADIAL)

    def low(r):
        return jnp.maximum(r - 1, jnp.where(pair_lo, -2, 0))

    def high(r):
        return jnp.minimum(r + 1, jnp.where(pair_hi, pr + 1, pr - 1))

    def sweep(first, count, body, stride=1):
        def step(at, carry):
            t = first + at * stride
            body(pick(t, pr - 1 - t))
            return carry

        lax.fori_loop(0, count, step, 0)

    def turn_slope(ref, a, row, first, n):
        return ref[a, row, pl.ds(first + 1, n), :] - ref[a, row, pl.ds(first - 1, n), :]

    def first_block(r, with_pairs, exact, held, c, n):
        rows = (low(r) + 2, r + 2, high(r) + 2)
        rho = [S[0, q, pl.ds(c, n), :] for q in rows]
        vel = [[S[1 + a, q, pl.ds(c, n), :] for a in range(3)] for q in rows]
        inv_r, az_scale, width = (spread(geo_ref[g, mine], n) for g in (0, 1, 2))
        dx = [vel[2][a] - vel[0][a] for a in range(3)]
        dr = [whole_slope(a, vel[1][a], c, r, held) if exact else slope(vel[1][a]) for a in range(3)]
        dt = [turn_slope(S, 1 + a, r + 2, c, n) * az_scale for a in range(3)]
        dev, size = strain(dx, dr, dt, vel[1][1], vel[1][2], inv_r)
        scale = rho[1] * width * size
        for a in range(6):
            M[mine, a, r + 1, pl.ds(c, n), :] = scale * dev[a]
        mom = [[rho[q] * vel[q][a] for a in range(3)] for q in range(3)]
        H[0, r + 1, pl.ds(c, n), :] = (rho[0] + rho[1]) + (rho[1] + rho[2])
        for a in range(3):
            H[1 + a, r + 1, pl.ds(c, n), :] = (mom[0][a] + mom[1][a]) + (mom[1][a] + mom[2][a])
        if with_pairs:
            for at, p in enumerate(zip(*(pairs(mom[q], vel[q]) for q in range(3)))):
                PX[at, r, pl.ds(c, n), :] = (p[0] + p[1]) + (p[1] + p[2])

    def hat_block(r, c, n):
        hat = [smooth(H, a, r + 1, c, n) for a in range(4)]
        inv = 1.0 / hat[0]
        for a in range(4):
            HM[a, r + 1, pl.ds(c, n), :] = hat[a]
        for a in range(3):
            V[a, r + 1, pl.ds(c, n), :] = hat[1 + a] * inv

    def model_pass(r):
        n = math.gcd(BLOCKS["model"], wide)
        for c in range(outer_cols, outer_cols + wide, n):
            for q, a in enumerate(KEPT):
                x = M[mine, a, r + 1, pl.ds(c, n), :]
                lo = M[mine, a, low(r) + 1, pl.ds(c, n), :]
                MX[q, r, pl.ds(c, n), :] = (lo + x) + (x + M[mine, a, high(r) + 1, pl.ds(c, n), :])

    def leonard_pass(r):
        n = math.gcd(BLOCKS["closure"], nt)
        for c in range(EDGE, EDGE + nt, n):
            hv = [V[a, r + 1, pl.ds(c, n), :] for a in range(3)]
            hm = [HM[1 + a, r + 1, pl.ds(c, n), :] for a in range(3)]
            for q, p in enumerate(pairs(hm, hv)):
                LE[q, r, pl.ds(c, n), :] = smooth(PX, q, r, c, n) - p

    def closure_pass(r):
        sums = [0.0, 0.0]
        n = math.gcd(BLOCKS["closure"], nt)
        for c in range(EDGE, EDGE + nt, n):
            inv_r, az_scale, width4 = (spread(geo_ref[g, mine], n) for g in (0, 1, 3))
            hv = [V[a, r + 1, pl.ds(c, n), :] for a in range(3)]
            dx = [V[a, high(r) + 1, pl.ds(c, n), :] - V[a, low(r) + 1, pl.ds(c, n), :] for a in range(3)]
            dr = [slope(hv[a]) for a in range(3)]
            dt = [turn_slope(V, a, r + 1, c, n) * az_scale for a in range(3)]
            dev, size = strain(dx, dr, dt, hv[1], hv[2], inv_r)
            terms = contractions(
                dev, width4 * HM[0, r + 1, pl.ds(c, n), :] * size,
                [LE[q, r, pl.ds(c, n), :] for q in range(5)], [smooth(MX, q, r, c, n) for q in range(5)])
            sums = [x + fold_rows(y) for x, y in zip(sums, terms)]
        lane = lanes_at(1)
        at_seam = jnp.where(odd == 0, LANES - 1 - lane, lane) < 2
        for q in range(2):
            row = jnp.sum(sums[q], axis=0, keepdims=True)
            part[r, pl.ds(q, 1), :] = jnp.where(at_seam, SP[r, pl.ds(q, 1), :], row)

    def first_two(first, count, with_pairs=True, held=False):
        n = math.gcd(BLOCKS["first"], wide)
        blocks = list(range(outer_cols, outer_cols + wide, n))

        def both(exact, r):
            for at, c in enumerate(blocks):
                first_block(r, with_pairs, exact, held, c, n)
                if at >= 2:
                    hat_block(r, blocks[at - 2], n)
            for c in blocks[-2:]:
                hat_block(r, c, n)

        exact = min(max(nx + 1 - first, 0), count)
        if exact:
            sweep(first, exact, functools.partial(both, True))
        if exact < count:
            sweep(first + exact, count - exact, functools.partial(both, False))

    def close(first, count, stride=1, leonard=True):
        def both(r):
            if leonard:
                leonard_pass(r)
            model_pass(r)
            closure_pass(r)

        sweep(first, count, both, stride)

    def other_half(i):
        n = math.gcd(BLOCKS["other"], wide)
        for c in range(outer_cols, outer_cols + wide, n):
            inv_r, az_scale, width = (spread(geo_ref[g, other], n) for g in (0, 1, 2))
            lo = jnp.maximum(i - 1, jnp.where(has_lo, -1, 0)) + 1
            hi = jnp.minimum(i + 1, jnp.where(has_hi, nx, nx - 1)) + 1
            vel = [T[1 + a, i + 1, pl.ds(c, n), :] for a in range(3)]
            dx = [T[1 + a, hi, pl.ds(c, n), :] - T[1 + a, lo, pl.ds(c, n), :] for a in range(3)]
            dr = []
            for a in range(3):
                far = pltpu.roll(S[1 + a, own_at + i, pl.ds(c, n), :], pick(1, LANES - 1), 1)
                lane = lane_of(far)
                end = jnp.where(lane == pick(0, LANES - 1), far, vel[a])
                lo_side = jnp.where(lane == 0, end, pltpu.roll(vel[a], 1, 1))
                hi_side = jnp.where(lane == LANES - 1, end, pltpu.roll(vel[a], LANES - 1, 1))
                dr.append((hi_side - lo_side) * (0.5 / STEP_RADIAL))
            dt = [turn_slope(T, 1 + a, i + 1, c, n) * az_scale for a in range(3)]
            dev, size = strain(dx, dr, dt, vel[1], vel[2], inv_r)
            scale = T[0, i + 1, pl.ds(c, n), :] * width * size
            for a in range(6):
                M[other, a, own_row + i + 1, pl.ds(c, n), :] = scale * dev[a]

    def rows_of(first, count, body):
        def step(at, carry):
            body(first + at)
            return carry

        lax.fori_loop(0, count, step, 0)

    for c in own:
        c.wait()
    pack_seam()
    pl.semaphore_wait(barrier, peers)
    seam_swap.start()

    @pl.when(has_near)
    def _():
        seam_near.start()

    start(swap_ends + seam_own + own_around)

    @pl.when(has_near)
    def _():
        start(near_ends + near_rows)

    for q in [nx - 1, nx - 2] + list(range(nx - 2)):
        start(swap_rows[q])
    swap_vel.start()

    seam_swap.wait_recv()
    start(seam_partner_around)

    @pl.when(has_far)
    def _():
        seam_pass.start()
        seam_near.wait_recv()
        start(seam_beyond_around)

    arrive(own_around)
    for c in tables:
        c.wait()
    rows_of(1, nx - 2, other_half)

    @pl.when(has_near)
    def _():
        seam_pass.wait_recv()
        start(seam_ahead_around)

    first_two(1, nx - 2, held=True)
    arrive(swap_ends)
    start(partner_around)

    @pl.when(has_far)
    def _():
        start(pass_ends)
        arrive(near_ends)
        start(beyond_around)

    arrive(seam_own + seam_partner_around)

    @pl.when(has_far)
    def _():
        arrive(seam_beyond_around)

    @pl.when(has_near)
    def _():
        arrive(seam_ahead_around)

    seam_pass_all()

    @pl.when(has_near)
    def _():
        arrive(pass_ends)
        start(ahead_around)

    def hand_on(at):
        arrive(swap_rows[nx - 1 - at])

        @pl.when(has_far)
        def _():
            pass_rows[at].start()

    hand_on(0)

    @pl.when(has_far)
    def _():
        arrive(near_rows + beyond_around)

    arrive(partner_around)
    first_two(pr, 1, False)
    hand_on(1)
    first_two(pr - 1, 1)
    sweep(pr - 1, 1, leonard_pass)

    @pl.when(has_near)
    def _():
        edge_vel.start()
        arrive([pass_rows[0]] + ahead_around)

    first_two(0, 1)
    close(1, 1)
    for q in range(nx - 3):
        arrive(swap_rows[q])
        first_two(nx - 1 + q, 1)
        close(nx - 2 + q, 1)
    sweep(pr - 5, 1, leonard_pass)

    @pl.when(has_near)
    def _():
        arrive([pass_rows[1]])

    first_two(-1, 1, False)
    close(0, 1)
    arrive(swap_rows[nx - 3])
    swap_stress.start()

    @pl.when(has_near)
    def _():
        edge_stress.start()

    first_two(pr - 4, 3)
    close(pr - 4, 3)
    close(pr - 5, 2, 4, False)

    def share(at, src, dst, ax, d):
        return pltpu.make_async_remote_copy(
            src_ref=src, dst_ref=dst, send_sem=sum_send.at[at], recv_sem=sum_recv.at[at],
            device_id=(ax, lax.rem(me_az + d, n_az)), device_id_type=MESH_ID)

    def end_row(kind, half, row, ax):
        return [
            share((2 + 2 * kind + half) * n_az + d, part.at[row], rec_out.at[half, me_az], ax, d)
            for d in range(n_az)
        ]

    across = [share(d, part, rec.at[mine, me_az], me_ax, d) for d in range(1, n_az)]
    over = [share(n_az + d, part, rec.at[mine, me_az], partner, d) for d in range(n_az)]
    lower_ax, upper_ax = me_ax - odd - 1, me_ax - odd + 2
    down, up = end_row(0, mine, 0, lower_ax), end_row(1, mine, pr - 1, upper_ax)
    end_sums = end_row(even, 0, 0, me_ax) + end_row(even, 1, 0, me_ax)

    start(over)
    start(across)

    @pl.when(pair_lo)
    def _():
        start(down)

    @pl.when(pair_hi)
    def _():
        start(up)

    rec[mine, me_az] = part[...]
    swap_vel.wait_recv()
    start(swap_vel_around)

    @pl.when(has_near)
    def _():
        edge_vel.wait_recv()
        start(edge_vel_around)

    arrive(swap_vel_around)
    other_half(swap_row)

    @pl.when(has_near)
    def _():
        arrive(edge_vel_around)

    other_half(edge_row)

    def ratio(sums):
        lm, mm = sums[0:1], sums[1:2]
        return -0.5 * (lm * (1.0 / azimuth_cells)) / (mm * (1.0 / azimuth_cells) + TINY)

    def total(ref, h, row):
        terms = [ref[h, d] if row is None else ref[h, d, row] for d in range(n_az)]
        sums = terms[0]
        for x in terms[1:]:
            sums = sums + x
        return sums

    def keep(row, h, value):
        CS[row, h] = jnp.broadcast_to(-2.0 * value, (SUB, LANES))

    arrive(across)
    arrive(over)
    for i in range(nx + 1):
        row = i + even
        for h in range(2):
            keep(row, h, ratio(total(rec, h, own_row + row - 1)))
    for i in range(nx):
        for h in range(2):
            coef_ref[pl.ds(i, 1), pl.ds(h * LANES, LANES)] = -0.5 * CS[i + 1, h, pl.ds(0, 1), :]

    def flux_pass(i):
        n = math.gcd(BLOCKS["flux"], nt)
        for c in range(EDGE, EDGE + nt, n):
            r = own_row + i + 1
            inv_r, az_scale, radius, back, radius2, back2 = (spread(geo_ref[g], n) for g in (0, 1, 4, 5, 6, 7))
            lo = jnp.maximum(i - 1, jnp.where(has_lo, -1, 0)) + 1
            hi = jnp.minimum(i + 1, jnp.where(has_hi, nx, nx - 1)) + 1
            here, below, above = (spread(CS[q], n) for q in (i + 1, lo, hi))

            def at(a, row, shift=0):
                return M[:, a, row, pl.ds(c + shift, n), :]

            def axial(a):
                return above * at(a, own_row + hi) - below * at(a, own_row + lo)

            def around_of(a):
                return (at(a, r, 1) - at(a, r, -1)) * turn

            turn = here * az_scale
            once = here * radius
            d_xr = rise(once * at(1, r)) * back
            d_rr = rise(once * at(3, r)) * back
            d_rt = rise(here * radius2 * at(5, r)) * back2
            out = (
                axial(0) + d_xr + around_of(2),
                axial(1) + d_rr + around_of(5) - here * at(4, r) * inv_r,
                axial(2) + d_rt + around_of(4),
            )
            for a in range(3):
                for h in range(2):
                    flux_ref[a, i, pl.ds(c - EDGE, n), pl.ds(h * LANES, LANES)] = out[a][h]

    rows_of(1, nx - 2, flux_pass)

    @pl.when(has_near)
    def _():
        arrive(end_sums)

    swap_stress.wait_recv()
    flux_pass(swap_row)

    @pl.when(has_near)
    def _():
        for h in range(2):
            keep(pick(0, nx + 1), h, ratio(total(rec_out, h, None)))
        edge_stress.wait_recv()

    flux_pass(edge_row)

    leave([seam_swap, swap_vel, swap_stress] + swap_ends + own_around + seam_own + seam_partner_around)
    leave(partner_around + swap_vel_around + across + over)
    for q in range(nx):
        leave(swap_rows[q])

    @pl.when(has_near)
    def _():
        leave([seam_near, edge_vel, edge_stress] + near_ends + near_rows)
        leave(seam_ahead_around + ahead_around + edge_vel_around)

    @pl.when(has_far)
    def _():
        leave([seam_pass] + pass_ends + pass_rows + seam_beyond_around + beyond_around)

    @pl.when(pair_lo)
    def _():
        leave(down)

    @pl.when(pair_hi)
    def _():
        leave(up)


def hand_over(flux_in, coef_in, flux_out, coef_out, flux_buf, coef_buf, sems):
    count = flux_in.shape[0]
    pieces = [(flux_in.at[a], flux_buf.at[a], flux_out.at[a]) for a in range(count)]
    pieces.append((coef_in, coef_buf, coef_out))
    give = [pltpu.make_async_copy(a, c, sems.at[1, at]) for at, (a, b, c) in enumerate(pieces)]
    for c in give:
        c.start()
    for c in give:
        c.wait()


def shards(n_ax, n_az, density, velocity):
    nx, nt, radial = density.shape
    assert radial == 2 * LANES and 4 * nx * SEAM == LANES and n_ax % 2 == 0
    pr, seam_rows = 2 * nx, nt + 2 * SUB
    halves, seam = geometry(radial, nt * n_az)

    def field(*lead):
        return pltpu.VMEM(lead + (nt + 2 * EDGE, LANES), jnp.float32)

    def vmem(*shape):
        return pltpu.VMEM(shape, jnp.float32)

    dma = pltpu.SemaphoreType.DMA
    flux, coef = pl.pallas_call(
        functools.partial(kernel, n_ax, n_az, nx, nt),
        out_shape=(
            jax.ShapeDtypeStruct(velocity.shape, jnp.float32),
            jax.ShapeDtypeStruct((nx, radial), jnp.float32),
        ),
        in_specs=[
            pl.BlockSpec(memory_space=pltpu.HBM),
            pl.BlockSpec(memory_space=pltpu.HBM),
            pl.BlockSpec(memory_space=pltpu.HBM),
            pl.BlockSpec(memory_space=pltpu.HBM),
        ],
        out_specs=(
            pl.BlockSpec(memory_space=pltpu.VMEM),
            pl.BlockSpec(memory_space=pltpu.VMEM),
        ),
        scratch_shapes=[
            field(4, pr + 4),
            field(4, nx + 2),
            field(2, 6, pr + 2),
            field(4, pr + 2),
            field(3, pr + 2),
            field(4, pr + 2),
            field(5, pr),
            field(5, pr),
            field(5, pr),
            vmem(4, seam_rows, LANES),
            field(4),
            field(5),
            field(4),
            field(5),
            field(4),
            field(3),
            vmem(pr, 2, LANES),
            vmem(pr, 2, LANES),
            vmem(2, n_az, pr, 2, LANES),
            vmem(2, n_az, 2, LANES),
            vmem(nx + 2, 2, SUB, LANES),
            vmem(*halves.shape),
            vmem(*seam.shape),
            dma((6,)),
            dma((COPIES,)),
            dma((COPIES,)),
            dma((6 * n_az,)),
            dma((6 * n_az,)),
        ],
        compiler_params=pltpu.CompilerParams(collective_id=0, has_side_effects=True, vmem_limit_bytes=40 << 20),
        name="closure",
    )(pltpu.with_memory_space_constraint(density, pltpu.HBM), pltpu.with_memory_space_constraint(velocity, pltpu.HBM), pltpu.with_memory_space_constraint(jnp.asarray(halves), pltpu.HBM), pltpu.with_memory_space_constraint(jnp.asarray(seam), pltpu.HBM))
    flux, coef = (pltpu.with_memory_space_constraint(x, pltpu.VMEM) for x in (flux, coef))
    anywhere = pl.BlockSpec(memory_space=pl.ANY)
    return pl.pallas_call(
        hand_over,
        out_shape=(
            jax.ShapeDtypeStruct(flux.shape, jnp.float32),
            jax.ShapeDtypeStruct(coef.shape, jnp.float32),
        ),
        in_specs=[pl.BlockSpec(memory_space=pltpu.VMEM)] * 2,
        out_specs=(pl.BlockSpec(memory_space=pltpu.HBM),) * 2,
        scratch_shapes=[
            pltpu.VMEM(flux.shape, jnp.float32),
            pltpu.VMEM(coef.shape, jnp.float32),
            dma((2, flux.shape[0] + 1)),
        ],
        name="hand_over",
    )(flux, coef)


def solution(mesh):
    in_specs = (P("ax", "az", None), P(None, "ax", "az", None))
    out_specs = (P(None, "ax", "az", None), P("ax", None))
    body = functools.partial(shards, mesh.shape["ax"], mesh.shape["az"])
    return jax.shard_map(body, mesh=mesh, in_specs=in_specs, out_specs=out_specs, check_vma=False)
```
